32 devices in a mesh: dp: 8 (over y, x, core), tensor: 4 (over z).
Axes of the slice: x: 2, y: 2, z: 4, core: 2. Of those that a mesh axis runs over, the one named last changes fastest.
Arguments:
- teacher_input: bfloat16 [8, 1024, 1280], P('dp', 'tensor'), may hold values from -6 to 6
- teacher_upstream: bfloat16 [8, 1024, 1280], P('dp', 'tensor'), may hold values from -6 to 6
- teacher_attn_gain: bfloat16 [1280], P('dp'), may hold values from 0.25 to 1.75
- teacher_attn_shift: bfloat16 [1280], P('dp'), may hold values from -1.75 to 1.75
- teacher_qkv_weight: bfloat16 [3, 1280, 1536], P(None, 'dp', 'tensor'), may hold values from -0.15625 to 0.15625
- teacher_qv_bias: bfloat16 [2, 1536], P(None, 'tensor'), may hold values from -0.625 to 0.625
- teacher_out_weight: bfloat16 [1536, 1280], P('tensor', 'dp'), may hold values from -1.25 to 1.25
- teacher_out_bias: bfloat16 [1280], P('dp'), may hold values from -1.75 to 1.75
- teacher_mlp_gain: bfloat16 [1280], P('dp'), may hold values from 0.25 to 1.75
- teacher_mlp_shift: bfloat16 [1280], P('dp'), may hold values from -1.75 to 1.75
- teacher_fc_weight: bfloat16 [1280, 5120], P('dp', 'tensor'), may hold values from -0.15625 to 0.15625
- teacher_fc_bias: bfloat16 [5120], P('tensor'), may hold values from -1.75 to 1.75
- teacher_proj_weight: bfloat16 [5120, 1280], P('tensor', 'dp'), may hold values from -0.078125 to 0.078125
- teacher_proj_bias: bfloat16 [1280], P('dp'), may hold values from -1.75 to 1.75
- student_input: bfloat16 [8, 1024, 768], P('dp', 'tensor'), may hold values from -6 to 6
- student_upstream: bfloat16 [8, 1024, 768], P('dp', 'tensor'), may hold values from -6 to 6
- student_attn_gain: bfloat16 [768], P('dp'), may hold values from 0.25 to 1.75
- student_attn_shift: bfloat16 [768], P('dp'), may hold values from -1.75 to 1.75
- student_qkv_weight: bfloat16 [3, 768, 768], P(None, 'dp', 'tensor'), may hold values from -0.21875 to 0.21875
- student_qv_bias: bfloat16 [2, 768], P(None, 'tensor'), may hold values from -0.625 to 0.625
- student_out_weight: bfloat16 [768, 768], P('tensor', 'dp'), may hold values from -1.75 to 1.75
- student_out_bias: bfloat16 [768], P('dp'), may hold values from -1.75 to 1.75
- student_mlp_gain: bfloat16 [768], P('dp'), may hold values from 0.25 to 1.75
- student_mlp_shift: bfloat16 [768], P('dp'), may hold values from -1.75 to 1.75
- student_fc_weight: bfloat16 [768, 3072], P('dp', 'tensor'), may hold values from -0.21875 to 0.21875
- student_fc_bias: bfloat16 [3072], P('tensor'), may hold values from -1.75 to 1.75
- student_proj_weight: bfloat16 [3072, 768], P('tensor', 'dp'), may hold values from -0.109375 to 0.109375
- student_proj_bias: bfloat16 [768], P('dp'), may hold values from -1.75 to 1.75
- span_starts: int32 [8], P('dp'), may hold values from 0 to 768, as said below
- head_slots: int32 [24], P('tensor'), may hold values from 0 to 1, as said below
Outputs:
- teacher_output: bfloat16 [8, 1024, 1280], P('dp', 'tensor')
- teacher_input_grad: bfloat16 [8, 1024, 1280], P('dp', 'tensor')
- teacher_attn_gain_grad: float32 [1280], P('dp')
- teacher_attn_shift_grad: float32 [1280], P('dp')
- teacher_qkv_weight_grad: float32 [3, 1280, 1536], P(None, 'dp', 'tensor')
- teacher_qv_bias_grad: float32 [2, 1536], P(None, 'tensor')
- teacher_out_weight_grad: float32 [1536, 1280], P('tensor', 'dp')
- teacher_out_bias_grad: float32 [1280], P('dp')
- teacher_mlp_gain_grad: float32 [1280], P('dp')
- teacher_mlp_shift_grad: float32 [1280], P('dp')
- teacher_fc_weight_grad: float32 [1280, 5120], P('dp', 'tensor')
- teacher_fc_bias_grad: float32 [5120], P('tensor')
- teacher_proj_weight_grad: float32 [5120, 1280], P('tensor', 'dp')
- teacher_proj_bias_grad: float32 [1280], P('dp')
- student_output: bfloat16 [8, 1024, 768], P('dp', 'tensor')
- student_input_grad: bfloat16 [8, 1024, 768], P('dp', 'tensor')
- student_attn_gain_grad: float32 [768], P('dp')
- student_attn_shift_grad: float32 [768], P('dp')
- student_qkv_weight_grad: float32 [3, 768, 768], P(None, 'dp', 'tensor')
- student_qv_bias_grad: float32 [2, 768], P(None, 'tensor')
- student_out_weight_grad: float32 [768, 768], P('tensor', 'dp')
- student_out_bias_grad: float32 [768], P('dp')
- student_mlp_gain_grad: float32 [768], P('dp')
- student_mlp_shift_grad: float32 [768], P('dp')
- student_fc_weight_grad: float32 [768, 3072], P('dp', 'tensor')
- student_fc_bias_grad: float32 [3072], P('tensor')
- student_proj_weight_grad: float32 [3072, 768], P('tensor', 'dp')
- student_proj_bias_grad: float32 [768], P('dp')
The draws below stay inside these ranges and needn't reach their ends.
Inputs may be any that keep to these rules, and one draw needn't show every extreme that they name: `span_starts`: some sequence starts its span at 0 and some at 768. `head_slots`: exactly 20 of the 24 slots are 1.
All inputs are finite; a program needn't handle non-finite values.
Results may differ from the reference program's by a relative error of at most 0.02.
Values may be sent and summed in bfloat16 or wider, within the bound.
No kernel may reach another device: no remote copies, remote signals or barrier semaphores. Data moves between devices by JAX's collectives and lax.ppermute only.
A program may use at most 256 MiB of HBM per device.

```python
import math
import jax
import jax.numpy as jnp
from jax import lax

DT = 1280
HT = 24
HT_REAL = 20
HD = 64
FT = 5120
DS = 768
HS = 12
FS = 3072
LEN = 1024
SPAN = 256
SEQS = 8


def draw_span_starts(key, part):
    first_key = jax.random.fold_in(key, 11)
    second_key = jax.random.fold_in(key, 12)
    starts = jax.random.randint(first_key, (SEQS,), 0, LEN - SPAN + 1, dtype=jnp.int32)
    ranking = jax.random.permutation(second_key, SEQS)
    starts = starts.at[ranking[0]].set(0)
    starts = starts.at[ranking[1]].set(LEN - SPAN)
    return starts.astype(jnp.int32)


def draw_head_slots(key, part):
    ranking = jax.random.permutation(jax.random.fold_in(key, 21), HT)
    return (ranking < HT_REAL).astype(jnp.int32)


def spiked(values, own_key, source, target, shards_of, factor):
    def block_of(dim):
        return (jnp.arange(values.shape[dim]) // (values.shape[dim] // shards_of)).reshape((-1,) + (1,) * (values.ndim - 1 - dim))

    near = jax.random.permutation(own_key, shards_of)[block_of(target)]
    far = (block_of(target) + shards_of // 2) % shards_of
    return jnp.where((block_of(source) == near) | (block_of(source) == far), factor * values, values)


def shard_levels(own_key, dims, shards, least, top_value):
    def one(dim, blocks):
        steps = jax.random.uniform(jax.random.fold_in(jax.random.fold_in(own_key, 6), dim), (blocks,), jnp.float32, least / len(shards), top_value / len(shards))
        return jnp.repeat(jnp.exp(steps), dims[dim] // blocks).reshape((-1,) + (1,) * (len(dims) - dim - 1))

    factor_of = one(*shards[0])
    for cut in shards[1:]:
        factor_of = factor_of * one(*cut)
    return factor_of


def bell_draw(own_key, shape, scale, reach, split=(), kind=jnp.bfloat16):
    values = jax.random.normal(own_key, shape, jnp.float32) * scale
    if len(split) > 0:
        values = shard_levels(own_key, shape, split, -0.22, 0.18) * values
    return jnp.clip(values, min=-reach, max=reach).astype(kind)


def gaussian_with(rng, dims, deviation, bound, split, heavy, held_as=jnp.bfloat16):
    entries = deviation * jax.random.normal(rng, dims, jnp.float32)
    if split:
        entries = entries * shard_levels(rng, dims, split, -0.22, 0.18)
    return jnp.clip(spiked(entries, jax.random.fold_in(rng, 3), *heavy), -bound, bound).astype(held_as)


def setup_inputs(seed: int = 0) -> dict:
    seeds = jax.random.split(jax.random.key(seed), 31)
    return {
        "teacher_input": bell_draw(seeds[0], (SEQS, LEN, DT), 1.0, 6.0, ((0, 8), (1, 4))),
        "teacher_upstream": gaussian_with(seeds[1], (SEQS, LEN, DT), 1.0, 6.0, ((0, 8), (1, 4)), (0, 2, 8, 2.0)),
        "teacher_attn_gain": jnp.clip(1.0 + 0.15 * jax.random.normal(seeds[2], (DT,), jnp.float32), 0.25, 1.75).astype(jnp.bfloat16),
        "teacher_attn_shift": bell_draw(seeds[3], (DT,), 0.3, 1.75, ((0, 8),)),
        "teacher_qkv_weight": bell_draw(seeds[4], (3, DT, HT * HD), DT ** -0.5, 0.15625, ((1, 8), (2, 4))),
        "teacher_qv_bias": bell_draw(seeds[5], (2, HT * HD), 0.1, 0.625, ((1, 4),)),
        "teacher_out_weight": bell_draw(seeds[6], (HT * HD, DT), (HT * HD // 64) ** -0.5, 1.25, ((0, 4), (1, 8))),
        "teacher_out_bias": bell_draw(seeds[7], (DT,), 0.3, 1.75, ((0, 8),)),
        "teacher_mlp_gain": jnp.clip(1.0 + 0.15 * jax.random.normal(seeds[8], (DT,), jnp.float32), 0.25, 1.75).astype(jnp.bfloat16),
        "teacher_mlp_shift": bell_draw(seeds[9], (DT,), 0.3, 1.75, ((0, 8),)),
        "teacher_fc_weight": bell_draw(seeds[10], (DT, FT), DT ** -0.5, 0.15625, ((0, 8), (1, 4))),
        "teacher_fc_bias": bell_draw(seeds[11], (FT,), 0.3, 1.75, ((0, 4),)),
        "teacher_proj_weight": bell_draw(seeds[12], (FT, DT), FT ** -0.5, 0.078125, ((0, 4), (1, 8))),
        "teacher_proj_bias": bell_draw(seeds[13], (DT,), 0.3, 1.75, ((0, 8),)),
        "student_input": bell_draw(seeds[14], (SEQS, LEN, DS), 1.0, 6.0, ((0, 8), (1, 4))),
        "student_upstream": gaussian_with(seeds[15], (SEQS, LEN, DS), 1.0, 6.0, ((0, 8), (1, 4)), (0, 2, 8, 2.0)),
        "student_attn_gain": jnp.clip(1.0 + 0.15 * jax.random.normal(seeds[16], (DS,), jnp.float32), 0.25, 1.75).astype(jnp.bfloat16),
        "student_attn_shift": bell_draw(seeds[17], (DS,), 0.3, 1.75, ((0, 8),)),
        "student_qkv_weight": bell_draw(seeds[18], (3, DS, HS * HD), DS ** -0.5, 0.21875, ((1, 8), (2, 4))),
        "student_qv_bias": bell_draw(seeds[19], (2, HS * HD), 0.1, 0.625, ((1, 4),)),
        "student_out_weight": bell_draw(seeds[20], (HS * HD, DS), (HS * HD // 64) ** -0.5, 1.75, ((0, 4), (1, 8))),
        "student_out_bias": bell_draw(seeds[21], (DS,), 0.3, 1.75, ((0, 8),)),
        "student_mlp_gain": jnp.clip(1.0 + 0.15 * jax.random.normal(seeds[22], (DS,), jnp.float32), 0.25, 1.75).astype(jnp.bfloat16),
        "student_mlp_shift": bell_draw(seeds[23], (DS,), 0.3, 1.75, ((0, 8),)),
        "student_fc_weight": bell_draw(seeds[24], (DS, FS), DS ** -0.5, 0.21875, ((0, 8), (1, 4))),
        "student_fc_bias": bell_draw(seeds[25], (FS,), 0.3, 1.75, ((0, 4),)),
        "student_proj_weight": bell_draw(seeds[26], (FS, DS), FS ** -0.5, 0.109375, ((0, 4), (1, 8))),
        "student_proj_bias": bell_draw(seeds[27], (DS,), 0.3, 1.75, ((0, 8),)),
        "span_starts": draw_span_starts(jax.random.fold_in(seeds[30], 71), 0),
        "head_slots": draw_head_slots(jax.random.fold_in(seeds[30], 71), 0),
    }


@jax.custom_vjp
def low(v):
    return lax.optimization_barrier(v.astype(jnp.bfloat16)).astype(jnp.float32)

@jax.custom_vjp
def low_back(v):
    return v

def low_keep(v):
    return (low(v), None)

def low_pass(kept, grad):
    return (grad,)

def back_keep(v):
    return (v, None)

def back_low(kept, grad):
    return (low(grad),)
low.defvjp(low_keep, low_pass)
low_back.defvjp(back_keep, back_low)
highest = lax.Precision.HIGHEST
epsilon = 1e-05

def layer_norm(values, norm_gain, norm_shift):
    center = values - lax.optimization_barrier(jnp.mean(values, axis=-1, keepdims=True))
    spread = lax.optimization_barrier(jnp.mean(center * center, axis=-1, keepdims=True))
    return center * lax.rsqrt(spread + epsilon) * norm_gain + norm_shift

def attend(queries, key_rows, value_rows, starts):
    group_size, length, head_count, head_size = queries.shape
    block_rows = min(512, length)
    score_scale = 1.0 / math.sqrt(head_size)
    key_pos = jnp.arange(length, dtype=jnp.int32)
    key_in = (key_pos[None, :] >= starts[:, None]) & (key_pos[None, :] < starts[:, None] + SPAN)

    def one_block(block_index):
        first_row = block_index * block_rows
        query_block = lax.dynamic_slice_in_dim(queries, first_row, block_rows, 1)
        query_pos = first_row + jnp.arange(block_rows, dtype=jnp.int32)
        query_in = (query_pos[None, :] >= starts[:, None]) & (query_pos[None, :] < starts[:, None] + SPAN)
        visible = (key_pos[None, None, :] <= query_pos[None, :, None]) | query_in[:, :, None] & key_in[:, None, :]
        scores = low_back(jnp.einsum('gqhe,gkhe->ghqk', query_block, key_rows, precision=highest) * score_scale)
        scores = jnp.where(visible[:, None, :, :], scores, -1e+30)
        weights = low(jax.nn.softmax(scores, axis=-1))
        return jnp.einsum('ghqk,gkhe->gqhe', weights, value_rows, precision=highest)
    blocks = lax.map(jax.checkpoint(one_block), jnp.arange(length // block_rows, dtype=jnp.int32))
    return jnp.moveaxis(blocks, 0, 1).reshape(group_size, length, head_count, head_size)

def block_forward(inputs, attn_gain, attn_shift, qkv_weight, qv_bias, out_weight, out_bias, mlp_gain, mlp_shift, fc_weight, fc_bias, proj_weight, proj_bias, starts, head_keep):
    group_size = inputs.shape[0]
    length = inputs.shape[1]
    head_count = head_keep.shape[0]
    normed = low(layer_norm(inputs, attn_gain, attn_shift))
    projected = jnp.einsum('gld,tde->tgle', normed, qkv_weight, precision=highest)
    queries = low(low_back(projected[0] + qv_bias[0]))
    key_rows = low(low_back(projected[1]))
    value_rows = low(low_back(projected[2] + qv_bias[1]))
    head_split = (group_size, length, head_count, HD)
    attended = attend(queries.reshape(head_split), key_rows.reshape(head_split), value_rows.reshape(head_split), starts)
    attended = attended * head_keep.astype(jnp.float32)[None, None, :, None]
    attended = low(low_back(attended.reshape(group_size, length, head_count * HD)))
    branch = low_back(jnp.einsum('gle,ed->gld', attended, out_weight, precision=highest) + out_bias)
    middle = inputs + branch
    normed_two = low(layer_norm(middle, mlp_gain, mlp_shift))
    pre_act = low_back(jnp.einsum('gld,df->glf', normed_two, fc_weight, precision=highest) + fc_bias)
    hidden = low(jax.nn.gelu(pre_act, approximate=True))
    branch_two = low_back(jnp.einsum('glf,fd->gld', hidden, proj_weight, precision=highest) + proj_bias)
    return middle + branch_two

def run_block(inputs, upstream, weight_list, starts, head_keep):
    seq_count = inputs.shape[0]
    group_size = math.gcd(seq_count, 4)
    params = tuple((piece.astype(jnp.float32) for piece in weight_list))

    def scan_step(totals, pieces):
        x_piece, up_piece, start_piece = pieces

        def forward(x_arg, *param_args):
            return block_forward(x_arg, *param_args, start_piece, head_keep)
        result, pullback = jax.vjp(forward, x_piece.astype(jnp.float32), *params)
        gradients = pullback(up_piece.astype(jnp.float32))
        totals = tuple((total + grad_piece for total, grad_piece in zip(totals, gradients[1:])))
        return (totals, (result.astype(jnp.bfloat16), gradients[0].astype(jnp.bfloat16)))
    zero_sums = tuple((jnp.zeros_like(piece) for piece in params))
    grouped = (seq_count // group_size, group_size) + inputs.shape[1:]
    totals, (results, input_grads) = lax.scan(scan_step, zero_sums, (inputs.reshape(grouped), upstream.reshape(grouped), starts.reshape(seq_count // group_size, group_size)))
    return (results.reshape(inputs.shape), input_grads.reshape(inputs.shape), totals)

def reference(teacher_input, teacher_upstream, teacher_attn_gain, teacher_attn_shift, teacher_qkv_weight, teacher_qv_bias, teacher_out_weight, teacher_out_bias, teacher_mlp_gain, teacher_mlp_shift, teacher_fc_weight, teacher_fc_bias, teacher_proj_weight, teacher_proj_bias, student_input, student_upstream, student_attn_gain, student_attn_shift, student_qkv_weight, student_qv_bias, student_out_weight, student_out_bias, student_mlp_gain, student_mlp_shift, student_fc_weight, student_fc_bias, student_proj_weight, student_proj_bias, span_starts, head_slots):
    teacher = run_block(teacher_input, teacher_upstream, (teacher_attn_gain, teacher_attn_shift, teacher_qkv_weight, teacher_qv_bias, teacher_out_weight, teacher_out_bias, teacher_mlp_gain, teacher_mlp_shift, teacher_fc_weight, teacher_fc_bias, teacher_proj_weight, teacher_proj_bias), span_starts, head_slots)
    student = run_block(student_input, student_upstream, (student_attn_gain, student_attn_shift, student_qkv_weight, student_qv_bias, student_out_weight, student_out_bias, student_mlp_gain, student_mlp_shift, student_fc_weight, student_fc_bias, student_proj_weight, student_proj_bias), span_starts, jnp.ones((HS,), jnp.int32))
    teacher_grads = teacher[2]
    student_grads = student[2]
    return (teacher[0], teacher[1], teacher_grads[0], teacher_grads[1], teacher_grads[2], teacher_grads[3], teacher_grads[4], teacher_grads[5], teacher_grads[6], teacher_grads[7], teacher_grads[8], teacher_grads[9], teacher_grads[10], teacher_grads[11], student[0], student[1], student_grads[0], student_grads[1], student_grads[2], student_grads[3], student_grads[4], student_grads[5], student_grads[6], student_grads[7], student_grads[8], student_grads[9], student_grads[10], student_grads[11])
```

```python
import functools

import jax
import jax.numpy as jnp
import numpy as np
from jax import lax
from jax.experimental import pallas as pl
from jax.experimental.pallas import tpu as pltpu
from jax.sharding import Mesh
from jax.sharding import PartitionSpec as P

HD = 64
SPAN = 256


epsilon = 1e-05
negative = -1e30


def layer_norm(values, norm_gain, norm_shift):
    center = values - jnp.mean(values, axis=-1, keepdims=True)
    spread = jnp.mean(center * center, axis=-1, keepdims=True)
    return center * lax.rsqrt(spread + epsilon) * norm_gain + norm_shift


def gelu_tanh(values):
    return jax.nn.gelu(values, approximate=True)


def visibility(first_row, block_rows, length, span_start):
    query_pos = first_row + jnp.arange(block_rows, dtype=jnp.int32)
    key_pos = jnp.arange(length, dtype=jnp.int32)
    query_in = (query_pos >= span_start) & (query_pos < span_start + SPAN)
    key_in = (key_pos >= span_start) & (key_pos < span_start + SPAN)
    return (key_pos[None, :] <= query_pos[:, None]) | query_in[:, None] & key_in[None, :]


def block_scores(query_block, key_rows, visible, score_scale):
    scores = (
        jnp.einsum("qhe,khe->hqk", query_block, key_rows, preferred_element_type=jnp.float32)
        * score_scale
    )
    return jnp.where(visible[None], scores, negative)


def attention_forward(query_rows, key_rows, value_rows, span_start, block_rows, score_scale):
    length = query_rows.shape[0]
    results = []
    log_sums = []
    for block_index in range(length // block_rows):
        first_row = block_index * block_rows
        visible = visibility(first_row, block_rows, length, span_start)
        scores = block_scores(
            query_rows[first_row : first_row + block_rows], key_rows, visible, score_scale
        )
        row_peak = jnp.max(scores, axis=-1, keepdims=True)
        raised = jnp.exp(scores - row_peak)
        row_total = jnp.sum(raised, axis=-1, keepdims=True)
        weights = (raised / row_total).astype(jnp.bfloat16)
        results.append(
            jnp.einsum("hqk,khe->qhe", weights, value_rows, preferred_element_type=jnp.float32)
        )
        log_sums.append(row_peak + jnp.log(row_total))
    return (jnp.concatenate(results, axis=0), log_sums)


def attention_backward(
    query_rows, key_rows, value_rows, log_sums, heads_grad, span_start, block_rows, score_scale
):
    length = query_rows.shape[0]
    query_grads = []
    key_grad = jnp.zeros(key_rows.shape, jnp.float32)
    value_grad = jnp.zeros(value_rows.shape, jnp.float32)
    for block_index in range(length // block_rows):
        first_row = block_index * block_rows
        last_row = first_row + block_rows
        visible = visibility(first_row, block_rows, length, span_start)
        scores = block_scores(query_rows[first_row:last_row], key_rows, visible, score_scale)
        probability = jnp.exp(scores - log_sums[block_index])
        grad_block = heads_grad[first_row:last_row]
        value_grad = value_grad + jnp.einsum(
            "hqk,qhe->khe",
            probability.astype(jnp.bfloat16),
            grad_block,
            preferred_element_type=jnp.float32,
        )
        prob_grad = jnp.einsum(
            "qhe,khe->hqk", grad_block, value_rows, preferred_element_type=jnp.float32
        )
        weighted = jnp.sum(probability * prob_grad, axis=-1, keepdims=True)
        score_grad = (probability * (prob_grad - weighted)).astype(jnp.bfloat16)
        query_grads.append(
            jnp.einsum("hqk,khe->qhe", score_grad, key_rows, preferred_element_type=jnp.float32)
            * score_scale
        )
        key_grad = (
            key_grad
            + jnp.einsum(
                "hqk,qhe->khe",
                score_grad,
                query_rows[first_row:last_row],
                preferred_element_type=jnp.float32,
            )
            * score_scale
        )
    return (jnp.concatenate(query_grads, axis=0), key_grad, value_grad)


def gather_rows(normed):
    return lax.all_gather(normed, "tensor", axis=0, tiled=True)


def gather_grads(branch_grad):
    return lax.all_gather(branch_grad, "tensor", axis=0, tiled=True)


def sum_rows(left_rows, right_weight):
    return lax.psum_scatter(
        jnp.dot(left_rows, right_weight, preferred_element_type=jnp.float32).astype(jnp.bfloat16),
        "tensor",
        scatter_dimension=0,
        tiled=True,
    ).astype(jnp.float32)


def back_rows(grad_stack, weight_stack):
    return lax.psum_scatter(
        jnp.einsum(
            "sle,sde->ld", grad_stack, weight_stack, preferred_element_type=jnp.float32
        ).astype(jnp.bfloat16),
        "tensor",
        scatter_dimension=0,
        tiled=True,
    ).astype(jnp.float32)


def run_block(
    inputs,
    upstream,
    attn_gain,
    attn_shift,
    qkv_weight,
    qv_bias,
    out_weight,
    out_bias,
    mlp_gain,
    mlp_shift,
    fc_weight,
    fc_bias,
    proj_weight,
    proj_bias,
    span_start,
    head_keep,
):
    gathered = (
        lax.all_gather(qkv_weight, "dp", axis=1, tiled=True),
        lax.all_gather(out_weight, "dp", axis=1, tiled=True),
        lax.all_gather(fc_weight, "dp", axis=0, tiled=True),
        lax.all_gather(proj_weight, "dp", axis=1, tiled=True),
        lax.all_gather(attn_gain, "dp", axis=0, tiled=True),
        lax.all_gather(attn_shift, "dp", axis=0, tiled=True),
        lax.all_gather(out_bias, "dp", axis=0, tiled=True),
        lax.all_gather(mlp_gain, "dp", axis=0, tiled=True),
        lax.all_gather(mlp_shift, "dp", axis=0, tiled=True),
        lax.all_gather(proj_bias, "dp", axis=0, tiled=True),
    )
    qkv_full, out_full, fc_full, proj_full = (gathered[0], gathered[1], gathered[2], gathered[3])
    gain_one = gathered[4].astype(jnp.float32)
    shift_one = gathered[5].astype(jnp.float32)
    bias_out = gathered[6].astype(jnp.float32)
    gain_two = gathered[7].astype(jnp.float32)
    shift_two = gathered[8].astype(jnp.float32)
    bias_proj = gathered[9].astype(jnp.float32)
    rows_first = inputs[0].astype(jnp.float32)
    normed, norm_back_one = jax.vjp(layer_norm, rows_first, gain_one, shift_one)
    normed_all = gather_rows(normed.astype(jnp.bfloat16))
    projected = jnp.einsum("ld,tde->tle", normed_all, qkv_full, preferred_element_type=jnp.float32)
    bias_pair = qv_bias.astype(jnp.float32)
    length = normed_all.shape[0]
    head_count = head_keep.shape[0]
    head_split = (length, head_count, HD)
    query_rows = (projected[0] + bias_pair[0]).astype(jnp.bfloat16).reshape(head_split)
    key_rows = projected[1].astype(jnp.bfloat16).reshape(head_split)
    value_rows = (projected[2] + bias_pair[1]).astype(jnp.bfloat16).reshape(head_split)
    block_rows = min(512, length)
    score_scale = 1.0 / HD**0.5
    attended, log_sums = attention_forward(
        query_rows, key_rows, value_rows, span_start, block_rows, score_scale
    )
    keep_float = head_keep.astype(jnp.float32)[None, :, None]
    heads_low = (attended * keep_float).astype(jnp.bfloat16).reshape(length, head_count * HD)
    attn_sum = sum_rows(heads_low, out_full)
    middle = rows_first + (attn_sum + bias_out)
    normed_two, norm_back_two = jax.vjp(layer_norm, middle, gain_two, shift_two)
    normed_two_all = gather_rows(normed_two.astype(jnp.bfloat16))
    hidden_pre = jnp.dot(
        normed_two_all, fc_full, preferred_element_type=jnp.float32
    ) + fc_bias.astype(jnp.float32)
    hidden, gelu_back = jax.vjp(gelu_tanh, hidden_pre)
    hidden_low = hidden.astype(jnp.bfloat16)
    mlp_sum = sum_rows(hidden_low, proj_full)
    result = middle + (mlp_sum + bias_proj)
    outputs = result.astype(jnp.bfloat16)[None]
    grad_result = upstream[0].astype(jnp.float32)
    grad_mlp_all = gather_grads(upstream[0])
    proj_bias_grad = jnp.sum(grad_mlp_all, axis=0, dtype=jnp.float32)
    proj_grad = jnp.einsum(
        "lf,ld->fd", hidden_low, grad_mlp_all, preferred_element_type=jnp.float32
    )
    hidden_grad = jnp.einsum(
        "ld,fd->lf", grad_mlp_all, proj_full, preferred_element_type=jnp.float32
    )
    pre_grad = gelu_back(hidden_grad)[0].astype(jnp.bfloat16)
    fc_bias_grad = jnp.sum(pre_grad, axis=0, dtype=jnp.float32)
    fc_grad = jnp.einsum("ld,lf->df", normed_two_all, pre_grad, preferred_element_type=jnp.float32)
    normed_two_grad = back_rows(pre_grad[None], fc_full[None])
    middle_from_norm, gain_two_grad, shift_two_grad = norm_back_two(normed_two_grad)
    middle_grad = grad_result + middle_from_norm
    grad_attn_all = gather_grads(middle_grad.astype(jnp.bfloat16))
    out_bias_grad = jnp.sum(grad_attn_all, axis=0, dtype=jnp.float32)
    out_grad = jnp.einsum("le,ld->ed", heads_low, grad_attn_all, preferred_element_type=jnp.float32)
    heads_grad = (
        jnp.einsum("ld,ed->le", grad_attn_all, out_full, preferred_element_type=jnp.float32)
        .astype(jnp.bfloat16)
        .reshape(head_split)
    )
    heads_grad = heads_grad * head_keep.astype(jnp.bfloat16)[None, :, None]
    query_grad, key_grad, value_grad = attention_backward(
        query_rows, key_rows, value_rows, log_sums, heads_grad, span_start, block_rows, score_scale
    )
    qkv_low = jnp.stack(
        [
            query_grad.reshape(length, head_count * HD),
            key_grad.reshape(length, head_count * HD),
            value_grad.reshape(length, head_count * HD),
        ]
    ).astype(jnp.bfloat16)
    qv_bias_grad = jnp.stack(
        [
            jnp.sum(qkv_low[0], axis=0, dtype=jnp.float32),
            jnp.sum(qkv_low[2], axis=0, dtype=jnp.float32),
        ]
    )
    qkv_grad = jnp.einsum("ld,tle->tde", normed_all, qkv_low, preferred_element_type=jnp.float32)
    normed_grad = back_rows(qkv_low, qkv_full)
    rows_from_norm, gain_one_grad, shift_one_grad = norm_back_one(normed_grad)
    input_grad = (middle_grad + rows_from_norm).astype(jnp.bfloat16)[None]
    norm_sums = lax.psum((gain_one_grad, shift_one_grad, gain_two_grad, shift_two_grad), "tensor")
    matrices = (
        qkv_grad,
        out_grad,
        fc_grad,
        proj_grad,
        norm_sums[0],
        norm_sums[1],
        out_bias_grad,
        norm_sums[2],
        norm_sums[3],
        proj_bias_grad,
    )
    biases = (qv_bias_grad, fc_bias_grad)
    return (outputs, input_grad, matrices, biases)


def arrange(outputs, input_grad, matrices, biases):
    return (
        outputs,
        input_grad,
        matrices[4],
        matrices[5],
        matrices[0],
        biases[0],
        matrices[1],
        matrices[6],
        matrices[7],
        matrices[8],
        matrices[2],
        biases[1],
        matrices[3],
        matrices[9],
    )


def on_device(
    teacher_input,
    teacher_upstream,
    teacher_attn_gain,
    teacher_attn_shift,
    teacher_qkv_weight,
    teacher_qv_bias,
    teacher_out_weight,
    teacher_out_bias,
    teacher_mlp_gain,
    teacher_mlp_shift,
    teacher_fc_weight,
    teacher_fc_bias,
    teacher_proj_weight,
    teacher_proj_bias,
    student_input,
    student_upstream,
    student_attn_gain,
    student_attn_shift,
    student_qkv_weight,
    student_qv_bias,
    student_out_weight,
    student_out_bias,
    student_mlp_gain,
    student_mlp_shift,
    student_fc_weight,
    student_fc_bias,
    student_proj_weight,
    student_proj_bias,
    span_starts,
    head_slots,
):
    span_start = span_starts[0]
    teacher = run_block(
        teacher_input,
        teacher_upstream,
        teacher_attn_gain,
        teacher_attn_shift,
        teacher_qkv_weight,
        teacher_qv_bias,
        teacher_out_weight,
        teacher_out_bias,
        teacher_mlp_gain,
        teacher_mlp_shift,
        teacher_fc_weight,
        teacher_fc_bias,
        teacher_proj_weight,
        teacher_proj_bias,
        span_start,
        head_slots,
    )
    student_keep = jnp.ones((student_qv_bias.shape[1] // HD,), jnp.int32)
    student = run_block(
        student_input,
        student_upstream,
        student_attn_gain,
        student_attn_shift,
        student_qkv_weight,
        student_qv_bias,
        student_out_weight,
        student_out_bias,
        student_mlp_gain,
        student_mlp_shift,
        student_fc_weight,
        student_fc_bias,
        student_proj_weight,
        student_proj_bias,
        span_start,
        student_keep,
    )
    teach_parts = teacher[2]
    learn_parts = student[2]
    summed = (
        lax.psum_scatter(teach_parts[0], "dp", scatter_dimension=1, tiled=True),
        lax.psum_scatter(teach_parts[1], "dp", scatter_dimension=1, tiled=True),
        lax.psum_scatter(teach_parts[2], "dp", scatter_dimension=0, tiled=True),
        lax.psum_scatter(teach_parts[3], "dp", scatter_dimension=1, tiled=True),
        lax.psum_scatter(teach_parts[4], "dp", scatter_dimension=0, tiled=True),
        lax.psum_scatter(teach_parts[5], "dp", scatter_dimension=0, tiled=True),
        lax.psum_scatter(teach_parts[6], "dp", scatter_dimension=0, tiled=True),
        lax.psum_scatter(teach_parts[7], "dp", scatter_dimension=0, tiled=True),
        lax.psum_scatter(teach_parts[8], "dp", scatter_dimension=0, tiled=True),
        lax.psum_scatter(teach_parts[9], "dp", scatter_dimension=0, tiled=True),
        lax.psum_scatter(learn_parts[0], "dp", scatter_dimension=1, tiled=True),
        lax.psum_scatter(learn_parts[1], "dp", scatter_dimension=1, tiled=True),
        lax.psum_scatter(learn_parts[2], "dp", scatter_dimension=0, tiled=True),
        lax.psum_scatter(learn_parts[3], "dp", scatter_dimension=1, tiled=True),
        lax.psum_scatter(learn_parts[4], "dp", scatter_dimension=0, tiled=True),
        lax.psum_scatter(learn_parts[5], "dp", scatter_dimension=0, tiled=True),
        lax.psum_scatter(learn_parts[6], "dp", scatter_dimension=0, tiled=True),
        lax.psum_scatter(learn_parts[7], "dp", scatter_dimension=0, tiled=True),
        lax.psum_scatter(learn_parts[8], "dp", scatter_dimension=0, tiled=True),
        lax.psum_scatter(learn_parts[9], "dp", scatter_dimension=0, tiled=True),
    )
    totals = lax.psum((teacher[3][0], teacher[3][1], student[3][0], student[3][1]), "dp")
    teacher_matrices = summed[0:10]
    student_matrices = summed[10:20]
    teacher_biases = (totals[0], totals[1])
    student_biases = (totals[2], totals[3])
    return arrange(teacher[0], teacher[1], teacher_matrices, teacher_biases) + arrange(
        student[0], student[1], student_matrices, student_biases
    )


PLANE = ("y", "x", "c")
EVERY = ("y", "x", "c", "z")
TILE = 256


def swap(values, axis):
    return lax.ppermute(values, axis, ((0, 1), (1, 0)))


def ring(values, step):
    return lax.ppermute(values, "z", tuple((i, (i + step) % 4) for i in range(4)))


def cross(values):
    pairs = tuple(
        ((y * 4 + a) * 4 + z, (y * 4 + z) * 4 + a) for y in range(2) for a in range(4) for z in range(4)
    )
    return lax.ppermute(values, EVERY, pairs)


def pick(values, index, axis=0):
    return lax.dynamic_index_in_dim(values, index, axis, keepdims=False)


def wide(values):
    return values.astype(jnp.float32)


def low(values):
    return values.astype(jnp.bfloat16)


def matmul(left, right, left_dim, right_dim):
    return lax.dot_general(
        left, right, (((left_dim,), (right_dim,)), ((), ())), preferred_element_type=jnp.float32
    )


def after(values, *earlier):
    return lax.optimization_barrier((values, *earlier))[0]


def gather_tokens(own):
    other = swap(own, "x")
    return own, other, swap(own, "c"), swap(other, "c")


def scatter_tokens(near, far):
    count = near.shape[0] // 2
    got = swap(far, "c")
    ahead = low(wide(near[count:]) + wide(got[count:]))
    return near, got, swap(ahead, "x")


def plane_out(blocks):
    got = lax.all_to_all(blocks, PLANE, 0, 0)
    return jnp.transpose(got, (1, 0, 2)).reshape(got.shape[1], -1)


def plane_back(rows):
    split = jnp.transpose(rows.reshape(rows.shape[0], 8, -1), (1, 0, 2))
    return lax.all_to_all(split, PLANE, 0, 0)


def ring_pieces(piece):
    held = [piece]
    for _ in range(3):
        held.append(ring(held[-1], 1))
    return held


def ring_sum(parts):
    total = None
    for k in (1, 2, 3):
        part = parts[k] if total is None else parts[k] + wide(total)
        total = ring(low(part), 1)
    return parts[0] + wide(total)


def sum_everywhere(vector):
    for axis in ("c", "x", "y"):
        vector = vector + swap(vector, axis)
    for bit in (1, 2):
        vector = vector + lax.ppermute(vector, "z", tuple((i, i ^ bit) for i in range(4)))
    return vector


def row_call(kernel, name, outs, *args):
    rows = outs[0][0][0]
    size = sum(a.size * a.dtype.itemsize for a in args)

    def spec(shape):
        return pl.BlockSpec((min(shape[0], rows), shape[1]), lambda i: (0, 0))

    return pl.pallas_call(
        kernel,
        grid=(1,),
        in_specs=[spec(a.shape) for a in args],
        out_specs=[spec(shape) for shape, _ in outs],
        out_shape=[jax.ShapeDtypeStruct(shape, dtype) for shape, dtype in outs],
        cost_estimate=pl.CostEstimate(flops=args[0].size * 20, transcendentals=0, bytes_accessed=2 * size),
        name=name,
    )(*args)


def centered(rows):
    center = rows - jnp.mean(rows, axis=-1, keepdims=True)
    spread = jnp.mean(center * center, axis=-1, keepdims=True)
    scale = lax.rsqrt(spread + epsilon)
    return center * scale, scale


def first_norm_kernel(x_ref, gain_ref, shift_ref, out_ref):
    unit, _ = centered(wide(x_ref[...]))
    out_ref[...] = low(unit * gain_ref[...] + shift_ref[...])


def mid_norm_kernel(x_ref, a_ref, b_ref, c_ref, bias_ref, gain_ref, shift_ref, mid_ref, out_ref):
    branch = wide(a_ref[...]) + wide(b_ref[...]) + wide(c_ref[...])
    middle = wide(x_ref[...]) + (branch + bias_ref[...])
    mid_ref[...] = middle
    unit, _ = centered(middle)
    out_ref[...] = low(unit * gain_ref[...] + shift_ref[...])


def norm_back(grad, rows, gain):
    unit, scale = centered(rows)
    t = grad * gain
    back = scale * (
        t - jnp.mean(t, axis=-1, keepdims=True) - unit * jnp.mean(t * unit, axis=-1, keepdims=True)
    )
    return back, jnp.sum(grad * unit, axis=0, keepdims=True), jnp.sum(grad, axis=0, keepdims=True)


def mid_back_kernel(g_ref, a_ref, b_ref, c_ref, mid_ref, gain_ref, dmid_ref, ga_ref, sums_ref):
    up = wide(g_ref[...])
    grad = wide(a_ref[...]) + wide(b_ref[...]) + wide(c_ref[...])
    back, gain_sum, shift_sum = norm_back(grad, mid_ref[...], gain_ref[...])
    dmid = up + back
    dmid_ref[...] = dmid
    ga = low(dmid)
    ga_ref[...] = ga
    sums_ref[0:1] = jnp.sum(wide(ga), axis=0, keepdims=True)
    sums_ref[1:2] = gain_sum
    sums_ref[2:3] = shift_sum
    sums_ref[3:4] = jnp.sum(up, axis=0, keepdims=True)


def first_back_kernel(a_ref, b_ref, c_ref, x_ref, dmid_ref, gain_ref, dx_ref, sums_ref):
    grad = wide(a_ref[...]) + wide(b_ref[...]) + wide(c_ref[...])
    back, gain_sum, shift_sum = norm_back(grad, wide(x_ref[...]), gain_ref[...])
    dx_ref[...] = low(dmid_ref[...] + back)
    sums_ref[0:1] = gain_sum
    sums_ref[1:2] = shift_sum


def place_of(block, rank):
    turn = block ^ rank
    return ((turn & 1) << 1) | (turn >> 1)


def tile_visible(first_key, first_query, start):
    shape = (TILE, TILE)
    key = first_key + lax.broadcasted_iota(jnp.int32, shape, 0)
    query = first_query + lax.broadcasted_iota(jnp.int32, shape, 1)
    key_in = (key >= start) & (key < start + SPAN)
    query_in = (query >= start) & (query < start + SPAN)
    return (key <= query) | (key_in & query_in)


def tile_bounds(block, blocks, start):
    more = (start // TILE == block) & (start % TILE != 0)
    return jnp.minimum(block + 1 + more.astype(jnp.int32), blocks)


def head_lanes(width, head):
    lane = lax.broadcasted_iota(jnp.int32, (1, width), 1)
    return (lane >= head * HD) & (lane < (head + 1) * HD)


def forward_kernel(info_ref, keep_ref, q_ref, k_ref, v_ref, out_ref, log_ref, *, group, blocks):
    width = q_ref.shape[-1]
    block = pl.program_id(1)
    start, rank = info_ref[0], info_ref[1]
    query = q_ref[0]
    queries = [jnp.where(head_lanes(width, h), query, jnp.zeros_like(query)) for h in range(group)]

    def tile(index, carry, masked):
        rows = pl.ds(pl.multiple_of(place_of(index, rank) * TILE, TILE), TILE)
        keys = k_ref[0, rows, :]
        values = v_ref[0, rows, :]
        if masked:
            visible = tile_visible(index * TILE, block * TILE, start)
        out = []
        for h in range(group):
            peak, total, acc = carry[h]
            scores = matmul(keys, queries[h], 1, 1)
            if masked:
                scores = jnp.where(visible, scores, negative)
            new_peak = jnp.maximum(peak, jnp.max(scores, axis=0, keepdims=True))
            decay = jnp.exp(peak - new_peak)
            raised = jnp.exp(scores - new_peak)
            total = total * decay + jnp.sum(raised, axis=0, keepdims=True)
            part = matmul(values, low(raised), 0, 0)
            acc = acc * decay + part[h * HD : (h + 1) * HD]
            out.append((new_peak, total, acc))
        return tuple(out)

    carry = tuple(
        (
            jnp.full((1, TILE), negative, jnp.float32),
            jnp.zeros((1, TILE), jnp.float32),
            jnp.zeros((HD, TILE), jnp.float32),
        )
        for _ in range(group)
    )
    carry = lax.fori_loop(0, block, lambda i, s: tile(i, s, False), carry)
    carry = lax.fori_loop(
        block, tile_bounds(block, blocks, start), lambda i, s: tile(i, s, True), carry
    )
    first = pl.program_id(0) * group
    outs = []
    for h in range(group):
        peak, total, acc = carry[h]
        outs.append(acc * (keep_ref[first + h] / total))
        log_ref[0, h : h + 1, :] = peak + jnp.log(total)
    out_ref[...] = low(jnp.concatenate(outs, axis=0).T)


def backward_kernel(
    info_ref, keep_ref, q_ref, k_ref, v_ref, heads_ref, grad_ref, log_ref,
    dq_ref, dk_ref, dv_ref, dk_sum, dv_sum, *, group, blocks,
):
    width = q_ref.shape[-1]
    block = pl.program_id(1)
    start, rank = info_ref[0], info_ref[1]
    first = pl.program_id(0) * group

    @pl.when(block == 0)
    def _():
        dk_sum[...] = jnp.zeros_like(dk_sum)
        dv_sum[...] = jnp.zeros_like(dv_sum)

    query = q_ref[0]
    grad = grad_ref[...]
    turned = (wide(grad) * wide(heads_ref[...])).T
    queries, grads, weighted, logs = [], [], [], []
    for h in range(group):
        lanes = head_lanes(width, h)
        keep = keep_ref[first + h]
        queries.append(jnp.where(lanes, query, jnp.zeros_like(query)))
        grads.append(low(jnp.where(lanes, wide(grad) * keep, 0.0)))
        weighted.append(keep * jnp.sum(turned[h * HD : (h + 1) * HD], axis=0, keepdims=True))
        logs.append(log_ref[0, h : h + 1, :])

    def tile(index, carry, masked):
        rows = pl.ds(pl.multiple_of(place_of(index, rank) * TILE, TILE), TILE)
        keys = k_ref[0, rows, :]
        values = v_ref[0, rows, :]
        if masked:
            visible = tile_visible(index * TILE, block * TILE, start)
        dk = dv = None
        out = []
        for h in range(group):
            scores = matmul(keys, queries[h], 1, 1)
            if masked:
                scores = jnp.where(visible, scores, negative)
            prob = jnp.exp(scores - logs[h])
            dprob = matmul(values, grads[h], 1, 1)
            dscores = low(prob * (dprob - weighted[h]))
            dv_part = matmul(low(prob), grads[h], 1, 0)
            dk_part = matmul(dscores, queries[h], 1, 0)
            dv = dv_part if dv is None else dv + dv_part
            dk = dk_part if dk is None else dk + dk_part
            out.append(carry[h] + matmul(keys, dscores, 0, 0)[h * HD : (h + 1) * HD])
        dk_sum[rows, :] += dk
        dv_sum[rows, :] += dv
        return tuple(out)

    carry = tuple(jnp.zeros((HD, TILE), jnp.float32) for _ in range(group))
    carry = lax.fori_loop(0, block, lambda i, s: tile(i, s, False), carry)
    carry = lax.fori_loop(
        block, tile_bounds(block, blocks, start), lambda i, s: tile(i, s, True), carry
    )
    dq_ref[...] = low((jnp.concatenate(carry, axis=0) * (1.0 / HD**0.5)).T)

    @pl.when(block == blocks - 1)
    def _():
        dk_ref[...] = low(dk_sum[...])
        dv_ref[...] = low(dv_sum[...])


def attention_plan(columns):
    group = 2 if columns % (2 * HD) == 0 else columns // HD
    return group, group * HD


def attention_specs(columns, length):
    group, width = attention_plan(columns)
    keep = pl.BlockSpec(memory_space=pltpu.SMEM)
    query = pl.BlockSpec((1, TILE, width), lambda g, b, info: (0, place_of(b, info[1]), g))
    keys = pl.BlockSpec((1, length, width), lambda g, b, info: (1, 0, g))
    values = pl.BlockSpec((1, length, width), lambda g, b, info: (2, 0, g))
    rows = pl.BlockSpec((TILE, width), lambda g, b, info: (place_of(b, info[1]), g))
    logs = pl.BlockSpec((1, group, TILE), lambda g, b, info: (g, 0, place_of(b, info[1])))
    whole = pl.BlockSpec((length, width), lambda g, b, info: (0, g))
    return keep, query, keys, values, rows, logs, whole


def attend(info, keep, qkv):
    _, length, columns = qkv.shape
    group, width = attention_plan(columns)
    blocks = length // TILE
    keep_spec, query, keys, values, rows, logs, _ = attention_specs(columns, length)
    pairs = columns // HD * length * length // 2
    return pl.pallas_call(
        functools.partial(forward_kernel, group=group, blocks=blocks),
        grid_spec=pltpu.PrefetchScalarGridSpec(
            num_scalar_prefetch=1,
            grid=(columns // width, blocks),
            in_specs=[keep_spec, query, keys, values],
            out_specs=[rows, logs],
        ),
        out_shape=[
            jax.ShapeDtypeStruct((length, columns), jnp.bfloat16),
            jax.ShapeDtypeStruct((columns // width, group, length), jnp.float32),
        ],
        cost_estimate=pl.CostEstimate(
            flops=pairs * 4 * HD * 4, transcendentals=pairs, bytes_accessed=length * columns * 10
        ),
        name="attend",
    )(info, keep, qkv, qkv, qkv)


def attend_back(info, keep, qkv, heads_out, grads, logs):
    _, length, columns = qkv.shape
    group, width = attention_plan(columns)
    blocks = length // TILE
    keep_spec, query, keys, values, rows, logs_spec, whole = attention_specs(columns, length)
    pairs = columns // HD * length * length // 2
    flat = jax.ShapeDtypeStruct((length, columns), jnp.bfloat16)
    return pl.pallas_call(
        functools.partial(backward_kernel, group=group, blocks=blocks),
        grid_spec=pltpu.PrefetchScalarGridSpec(
            num_scalar_prefetch=1,
            grid=(columns // width, blocks),
            in_specs=[keep_spec, query, keys, values, rows, rows, logs_spec],
            out_specs=[rows, whole, whole],
            scratch_shapes=[
                pltpu.VMEM((length, width), jnp.float32),
                pltpu.VMEM((length, width), jnp.float32),
            ],
        ),
        out_shape=[flat, flat, flat],
        cost_estimate=pl.CostEstimate(
            flops=pairs * 10 * HD * 4, transcendentals=pairs, bytes_accessed=length * columns * 20
        ),
        name="attend_back",
    )(info, keep, qkv, qkv, qkv, heads_out, grads, logs)


ANY = pl.BlockSpec(memory_space=pl.ANY)
VMEM = pl.BlockSpec(memory_space=pltpu.VMEM)
LIMIT = 56 << 20


def fetch(parts, into, sem):
    first = 0
    for part in parts:
        rows = part.shape[0]
        pltpu.make_async_copy(part, into.at[pl.ds(first, rows)], sem).start()
        first += rows


def fetched(into, sem):
    pltpu.make_async_copy(into, into, sem).wait()


def send(source, into, sem):
    copy = pltpu.make_async_copy(source, into, sem)
    copy.start()
    return copy


def scratch(*shape):
    return pltpu.VMEM(shape, jnp.bfloat16)


def matmul_call(kernel, name, outs, args, specs, scratches, flops):
    size = sum(a.size * a.dtype.itemsize for a in args)
    return pl.pallas_call(
        kernel,
        in_specs=specs,
        out_specs=[spec for _, _, spec in outs],
        out_shape=[jax.ShapeDtypeStruct(shape, dtype) for shape, dtype, _ in outs],
        scratch_shapes=scratches,
        compiler_params=pltpu.CompilerParams(vmem_limit_bytes=LIMIT),
        cost_estimate=pl.CostEstimate(flops=flops, transcendentals=0, bytes_accessed=2 * size),
        name=name,
    )(*args)


def project(pieces, weights, places, bias, columns):
    count, width = pieces[0].shape
    length = 4 * count
    scales = (1.0 / HD**0.5, 1.0, 1.0)

    def kernel(*refs):
        piece_refs, refs = refs[:4], refs[4:]
        weight_refs, refs = refs[: len(weights)], refs[len(weights) :]
        bias_ref, qkv_ref, all_ref, full_ref, rows_s, full_s, qkv_s, sems, outs = refs
        for array, index, row, matrix, column, rows in places:
            source = weight_refs[array]
            source = source if index is None else source.at[index]
            pltpu.make_async_copy(
                source.at[pl.ds(row, rows)], full_s.at[matrix, pl.ds(column, rows)], sems.at[0]
            ).start()
        fetch(piece_refs, rows_s, sems.at[1])
        fetched(full_s, sems.at[0])
        fetched(rows_s, sems.at[1])
        sent = [send(full_s, full_ref, outs.at[0]), send(rows_s, all_ref, outs.at[1])]

        @pl.loop(0, 4)
        def _(block):
            rows = pl.ds(pl.multiple_of(block * count, count), count)
            for t in range(3):
                part = low(matmul(rows_s[rows, :], full_s[t], 1, 1) + bias_ref[t])
                qkv_s[t, rows, :] = low(wide(part) * scales[t])

        sent.append(send(qkv_s, qkv_ref, outs.at[2]))
        for copy in sent:
            copy.wait()

    return matmul_call(
        kernel,
        "project",
        [
            ((3, length, columns), jnp.bfloat16, ANY),
            ((length, width), jnp.bfloat16, ANY),
            ((4, columns, width), jnp.bfloat16, ANY),
        ],
        [*pieces, *weights, bias],
        [ANY] * (4 + len(weights)) + [VMEM],
        [
            scratch(length, width), scratch(4, columns, width), scratch(3, length, columns),
            pltpu.SemaphoreType.DMA((2,)), pltpu.SemaphoreType.DMA((3,)),
        ],
        6 * length * columns * width,
    )


def near_far(lefts, rights, name):
    length = lefts[0].shape[0]
    width = rights[0].shape[-1]
    half = length // 2
    count = length // 4
    pairs = len(lefts)

    def kernel(*refs):
        left_refs, refs = refs[:pairs], refs[pairs:]
        right_refs, refs = refs[:pairs], refs[pairs:]
        near_ref, far_ref = refs
        block = pl.program_id(0)
        total = matmul(left_refs[0][...], right_refs[0][...], 1, 0)
        for i in range(1, pairs):
            total = total + matmul(left_refs[i][...], right_refs[i][...], 1, 0)
        total = low(total)

        @pl.when(block < 2)
        def _():
            near_ref[...] = total

        @pl.when(block >= 2)
        def _():
            far_ref[...] = total

    left_specs = [pl.BlockSpec((count, left.shape[1]), lambda i: (i, 0)) for left in lefts]
    right_specs = []
    for right, index in zip(rights, name[1]):
        right_specs.append(pl.BlockSpec((None,) + right.shape[1:], lambda i, index=index: (index, 0, 0)))
    return pl.pallas_call(
        kernel,
        grid=(4,),
        in_specs=left_specs + right_specs,
        out_specs=[
            pl.BlockSpec((count, width), lambda i: (jnp.minimum(i, 1), 0)),
            pl.BlockSpec((count, width), lambda i: (jnp.maximum(i - 2, 0), 0)),
        ],
        out_shape=[jax.ShapeDtypeStruct((half, width), jnp.bfloat16)] * 2,
        cost_estimate=pl.CostEstimate(
            flops=2 * pairs * length * lefts[0].shape[1] * width,
            transcendentals=0,
            bytes_accessed=2 * pairs * (length + width) * lefts[0].shape[1] + 2 * length * width,
        ),
        compiler_params=pltpu.CompilerParams(vmem_limit_bytes=LIMIT),
        name=name[0],
    )(*lefts, *rights)


def gelu_pair(u):
    k = 0.7978845608028654
    t = jnp.tanh(k * (u + 0.044715 * (u * u * u)))
    value = 0.5 * u * (1.0 + t)
    slope = 0.5 * (1.0 + t) + 0.5 * u * (1.0 - t * t) * (k * (1.0 + 3 * 0.044715 * (u * u)))
    return value, slope


def mlp_main(rows, grads, weights, first, bias):
    count, width = rows[0].shape
    length = 4 * count
    units = (weights[0].shape[0] - first) // 2
    hidden = 8 * units
    half = length // 2

    def kernel(*refs):
        row_refs, grad_refs, weight_refs, refs = refs[:4], refs[4:8], refs[8:16], refs[16:]
        bias_ref, refs = refs[0], refs[1:]
        rows_ref, grads_ref, hidden_ref, pre_ref, near_ref, far_ref, sum_ref = refs[:7]
        rows_s, grads_s, fc_s, proj_s, hidden_s, slope_s, back_s, sems, outs = refs[7:]
        fetch([w.at[pl.ds(first, units)] for w in weight_refs], fc_s, sems.at[0])
        fetch(row_refs, rows_s, sems.at[1])
        fetch([w.at[pl.ds(first + units, units)] for w in weight_refs], proj_s, sems.at[2])
        fetch(grad_refs, grads_s, sems.at[3])
        fetched(fc_s, sems.at[0])
        fetched(rows_s, sems.at[1])
        sent = [send(rows_s, rows_ref, outs.at[0])]

        @pl.loop(0, 4)
        def _(block):
            at = pl.ds(pl.multiple_of(block * count, count), count)
            value, slope = gelu_pair(matmul(rows_s[at, :], fc_s[...], 1, 1) + bias_ref[...])
            hidden_s[at, :] = low(value)
            slope_s[at, :] = low(slope)

        sent.append(send(hidden_s, hidden_ref, outs.at[1]))
        fetched(proj_s, sems.at[2])
        fetched(grads_s, sems.at[3])
        sent.append(send(grads_s, grads_ref, outs.at[2]))
        sum_ref[...] = jnp.zeros_like(sum_ref)

        @pl.loop(0, 4)
        def _(block):
            at = pl.ds(pl.multiple_of(block * count, count), count)
            pre = low(matmul(grads_s[at, :], proj_s[...], 1, 1) * wide(slope_s[at, :]))
            slope_s[at, :] = pre
            sum_ref[...] += jnp.sum(wide(pre), axis=0, keepdims=True)
            back_s[at, :] = low(matmul(pre, fc_s[...], 1, 0))

        sent.append(send(slope_s, pre_ref, outs.at[3]))
        sent.append(send(back_s.at[pl.ds(0, half)], near_ref, outs.at[4]))
        sent.append(send(back_s.at[pl.ds(half, half)], far_ref, outs.at[5]))
        for copy in sent:
            copy.wait()

    def out(rows, columns):
        return ((rows, columns), jnp.bfloat16, ANY)

    return matmul_call(
        kernel,
        "mlp_main",
        [
            out(length, width), out(length, width), out(length, hidden), out(length, hidden),
            out(half, width), out(half, width), ((1, hidden), jnp.float32, VMEM),
        ],
        [*rows, *grads, *weights, bias],
        [ANY] * 16 + [VMEM],
        [
            scratch(length, width), scratch(length, width), scratch(hidden, width), scratch(hidden, width),
            scratch(length, hidden), scratch(length, hidden), scratch(length, width),
            pltpu.SemaphoreType.DMA((4,)), pltpu.SemaphoreType.DMA((6,)),
        ],
        6 * length * hidden * width,
    )


def mlp_rest(rows, grads, hidden, pre, weights, first):
    length, width = rows.shape
    units = (weights[0].shape[0] - first) // 2
    total = 8 * units
    half = length // 2
    count = length // 4
    tile = 256

    def kernel(*refs):
        rows_ref, grads_ref, hidden_ref, pre_ref = refs[:4]
        weight_refs, refs = refs[4:12], refs[12:]
        near_ref, far_ref, fc_one, fc_two, proj_one, proj_two = refs[:6]
        rows_s, grads_s, hidden_s, pre_s, proj_s, ahead_s, fc_s, back_s, sems, outs = refs[6:]
        fetch([hidden_ref], hidden_s, sems.at[0])
        fetch([w.at[pl.ds(first + units, units)] for w in weight_refs], proj_s, sems.at[1])
        fetch([pre_ref], pre_s, sems.at[2])
        fetch([rows_ref], rows_s, sems.at[3])
        fetch([grads_ref], grads_s, sems.at[4])
        fetched(hidden_s, sems.at[0])
        fetched(proj_s, sems.at[1])

        @pl.loop(0, 4)
        def _(block):
            at = pl.ds(pl.multiple_of(block * count, count), count)
            ahead_s[at, :] = low(matmul(hidden_s[at, :], proj_s[...], 1, 0))

        sent = [
            send(ahead_s.at[pl.ds(0, half)], near_ref, outs.at[0]),
            send(ahead_s.at[pl.ds(half, half)], far_ref, outs.at[1]),
        ]
        fetched(pre_s, sems.at[2])
        fetched(rows_s, sems.at[3])

        @pl.loop(0, total // tile)
        def _(block):
            at = pl.ds(pl.multiple_of(block * tile, tile), tile)
            fc_s[at, :] = low(matmul(pre_s[:, at], rows_s[...], 0, 0))

        sent.append(send(fc_s.at[pl.ds(0, total // 2)], fc_one, outs.at[2]))
        sent.append(send(fc_s.at[pl.ds(total // 2, total // 2)], fc_two, outs.at[3]))
        fetched(grads_s, sems.at[4])

        @pl.loop(0, total // tile)
        def _(block):
            at = pl.ds(pl.multiple_of(block * tile, tile), tile)
            back_s[at, :] = low(matmul(hidden_s[:, at], grads_s[...], 0, 0))

        sent.append(send(back_s.at[pl.ds(0, total // 2)], proj_one, outs.at[4]))
        sent.append(send(back_s.at[pl.ds(total // 2, total // 2)], proj_two, outs.at[5]))
        for copy in sent:
            copy.wait()

    def out(rows):
        return ((rows, width), jnp.bfloat16, ANY)

    return matmul_call(
        kernel,
        "mlp_rest",
        [out(half), out(half)] + [out(total // 2)] * 4,
        [rows, grads, hidden, pre, *weights],
        [ANY] * 12,
        [
            scratch(length, width), scratch(length, width), scratch(length, total), scratch(length, total),
            scratch(total, width), scratch(length, width), scratch(total, width), scratch(total, width),
            pltpu.SemaphoreType.DMA((5,)), pltpu.SemaphoreType.DMA((6,)),
        ],
        6 * length * total * width,
    )


def heads_back(pieces, weights):
    count, width = pieces[0].shape
    length = 4 * count
    columns = weights.shape[1]

    def kernel(*refs):
        piece_refs, (weight_ref, grad_ref, all_ref, rows_s, out_s, sems, outs) = refs[:4], refs[4:]
        fetch([weight_ref.at[3]], out_s, sems.at[0])
        fetch(piece_refs, rows_s, sems.at[1])
        fetched(out_s, sems.at[0])
        fetched(rows_s, sems.at[1])
        copy = send(rows_s, all_ref, outs.at[0])

        @pl.loop(0, 4)
        def _(block):
            at = pl.ds(pl.multiple_of(block * count, count), count)
            grad_ref[at, :] = low(matmul(rows_s[at, :], out_s[...], 1, 1))

        copy.wait()

    return matmul_call(
        kernel,
        "heads_back",
        [((length, columns), jnp.bfloat16, VMEM), ((length, width), jnp.bfloat16, ANY)],
        [*pieces, weights],
        [ANY] * 5,
        [
            scratch(length, width), scratch(columns, width),
            pltpu.SemaphoreType.DMA((2,)), pltpu.SemaphoreType.DMA((1,)),
        ],
        2 * length * columns * width,
    )


def head_weight_grads(lefts, rows, grad_rows, places, outs):
    length, columns = lefts[0].shape
    width = rows.shape[1]

    def kernel(*refs):
        left_refs, (rows_ref, grads_ref), refs = refs[:4], refs[4:6], refs[6:]
        out_refs, (full_s, sem) = refs[: len(outs)], refs[len(outs) :]
        for matrix in range(4):
            right = (rows_ref if matrix < 3 else grads_ref)[...]
            full_s[matrix] = low(matmul(left_refs[matrix][...], right, 0, 0))
        for array, index, row, matrix, column, count in places:
            into = out_refs[array]
            into = into if index is None else into.at[index]
            pltpu.make_async_copy(
                full_s.at[matrix, pl.ds(column, count)], into.at[pl.ds(row, count)], sem.at[0]
            ).start()
        pltpu.make_async_copy(full_s, full_s, sem.at[0]).wait()

    return matmul_call(
        kernel,
        "head_weight_grads",
        [(shape, jnp.bfloat16, ANY) for shape in outs],
        [*lefts, rows, grad_rows],
        [VMEM] * 6,
        [scratch(4, columns, width), pltpu.SemaphoreType.DMA((1,))],
        8 * length * columns * width,
    )


def teacher_blocks(qkv, out, fc, proj):
    columns, shard = out.shape
    stack = jnp.concatenate([jnp.transpose(qkv, (0, 2, 1)), out[None]], axis=0)
    stack = stack.reshape(4, 2, columns // (2 * HD), 2, 2, HD // 4, shard)
    stack = jnp.transpose(stack, (3, 1, 4, 0, 2, 5, 6)).reshape(8, -1, shard)
    return jnp.concatenate(
        [stack, jnp.transpose(fc).reshape(8, -1, shard), proj.reshape(8, -1, shard)], axis=1
    )


def teacher_unblock(heads, hidden):
    shard = heads.shape[-1]
    stack = heads.reshape(2, 2, 2, 4, -1, HD // 4, shard)
    stack = jnp.transpose(stack, (3, 1, 4, 0, 2, 5, 6)).reshape(4, -1, shard)
    hidden = hidden.reshape(8, 2, -1, shard)
    return stack, hidden[:, 0].reshape(-1, shard), hidden[:, 1].reshape(-1, shard)


def student_blocks(qkv, out, fc, proj):
    columns, shard = out.shape
    stack = jnp.concatenate([jnp.transpose(qkv, (0, 2, 1)), out[None]], axis=0)
    stack = stack.reshape(4, columns // HD, 8, HD // 8, shard)
    stack = jnp.transpose(stack, (2, 0, 1, 3, 4)).reshape(8, -1, shard)
    return jnp.concatenate(
        [stack, jnp.transpose(fc).reshape(8, -1, shard), proj.reshape(8, -1, shard)], axis=1
    )


def student_unblock(heads, hidden):
    shard = heads.shape[-1]
    stack = jnp.transpose(heads.reshape(8, 4, -1, HD // 8, shard), (1, 2, 0, 3, 4)).reshape(4, -1, shard)
    hidden = hidden.reshape(8, 2, -1, shard)
    return stack, hidden[:, 0].reshape(-1, shard), hidden[:, 1].reshape(-1, shard)


def hidden_sum(fc_near, fc_far, proj_near, proj_far, start=None):
    units = fc_near.shape[0] // 4
    fc_got, proj_got = swap(fc_far, "y"), swap(proj_far, "y")
    parts = []
    for k in range(4):
        at = slice(k * units, (k + 1) * units)
        parts.append(
            jnp.concatenate(
                [wide(fc_near[at]) + wide(fc_got[at]), wide(proj_near[at]) + wide(proj_got[at])], axis=0
            )
        )
    return ring_sum(parts)


def teacher_places(columns):
    sub = HD // 4
    heads = columns // (2 * HD)
    places = []
    for matrix in range(4):
        for plane in range(2):
            for head in range(heads):
                for dc in range(2):
                    for dy in range(2):
                        column = (plane * heads + head) * HD + (dc * 2 + dy) * sub
                        places.append((dc * 2 + dy, plane, (matrix * heads + head) * sub, matrix, column, sub))
    return places


def student_places(columns):
    sub = HD // 8
    heads = columns // HD
    places = []
    for matrix in range(4):
        for head in range(heads):
            for part in range(8):
                places.append((part, None, (matrix * heads + head) * sub, matrix, head * HD + part * sub, sub))
    return places


def student_grad_places(columns):
    return [(p // 4, p % 4, row, matrix, column, sub) for p, _, row, matrix, column, sub in student_places(columns)]


def teacher_heads(piece, pos):
    first = pos["c"] == 0
    held = ring_pieces(piece)
    over = [swap(part, "y") for part in held]

    def halves(parts):
        front, rear = jnp.stack(parts[:2]), jnp.stack(parts[2:])
        return jnp.where(first, front, rear), swap(jnp.where(first, rear, front), "c")

    own, near = halves(held)
    own_over, near_over = halves(over)
    return held, (own, own_over, near, near_over)


def teacher_heads_sum(parts, pos):
    first = pos["c"] == 0

    def planes(own, give):
        got = swap(give, "c")
        return jnp.where(first, own, got), jnp.where(first, got, own)

    front, rear = planes(parts[0], parts[2])
    front_over, rear_over = planes(parts[1], parts[3])
    front_got, rear_got = swap(front_over, "y"), swap(rear_over, "y")
    sums = [wide(front[k]) + wide(front_got[k]) for k in range(2)]
    sums += [wide(rear[k]) + wide(rear_got[k]) for k in range(2)]
    return ring_sum(sums)


def student_heads_sum(near, far):
    got = swap(far, "y")
    return ring_sum([wide(near[k]) + wide(got[k]) for k in range(4)])


def block_front(rows, vectors, keep, qv_bias, info, head_weights, places, columns):
    gain_one, shift_one = vectors[:2]
    full16 = (rows.shape, jnp.bfloat16)
    (normed,) = row_call(first_norm_kernel, "first_norm", [full16], rows, gain_one, shift_one)
    bias3 = jnp.stack([qv_bias[0], jnp.zeros_like(qv_bias[0]), qv_bias[1]])[:, None, :]
    qkv, normed_all, weights = project(gather_tokens(normed), head_weights, places, bias3, columns)
    heads_low, logs = attend(info, keep, qkv)
    near, far = near_far([heads_low], [weights], ("out_project", (3,)))
    return scatter_tokens(near, far), (qkv, normed_all, weights, heads_low, logs)


def block_middle(rows, branch, grad_all, vectors, fc_bias, hidden_weights, first):
    bias_out, gain_two, shift_two = vectors[2:5]
    full32, full16 = (rows.shape, jnp.float32), (rows.shape, jnp.bfloat16)
    middle, normed_two = row_call(
        mid_norm_kernel, "mid_norm", [full32, full16], rows, *branch, bias_out, gain_two, shift_two
    )
    rows_all, grads_all, hidden, pre, near, far, fc_bias_grad = mlp_main(
        gather_tokens(normed_two), grad_all, hidden_weights, first, fc_bias
    )
    return middle, scatter_tokens(near, far), (rows_all, grads_all, hidden, pre), fc_bias_grad[0]


def block_ahead(middle, saved, hidden_weights, first, bias_proj):
    near, far, *grads = mlp_rest(*saved, hidden_weights, first)
    near, got, over = scatter_tokens(near, far)
    count = middle.shape[0]
    ahead = wide(near[:count]) + wide(got[:count]) + wide(over)
    return low(middle + (ahead + bias_proj)), grads


def block_turn(grad_rows, back, middle, gain_two):
    width = middle.shape[1]
    full32, full16 = (middle.shape, jnp.float32), (middle.shape, jnp.bfloat16)
    return row_call(
        mid_back_kernel, "mid_back", [full32, full16, ((4, width), jnp.float32)], grad_rows, *back, middle, gain_two
    )


def block_back(attn_grad, saved, keep, info):
    qkv, normed_all, weights, heads_low, logs = saved
    heads_grad, attn_grad_all = heads_back(gather_tokens(attn_grad), weights)
    dq, dk, dv = attend_back(info, keep, qkv, heads_low, heads_grad, logs)
    near, far = near_far([dq, dk, dv], [weights] * 3, ("rows_back", (0, 1, 2)))
    return scatter_tokens(near, far), (dq, dk, dv, heads_low, normed_all, attn_grad_all)


def block_head_grads(saved, places, outs):
    dq, dk, dv, heads_low, normed_all, attn_grad_all = saved
    grads = head_weight_grads([dq, dk, dv, heads_low], normed_all, attn_grad_all, places, outs)
    qv_bias_grad = jnp.stack([jnp.sum(wide(dq), axis=0), jnp.sum(wide(dv), axis=0)])
    return grads, qv_bias_grad


def block_end(back, rows, dmid, gain_one):
    width = rows.shape[1]
    return row_call(
        first_back_kernel, "first_back", [(rows.shape, jnp.bfloat16), ((2, width), jnp.float32)],
        *back, rows, dmid, gain_one,
    )


def on_pairs(*args):
    teacher_in, student_in = args[0:14], args[14:28]
    span_starts, head_slots = args[28], args[29]
    pos = {name: lax.axis_index(name) for name in EVERY}
    rank = pos["x"] * 2 + pos["c"]

    teacher_piece = plane_out(teacher_blocks(teacher_in[4], teacher_in[6], teacher_in[10], teacher_in[12]))
    student_piece = plane_out(student_blocks(student_in[4], student_in[6], student_in[10], student_in[12]))
    teacher_columns, student_columns = teacher_in[6].shape[0], student_in[6].shape[0]
    teacher_rows = cross(teacher_in[0][0])
    student_rows = cross(student_in[0][0])
    head_rows = student_columns // 2
    teacher_head_rows = teacher_columns // 2
    held, teacher_head_weights = teacher_heads(teacher_piece[:teacher_head_rows], pos)
    student_piece = jnp.concatenate([cross(student_piece[:head_rows]), student_piece[head_rows:]], axis=0)
    student_piece = after(student_piece, held[2])
    held = ring_pieces(student_piece)
    student_weights = held + [swap(piece, "y") for piece in held]
    hidden_piece = after(teacher_piece[teacher_head_rows:], held[2])
    held = ring_pieces(hidden_piece)
    teacher_weights = held + [swap(piece, "y") for piece in held]
    teacher_up, student_up = cross(after(teacher_in[1][0], held[1])), cross(after(student_in[1][0], held[1]))
    teacher_grad_all, student_grad_all = gather_tokens(teacher_up), gather_tokens(student_up)

    order = (2, 3, 7, 8, 9, 13)
    tall = jnp.concatenate(
        [jnp.stack([block[i] for i in order]) for block in (teacher_in, student_in)], axis=1
    )
    marks = jnp.stack([span_starts[0] // 32, span_starts[0] % 32]).astype(jnp.bfloat16)
    packed = jnp.concatenate([tall, jnp.broadcast_to(marks[:, None], (2, tall.shape[1]))], axis=0)[None]
    for axis in ("c", "x", "y"):
        other = swap(packed, axis)
        here = pos[axis] == 0
        packed = jnp.concatenate([jnp.where(here, packed, other), jnp.where(here, other, packed)], axis=0)
    shard = teacher_in[2].shape[0]

    def width_vectors(block):
        block = wide(jnp.transpose(block[:, :6], (1, 0, 2)).reshape(6, 1, -1))
        return tuple(block[i] for i in range(6))

    teacher_vectors = width_vectors(packed[:, :, :shard])
    student_vectors = width_vectors(packed[:, :, shard:])
    starts = packed[:, 6:, 0].astype(jnp.int32)
    starts = starts[:, 0] * 32 + starts[:, 1]
    info = jnp.stack([pick(starts, pos["y"] * 4 + pos["z"]), rank])

    parts = [
        teacher_in[11], teacher_in[5].reshape(-1), student_in[11], student_in[5].reshape(-1),
        jnp.pad(head_slots.astype(jnp.bfloat16), (0, 128 - head_slots.shape[0])),
    ]
    limits = np.cumsum([0] + [part.shape[0] // 128 for part in parts])
    deep = jnp.concatenate([part.reshape(-1, 128) for part in parts], axis=0)
    deep = jnp.stack([deep] + [ring(deep, step) for step in (1, 2, 3)])
    deep = [deep[:, limits[i] : limits[i + 1]].reshape(4, -1) for i in range(5)]
    y, x, c, z = pos["y"], pos["x"], pos["c"], pos["z"]
    near_y = jnp.stack([y, 1 - y])
    near_c = jnp.stack([c, 1 - c])
    planes = (z - jnp.arange(4)) % 4
    device_of = near_y * 4 + rank
    hidden_hot = (jnp.arange(8)[None] == device_of[:, None]).astype(jnp.bfloat16)

    def hidden_bias(block):
        block = block.reshape(4, 8, -1)
        return jnp.einsum("dp,kpi->dki", hidden_hot, block, preferred_element_type=jnp.float32).reshape(1, -1)

    teacher_fc_bias, student_fc_bias = hidden_bias(deep[0]), hidden_bias(deep[2])
    two = jnp.where(c == 0, 0, 2)
    block = lax.dynamic_slice_in_dim(deep[1].reshape(4, -1), two, 2, 0)
    block = block.reshape(2, 2, 2, -1, 2, 2, HD // 4)
    block = pick(block, x, 2)
    block = jnp.where(y == 0, block, block[:, :, :, ::-1])
    block = jnp.where(c == 0, block, block[:, :, :, :, ::-1])
    teacher_qv = wide(jnp.transpose(block, (1, 0, 2, 4, 3, 5)).reshape(2, -1))
    slots = lax.dynamic_slice_in_dim(deep[4][:, : head_slots.shape[0]], two, 2, 0)
    keep = wide(pick(slots.reshape(2, 2, -1), x, 1).reshape(-1))
    block = pick(deep[3].reshape(4, 2, -1, 8, HD // 8), (z - rank) % 4)
    eighth = (near_y[:, None] * 4 + planes[None]).reshape(-1)
    order_hot = (jnp.arange(8)[None] == eighth[:, None]).astype(jnp.bfloat16)
    student_qv = jnp.einsum("rp,thpi->thri", order_hot, block, preferred_element_type=jnp.float32).reshape(2, -1)
    ones = jnp.ones((student_qv.shape[1] // HD,), jnp.float32)

    teacher_spots, student_spots = teacher_places(teacher_columns), student_places(student_columns)
    teacher_branch, teacher_saved = block_front(
        teacher_rows, teacher_vectors, keep, teacher_qv, info, teacher_head_weights, teacher_spots, teacher_columns
    )
    student_branch, student_saved = block_front(
        student_rows, student_vectors, ones, student_qv, info, student_weights, student_spots, student_columns
    )
    teacher_middle, teacher_back, teacher_mlp, teacher_fc = block_middle(
        teacher_rows, teacher_branch, teacher_grad_all, teacher_vectors, teacher_fc_bias, teacher_weights, 0
    )
    student_middle, student_back, student_mlp, student_fc = block_middle(
        student_rows, student_branch, student_grad_all, student_vectors, student_fc_bias, student_weights, head_rows
    )
    teacher_dmid, teacher_ga, teacher_two = block_turn(teacher_up, teacher_back, teacher_middle, teacher_vectors[3])
    student_dmid, student_ga, student_two = block_turn(student_up, student_back, student_middle, student_vectors[3])
    teacher_out, teacher_hidden = block_ahead(
        teacher_middle, teacher_mlp, teacher_weights, 0, teacher_vectors[5]
    )
    student_out, student_hidden = block_ahead(
        student_middle, student_mlp, student_weights, head_rows, student_vectors[5]
    )
    teacher_back, teacher_saved = block_back(teacher_ga, teacher_saved, keep, info)
    student_back, student_saved = block_back(student_ga, student_saved, ones, info)
    teacher_dx, teacher_one = block_end(teacher_back, teacher_rows, teacher_dmid, teacher_vectors[0])
    student_dx, student_one = block_end(student_back, student_rows, student_dmid, student_vectors[0])

    teacher_width, student_width = teacher_rows.shape[1], student_rows.shape[1]
    teacher_hidden = plane_back(low(hidden_sum(*teacher_hidden)))
    teacher_head, teacher_qv_grad = block_head_grads(
        teacher_saved, teacher_spots, [(2, teacher_head_rows, teacher_width)] * 4
    )
    teacher_head = plane_back(low(teacher_heads_sum(teacher_head, pos)))
    teacher_grads = teacher_unblock(teacher_head, teacher_hidden)
    student_hidden = low(hidden_sum(*student_hidden))
    student_head, student_qv_grad = block_head_grads(
        student_saved, student_grad_places(student_columns), [(4, head_rows, student_width)] * 2
    )
    student_head = cross(low(student_heads_sum(*student_head)))
    got = plane_back(jnp.concatenate([student_head, student_hidden], axis=0))
    student_grads = student_unblock(got[:, :head_rows], got[:, head_rows:])
    student_out, student_dx = cross(student_out)[None], cross(student_dx)[None]
    teacher_out, teacher_dx = cross(teacher_out)[None], cross(teacher_dx)[None]

    def matrices(grads):
        stack, fc_grad, proj_grad = grads
        return (
            wide(jnp.transpose(stack[:3], (0, 2, 1))), wide(stack[3]),
            wide(jnp.transpose(fc_grad)), wide(proj_grad),
        )

    def spread(places, values):
        hot = (jnp.arange(32)[:, None] == places[None]).astype(jnp.float32)
        return jnp.dot(hot, values, precision=lax.Precision.HIGHEST)

    hidden_places = (planes[None] * 8 + near_y[:, None] * 4 + rank).reshape(-1)
    head_planes = planes.reshape(2, 2)
    head_planes = jnp.where(c == 0, head_planes[0], head_planes[1])
    teacher_spots = (
        head_planes[:, None, None] * 8 + x * 4 + near_y[None, None, :] * 2 + near_c[None, :, None]
    ).reshape(-1)
    student_spots = rank * 8 + eighth

    teacher_qv_grad = teacher_qv_grad.reshape(2, 2, -1, 2, 2, HD // 4)
    teacher_qv_grad = jnp.transpose(teacher_qv_grad, (1, 3, 4, 0, 2, 5)).reshape(8, -1)
    student_qv_grad = jnp.transpose(student_qv_grad.reshape(2, -1, 8, HD // 8), (2, 0, 1, 3)).reshape(8, -1)
    pieces = [
        spread(hidden_places, teacher_fc.reshape(8, -1)),
        spread(hidden_places, student_fc.reshape(8, -1)),
        spread(teacher_spots, teacher_qv_grad),
        spread(student_spots, student_qv_grad),
        teacher_one, teacher_two, student_one, student_two,
    ]
    limits = np.cumsum([0] + [piece.size for piece in pieces])
    total = sum_everywhere(jnp.concatenate([piece.reshape(-1, 128) for piece in pieces], axis=0))
    total = total.reshape(-1)
    parts = [total[limits[i] : limits[i + 1]] for i in range(8)]
    own = y * 4 + rank
    teacher_fc = pick(parts[0].reshape(4, -1), z)
    student_fc = pick(parts[1].reshape(4, -1), z)
    block = pick(parts[2].reshape(4, 2, 2, 2, 2, -1, HD // 4), z)
    teacher_qv_grad = jnp.transpose(block, (3, 0, 4, 1, 2, 5)).reshape(2, -1)
    block = pick(parts[3].reshape(4, 8, 2, -1, HD // 8), z)
    student_qv_grad = jnp.transpose(block, (1, 2, 0, 3)).reshape(2, -1)

    def width_grads(one, two):
        one = pick(one.reshape(2, 8, -1), own, 1)
        two = pick(two.reshape(4, 8, -1), own, 1)
        return one[0], one[1], two[0], two[1], two[2], two[3]

    def arranged(outputs, input_grad, grads, sums, qv_grad, fc_grad):
        return (
            outputs, input_grad, sums[0], sums[1], grads[0], qv_grad, grads[1],
            sums[2], sums[3], sums[4], grads[2], fc_grad, grads[3], sums[5],
        )

    return arranged(
        teacher_out, teacher_dx, matrices(teacher_grads), width_grads(parts[4], parts[5]), teacher_qv_grad, teacher_fc
    ) + arranged(
        student_out, student_dx, matrices(student_grads), width_grads(parts[6], parts[7]), student_qv_grad, student_fc
    )


def on_plane(spec):
    names = {"dp": PLANE, "tensor": "z"}
    return P(*(names.get(entry, None) for entry in spec))


def solution(mesh):
    in_specs = (
        P("dp", "tensor", None),
        P("dp", "tensor", None),
        P("dp"),
        P("dp"),
        P(None, "dp", "tensor"),
        P(None, "tensor"),
        P("tensor", "dp"),
        P("dp"),
        P("dp"),
        P("dp"),
        P("dp", "tensor"),
        P("tensor"),
        P("tensor", "dp"),
        P("dp"),
        P("dp", "tensor", None),
        P("dp", "tensor", None),
        P("dp"),
        P("dp"),
        P(None, "dp", "tensor"),
        P(None, "tensor"),
        P("tensor", "dp"),
        P("dp"),
        P("dp"),
        P("dp"),
        P("dp", "tensor"),
        P("tensor"),
        P("tensor", "dp"),
        P("dp"),
        P("dp"),
        P("tensor"),
    )
    out_specs = (
        P("dp", "tensor", None),
        P("dp", "tensor", None),
        P("dp"),
        P("dp"),
        P(None, "dp", "tensor"),
        P(None, "tensor"),
        P("tensor", "dp"),
        P("dp"),
        P("dp"),
        P("dp"),
        P("dp", "tensor"),
        P("tensor"),
        P("tensor", "dp"),
        P("dp"),
        P("dp", "tensor", None),
        P("dp", "tensor", None),
        P("dp"),
        P("dp"),
        P(None, "dp", "tensor"),
        P(None, "tensor"),
        P("tensor", "dp"),
        P("dp"),
        P("dp"),
        P("dp"),
        P("dp", "tensor"),
        P("tensor"),
        P("tensor", "dp"),
        P("dp"),
    )
    if tuple(mesh.devices.shape) == (8, 4):
        finer = Mesh(mesh.devices.reshape(2, 2, 2, 4), EVERY)
        return jax.shard_map(
            on_pairs,
            mesh=finer,
            in_specs=tuple(on_plane(spec) for spec in in_specs),
            out_specs=tuple(on_plane(spec) for spec in out_specs),
            check_vma=False,
        )
    return jax.shard_map(
        on_device, mesh=mesh, in_specs=in_specs, out_specs=out_specs, check_vma=False
    )
```

```python
import functools

import jax
import jax.numpy as jnp
import numpy as np
from jax import lax
from jax.experimental import pallas as pl
from jax.experimental.pallas import tpu as pltpu
from jax.sharding import Mesh
from jax.sharding import PartitionSpec as P

HD = 64
SPAN = 256


epsilon = 1e-05
negative = -1e30


def layer_norm(values, norm_gain, norm_shift):
    center = values - jnp.mean(values, axis=-1, keepdims=True)
    spread = jnp.mean(center * center, axis=-1, keepdims=True)
    return center * lax.rsqrt(spread + epsilon) * norm_gain + norm_shift


def gelu_tanh(values):
    return jax.nn.gelu(values, approximate=True)


def visibility(first_row, block_rows, length, span_start):
    query_pos = first_row + jnp.arange(block_rows, dtype=jnp.int32)
    key_pos = jnp.arange(length, dtype=jnp.int32)
    query_in = (query_pos >= span_start) & (query_pos < span_start + SPAN)
    key_in = (key_pos >= span_start) & (key_pos < span_start + SPAN)
    return (key_pos[None, :] <= query_pos[:, None]) | query_in[:, None] & key_in[None, :]


def block_scores(query_block, key_rows, visible, score_scale):
    scores = (
        jnp.einsum("qhe,khe->hqk", query_block, key_rows, preferred_element_type=jnp.float32)
        * score_scale
    )
    return jnp.where(visible[None], scores, negative)


def attention_forward(query_rows, key_rows, value_rows, span_start, block_rows, score_scale):
    length = query_rows.shape[0]
    results = []
    log_sums = []
    for block_index in range(length // block_rows):
        first_row = block_index * block_rows
        visible = visibility(first_row, block_rows, length, span_start)
        scores = block_scores(
            query_rows[first_row : first_row + block_rows], key_rows, visible, score_scale
        )
        row_peak = jnp.max(scores, axis=-1, keepdims=True)
        raised = jnp.exp(scores - row_peak)
        row_total = jnp.sum(raised, axis=-1, keepdims=True)
        weights = (raised / row_total).astype(jnp.bfloat16)
        results.append(
            jnp.einsum("hqk,khe->qhe", weights, value_rows, preferred_element_type=jnp.float32)
        )
        log_sums.append(row_peak + jnp.log(row_total))
    return (jnp.concatenate(results, axis=0), log_sums)


def attention_backward(
    query_rows, key_rows, value_rows, log_sums, heads_grad, span_start, block_rows, score_scale
):
    length = query_rows.shape[0]
    query_grads = []
    key_grad = jnp.zeros(key_rows.shape, jnp.float32)
    value_grad = jnp.zeros(value_rows.shape, jnp.float32)
    for block_index in range(length // block_rows):
        first_row = block_index * block_rows
        last_row = first_row + block_rows
        visible = visibility(first_row, block_rows, length, span_start)
        scores = block_scores(query_rows[first_row:last_row], key_rows, visible, score_scale)
        probability = jnp.exp(scores - log_sums[block_index])
        grad_block = heads_grad[first_row:last_row]
        value_grad = value_grad + jnp.einsum(
            "hqk,qhe->khe",
            probability.astype(jnp.bfloat16),
            grad_block,
            preferred_element_type=jnp.float32,
        )
        prob_grad = jnp.einsum(
            "qhe,khe->hqk", grad_block, value_rows, preferred_element_type=jnp.float32
        )
        weighted = jnp.sum(probability * prob_grad, axis=-1, keepdims=True)
        score_grad = (probability * (prob_grad - weighted)).astype(jnp.bfloat16)
        query_grads.append(
            jnp.einsum("hqk,khe->qhe", score_grad, key_rows, preferred_element_type=jnp.float32)
            * score_scale
        )
        key_grad = (
            key_grad
            + jnp.einsum(
                "hqk,qhe->khe",
                score_grad,
                query_rows[first_row:last_row],
                preferred_element_type=jnp.float32,
            )
            * score_scale
        )
    return (jnp.concatenate(query_grads, axis=0), key_grad, value_grad)


def gather_rows(normed):
    return lax.all_gather(normed, "tensor", axis=0, tiled=True)


def gather_grads(branch_grad):
    return lax.all_gather(branch_grad, "tensor", axis=0, tiled=True)


def sum_rows(left_rows, right_weight):
    return lax.psum_scatter(
        jnp.dot(left_rows, right_weight, preferred_element_type=jnp.float32).astype(jnp.bfloat16),
        "tensor",
        scatter_dimension=0,
        tiled=True,
    ).astype(jnp.float32)


def back_rows(grad_stack, weight_stack):
    return lax.psum_scatter(
        jnp.einsum(
            "sle,sde->ld", grad_stack, weight_stack, preferred_element_type=jnp.float32
        ).astype(jnp.bfloat16),
        "tensor",
        scatter_dimension=0,
        tiled=True,
    ).astype(jnp.float32)


def run_block(
    inputs,
    upstream,
    attn_gain,
    attn_shift,
    qkv_weight,
    qv_bias,
    out_weight,
    out_bias,
    mlp_gain,
    mlp_shift,
    fc_weight,
    fc_bias,
    proj_weight,
    proj_bias,
    span_start,
    head_keep,
):
    gathered = (
        lax.all_gather(qkv_weight, "dp", axis=1, tiled=True),
        lax.all_gather(out_weight, "dp", axis=1, tiled=True),
        lax.all_gather(fc_weight, "dp", axis=0, tiled=True),
        lax.all_gather(proj_weight, "dp", axis=1, tiled=True),
        lax.all_gather(attn_gain, "dp", axis=0, tiled=True),
        lax.all_gather(attn_shift, "dp", axis=0, tiled=True),
        lax.all_gather(out_bias, "dp", axis=0, tiled=True),
        lax.all_gather(mlp_gain, "dp", axis=0, tiled=True),
        lax.all_gather(mlp_shift, "dp", axis=0, tiled=True),
        lax.all_gather(proj_bias, "dp", axis=0, tiled=True),
    )
    qkv_full, out_full, fc_full, proj_full = (gathered[0], gathered[1], gathered[2], gathered[3])
    gain_one = gathered[4].astype(jnp.float32)
    shift_one = gathered[5].astype(jnp.float32)
    bias_out = gathered[6].astype(jnp.float32)
    gain_two = gathered[7].astype(jnp.float32)
    shift_two = gathered[8].astype(jnp.float32)
    bias_proj = gathered[9].astype(jnp.float32)
    rows_first = inputs[0].astype(jnp.float32)
    normed, norm_back_one = jax.vjp(layer_norm, rows_first, gain_one, shift_one)
    normed_all = gather_rows(normed.astype(jnp.bfloat16))
    projected = jnp.einsum("ld,tde->tle", normed_all, qkv_full, preferred_element_type=jnp.float32)
    bias_pair = qv_bias.astype(jnp.float32)
    length = normed_all.shape[0]
    head_count = head_keep.shape[0]
    head_split = (length, head_count, HD)
    query_rows = (projected[0] + bias_pair[0]).astype(jnp.bfloat16).reshape(head_split)
    key_rows = projected[1].astype(jnp.bfloat16).reshape(head_split)
    value_rows = (projected[2] + bias_pair[1]).astype(jnp.bfloat16).reshape(head_split)
    block_rows = min(512, length)
    score_scale = 1.0 / HD**0.5
    attended, log_sums = attention_forward(
        query_rows, key_rows, value_rows, span_start, block_rows, score_scale
    )
    keep_float = head_keep.astype(jnp.float32)[None, :, None]
    heads_low = (attended * keep_float).astype(jnp.bfloat16).reshape(length, head_count * HD)
    attn_sum = sum_rows(heads_low, out_full)
    middle = rows_first + (attn_sum + bias_out)
    normed_two, norm_back_two = jax.vjp(layer_norm, middle, gain_two, shift_two)
    normed_two_all = gather_rows(normed_two.astype(jnp.bfloat16))
    hidden_pre = jnp.dot(
        normed_two_all, fc_full, preferred_element_type=jnp.float32
    ) + fc_bias.astype(jnp.float32)
    hidden, gelu_back = jax.vjp(gelu_tanh, hidden_pre)
    hidden_low = hidden.astype(jnp.bfloat16)
    mlp_sum = sum_rows(hidden_low, proj_full)
    result = middle + (mlp_sum + bias_proj)
    outputs = result.astype(jnp.bfloat16)[None]
    grad_result = upstream[0].astype(jnp.float32)
    grad_mlp_all = gather_grads(upstream[0])
    proj_bias_grad = jnp.sum(grad_mlp_all, axis=0, dtype=jnp.float32)
    proj_grad = jnp.einsum(
        "lf,ld->fd", hidden_low, grad_mlp_all, preferred_element_type=jnp.float32
    )
    hidden_grad = jnp.einsum(
        "ld,fd->lf", grad_mlp_all, proj_full, preferred_element_type=jnp.float32
    )
    pre_grad = gelu_back(hidden_grad)[0].astype(jnp.bfloat16)
    fc_bias_grad = jnp.sum(pre_grad, axis=0, dtype=jnp.float32)
    fc_grad = jnp.einsum("ld,lf->df", normed_two_all, pre_grad, preferred_element_type=jnp.float32)
    normed_two_grad = back_rows(pre_grad[None], fc_full[None])
    middle_from_norm, gain_two_grad, shift_two_grad = norm_back_two(normed_two_grad)
    middle_grad = grad_result + middle_from_norm
    grad_attn_all = gather_grads(middle_grad.astype(jnp.bfloat16))
    out_bias_grad = jnp.sum(grad_attn_all, axis=0, dtype=jnp.float32)
    out_grad = jnp.einsum("le,ld->ed", heads_low, grad_attn_all, preferred_element_type=jnp.float32)
    heads_grad = (
        jnp.einsum("ld,ed->le", grad_attn_all, out_full, preferred_element_type=jnp.float32)
        .astype(jnp.bfloat16)
        .reshape(head_split)
    )
    heads_grad = heads_grad * head_keep.astype(jnp.bfloat16)[None, :, None]
    query_grad, key_grad, value_grad = attention_backward(
        query_rows, key_rows, value_rows, log_sums, heads_grad, span_start, block_rows, score_scale
    )
    qkv_low = jnp.stack(
        [
            query_grad.reshape(length, head_count * HD),
            key_grad.reshape(length, head_count * HD),
            value_grad.reshape(length, head_count * HD),
        ]
    ).astype(jnp.bfloat16)
    qv_bias_grad = jnp.stack(
        [
            jnp.sum(qkv_low[0], axis=0, dtype=jnp.float32),
            jnp.sum(qkv_low[2], axis=0, dtype=jnp.float32),
        ]
    )
    qkv_grad = jnp.einsum("ld,tle->tde", normed_all, qkv_low, preferred_element_type=jnp.float32)
    normed_grad = back_rows(qkv_low, qkv_full)
    rows_from_norm, gain_one_grad, shift_one_grad = norm_back_one(normed_grad)
    input_grad = (middle_grad + rows_from_norm).astype(jnp.bfloat16)[None]
    norm_sums = lax.psum((gain_one_grad, shift_one_grad, gain_two_grad, shift_two_grad), "tensor")
    matrices = (
        qkv_grad,
        out_grad,
        fc_grad,
        proj_grad,
        norm_sums[0],
        norm_sums[1],
        out_bias_grad,
        norm_sums[2],
        norm_sums[3],
        proj_bias_grad,
    )
    biases = (qv_bias_grad, fc_bias_grad)
    return (outputs, input_grad, matrices, biases)


def arrange(outputs, input_grad, matrices, biases):
    return (
        outputs,
        input_grad,
        matrices[4],
        matrices[5],
        matrices[0],
        biases[0],
        matrices[1],
        matrices[6],
        matrices[7],
        matrices[8],
        matrices[2],
        biases[1],
        matrices[3],
        matrices[9],
    )


def on_device(
    teacher_input,
    teacher_upstream,
    teacher_attn_gain,
    teacher_attn_shift,
    teacher_qkv_weight,
    teacher_qv_bias,
    teacher_out_weight,
    teacher_out_bias,
    teacher_mlp_gain,
    teacher_mlp_shift,
    teacher_fc_weight,
    teacher_fc_bias,
    teacher_proj_weight,
    teacher_proj_bias,
    student_input,
    student_upstream,
    student_attn_gain,
    student_attn_shift,
    student_qkv_weight,
    student_qv_bias,
    student_out_weight,
    student_out_bias,
    student_mlp_gain,
    student_mlp_shift,
    student_fc_weight,
    student_fc_bias,
    student_proj_weight,
    student_proj_bias,
    span_starts,
    head_slots,
):
    span_start = span_starts[0]
    teacher = run_block(
        teacher_input,
        teacher_upstream,
        teacher_attn_gain,
        teacher_attn_shift,
        teacher_qkv_weight,
        teacher_qv_bias,
        teacher_out_weight,
        teacher_out_bias,
        teacher_mlp_gain,
        teacher_mlp_shift,
        teacher_fc_weight,
        teacher_fc_bias,
        teacher_proj_weight,
        teacher_proj_bias,
        span_start,
        head_slots,
    )
    student_keep = jnp.ones((student_qv_bias.shape[1] // HD,), jnp.int32)
    student = run_block(
        student_input,
        student_upstream,
        student_attn_gain,
        student_attn_shift,
        student_qkv_weight,
        student_qv_bias,
        student_out_weight,
        student_out_bias,
        student_mlp_gain,
        student_mlp_shift,
        student_fc_weight,
        student_fc_bias,
        student_proj_weight,
        student_proj_bias,
        span_start,
        student_keep,
    )
    teach_parts = teacher[2]
    learn_parts = student[2]
    summed = (
        lax.psum_scatter(teach_parts[0], "dp", scatter_dimension=1, tiled=True),
        lax.psum_scatter(teach_parts[1], "dp", scatter_dimension=1, tiled=True),
        lax.psum_scatter(teach_parts[2], "dp", scatter_dimension=0, tiled=True),
        lax.psum_scatter(teach_parts[3], "dp", scatter_dimension=1, tiled=True),
        lax.psum_scatter(teach_parts[4], "dp", scatter_dimension=0, tiled=True),
        lax.psum_scatter(teach_parts[5], "dp", scatter_dimension=0, tiled=True),
        lax.psum_scatter(teach_parts[6], "dp", scatter_dimension=0, tiled=True),
        lax.psum_scatter(teach_parts[7], "dp", scatter_dimension=0, tiled=True),
        lax.psum_scatter(teach_parts[8], "dp", scatter_dimension=0, tiled=True),
        lax.psum_scatter(teach_parts[9], "dp", scatter_dimension=0, tiled=True),
        lax.psum_scatter(learn_parts[0], "dp", scatter_dimension=1, tiled=True),
        lax.psum_scatter(learn_parts[1], "dp", scatter_dimension=1, tiled=True),
        lax.psum_scatter(learn_parts[2], "dp", scatter_dimension=0, tiled=True),
        lax.psum_scatter(learn_parts[3], "dp", scatter_dimension=1, tiled=True),
        lax.psum_scatter(learn_parts[4], "dp", scatter_dimension=0, tiled=True),
        lax.psum_scatter(learn_parts[5], "dp", scatter_dimension=0, tiled=True),
        lax.psum_scatter(learn_parts[6], "dp", scatter_dimension=0, tiled=True),
        lax.psum_scatter(learn_parts[7], "dp", scatter_dimension=0, tiled=True),
        lax.psum_scatter(learn_parts[8], "dp", scatter_dimension=0, tiled=True),
        lax.psum_scatter(learn_parts[9], "dp", scatter_dimension=0, tiled=True),
    )
    totals = lax.psum((teacher[3][0], teacher[3][1], student[3][0], student[3][1]), "dp")
    teacher_matrices = summed[0:10]
    student_matrices = summed[10:20]
    teacher_biases = (totals[0], totals[1])
    student_biases = (totals[2], totals[3])
    return arrange(teacher[0], teacher[1], teacher_matrices, teacher_biases) + arrange(
        student[0], student[1], student_matrices, student_biases
    )


PLANE = ("y", "x", "c")
EVERY = ("y", "x", "c", "z")
TILE = 256


def swap(values, axis):
    return lax.ppermute(values, axis, ((0, 1), (1, 0)))


def index_of(y, x, c, z):
    return ((y * 2 + x) * 2 + c) * 4 + z


def cross(values):
    pairs = tuple(
        ((y * 4 + a) * 4 + z, (y * 4 + z) * 4 + a) for y in range(2) for a in range(4) for z in range(4)
    )
    return lax.ppermute(values, EVERY, pairs)


def row_pairs():
    return tuple(
        (index_of(y, x, c, z), index_of(y, (z ^ c) & 1, z >> 1, 2 * x + c))
        for y in range(2)
        for x in range(2)
        for c in range(2)
        for z in range(4)
    )


def rows_out(values):
    return lax.ppermute(values, EVERY, row_pairs())


def rows_home(values):
    return lax.ppermute(values, EVERY, tuple((b, a) for a, b in row_pairs()))


def pick(values, index, axis=0):
    return lax.dynamic_index_in_dim(values, index, axis, keepdims=False)


def wide(values):
    return values.astype(jnp.float32)


def low(values):
    return values.astype(jnp.bfloat16)


def matmul(left, right, left_dim, right_dim):
    return lax.dot_general(
        left, right, (((left_dim,), (right_dim,)), ((), ())), preferred_element_type=jnp.float32
    )


class Order:
    def __init__(self):
        self.last = None

    def __call__(self, *values):
        if self.last is not None:
            values = lax.optimization_barrier((*values, self.last))[:-1]
        self.last = values[0]
        return values[0] if len(values) == 1 else values

    def mark(self, value):
        self.last = value


def after(values, earlier):
    return lax.optimization_barrier((values, earlier))[0]


def to_plane(blocks):
    return lax.all_to_all(blocks, PLANE, 0, 0)


def join_shards(blocks):
    return jnp.transpose(blocks, (1, 0, 2)).reshape(blocks.shape[1], -1)


def split_shards(rows):
    return jnp.transpose(rows.reshape(rows.shape[0], 8, -1), (1, 0, 2))


def ahead_sum(near, got):
    count = near.shape[0] // 2
    return low(wide(near[count:]) + wide(got[count:]))


def plane_swap(values, bit):
    return lax.ppermute(values, "z", tuple((i, i ^ bit) for i in range(4)))


def row_call(kernel, name, outs, *args):
    rows = outs[0][0][0]
    size = sum(a.size * a.dtype.itemsize for a in args)

    def spec(shape):
        return pl.BlockSpec((min(shape[0], rows), shape[1]), lambda i: (0, 0))

    return pl.pallas_call(
        kernel,
        grid=(1,),
        in_specs=[spec(a.shape) for a in args],
        out_specs=[spec(shape) for shape, _ in outs],
        out_shape=[jax.ShapeDtypeStruct(shape, dtype) for shape, dtype in outs],
        cost_estimate=pl.CostEstimate(flops=args[0].size * 20, transcendentals=0, bytes_accessed=2 * size),
        name=name,
    )(*args)


def centered(rows):
    center = rows - jnp.mean(rows, axis=-1, keepdims=True)
    spread = jnp.mean(center * center, axis=-1, keepdims=True)
    scale = lax.rsqrt(spread + epsilon)
    return center * scale, scale


def first_norm_kernel(x_ref, gain_ref, shift_ref, out_ref):
    unit, _ = centered(wide(x_ref[...]))
    out_ref[...] = low(unit * gain_ref[...] + shift_ref[...])


def mid_norm_kernel(x_ref, a_ref, b_ref, c_ref, bias_ref, gain_ref, shift_ref, mid_ref, out_ref):
    branch = wide(a_ref[...]) + wide(b_ref[...]) + wide(c_ref[...])
    middle = wide(x_ref[...]) + (branch + bias_ref[...])
    mid_ref[...] = middle
    unit, _ = centered(middle)
    out_ref[...] = low(unit * gain_ref[...] + shift_ref[...])


def norm_back(grad, rows, gain):
    unit, scale = centered(rows)
    t = grad * gain
    back = scale * (
        t - jnp.mean(t, axis=-1, keepdims=True) - unit * jnp.mean(t * unit, axis=-1, keepdims=True)
    )
    return back, jnp.sum(grad * unit, axis=0, keepdims=True), jnp.sum(grad, axis=0, keepdims=True)


def mid_back_kernel(g_ref, a_ref, b_ref, c_ref, mid_ref, gain_ref, dmid_ref, ga_ref, sums_ref):
    up = wide(g_ref[...])
    grad = wide(a_ref[...]) + wide(b_ref[...]) + wide(c_ref[...])
    back, gain_sum, shift_sum = norm_back(grad, mid_ref[...], gain_ref[...])
    dmid = up + back
    dmid_ref[...] = dmid
    ga = low(dmid)
    ga_ref[...] = ga
    sums_ref[0:1] = jnp.sum(wide(ga), axis=0, keepdims=True)
    sums_ref[1:2] = gain_sum
    sums_ref[2:3] = shift_sum
    sums_ref[3:4] = jnp.sum(up, axis=0, keepdims=True)


def first_back_kernel(a_ref, b_ref, c_ref, x_ref, dmid_ref, gain_ref, dx_ref, sums_ref):
    grad = wide(a_ref[...]) + wide(b_ref[...]) + wide(c_ref[...])
    back, gain_sum, shift_sum = norm_back(grad, wide(x_ref[...]), gain_ref[...])
    dx_ref[...] = low(dmid_ref[...] + back)
    sums_ref[0:1] = gain_sum
    sums_ref[1:2] = shift_sum


def place_of(block, own):
    return block ^ own


def tile_visible(first_key, first_query, start):
    shape = (TILE, TILE)
    key = first_key + lax.broadcasted_iota(jnp.int32, shape, 0)
    query = first_query + lax.broadcasted_iota(jnp.int32, shape, 1)
    key_in = (key >= start) & (key < start + SPAN)
    query_in = (query >= start) & (query < start + SPAN)
    return (key <= query) | (key_in & query_in)


def tile_bounds(block, blocks, start):
    more = (start // TILE == block) & (start % TILE != 0)
    return jnp.minimum(block + 1 + more.astype(jnp.int32), blocks)


def head_lanes(width, head):
    lane = lax.broadcasted_iota(jnp.int32, (1, width), 1)
    return (lane >= head * HD) & (lane < (head + 1) * HD)


def lane_chunks(columns):
    chunks = []
    for first in range(0, columns, 2 * HD):
        lanes = min(2 * HD, columns - first)
        chunks.append((first, lanes, lanes // HD))
    return chunks


def one_head(values, head, heads):
    if heads == 1:
        return values
    lane = lax.broadcasted_iota(jnp.int32, (1, values.shape[1]), 1)
    return jnp.where((lane >= HD) == (head == 1), values, jnp.zeros_like(values))


def attend_block(block, start, rank, keep_ref, qkv_s, heads_s, logs_ref):
    columns = qkv_s.shape[-1]
    chunks = lane_chunks(columns)
    here = pl.ds(pl.multiple_of(place_of(block, rank) * TILE, TILE), TILE)
    queries = []
    for first, lanes, heads in chunks:
        query = qkv_s[0, here, first : first + lanes]
        queries.append([one_head(query, h, heads) for h in range(heads)])

    def tile(index, carry, masked):
        rows = pl.ds(pl.multiple_of(place_of(index, rank) * TILE, TILE), TILE)
        if masked:
            visible = tile_visible(index * TILE, block * TILE, start)
        scores = []
        for (first, lanes, heads), query in zip(chunks, queries):
            keys = qkv_s[1, rows, first : first + lanes]
            for h in range(heads):
                score = matmul(keys, query[h], 1, 1)
                scores.append(jnp.where(visible, score, negative) if masked else score)
        out = []
        number = 0
        for first, lanes, heads in chunks:
            values = qkv_s[2, rows, first : first + lanes]
            for h in range(heads):
                peak, total, acc = carry[number]
                score = scores[number]
                new_peak = jnp.maximum(peak, jnp.max(score, axis=0, keepdims=True))
                decay = jnp.exp(peak - new_peak)
                raised = jnp.exp(score - new_peak)
                total = total * decay + jnp.sum(raised, axis=0, keepdims=True)
                part = matmul(values, low(raised), 0, 0)
                acc = acc * decay + part[h * HD : (h + 1) * HD]
                out.append((new_peak, total, acc))
                number += 1
        return tuple(out)

    carry = tuple(
        (
            jnp.full((1, TILE), negative, jnp.float32),
            jnp.zeros((1, TILE), jnp.float32),
            jnp.zeros((HD, TILE), jnp.float32),
        )
        for _ in range(columns // HD)
    )
    carry = lax.fori_loop(0, block, lambda i, s: tile(i, s, False), carry)
    carry = lax.fori_loop(block, tile_bounds(block, 4, start), lambda i, s: tile(i, s, True), carry)
    number = 0
    for first, lanes, heads in chunks:
        outs = []
        for _ in range(heads):
            peak, total, acc = carry[number]
            outs.append(acc * (keep_ref[number] / total))
            logs_ref[block, number : number + 1, :] = peak + jnp.log(total)
            number += 1
        heads_s[here, first : first + lanes] = low(jnp.concatenate(outs, axis=0).T)


def attend_back_block(block, start, rank, keep_ref, qkv_s, heads_s, grads_s, logs_ref, dq_s, dk_s, dv_s):
    columns = qkv_s.shape[-1]
    chunks = lane_chunks(columns)
    here = pl.ds(pl.multiple_of(place_of(block, rank) * TILE, TILE), TILE)
    queries, grads, weighted, logs = [], [], [], []
    number = 0
    for first, lanes, heads in chunks:
        query = qkv_s[0, here, first : first + lanes]
        grad = grads_s[here, first : first + lanes]
        turned = (wide(grad) * wide(heads_s[here, first : first + lanes])).T
        for h in range(heads):
            keep = keep_ref[number]
            queries.append(one_head(query, h, heads))
            grads.append(low(wide(one_head(grad, h, heads)) * keep))
            weighted.append(keep * jnp.sum(turned[h * HD : (h + 1) * HD], axis=0, keepdims=True))
            logs.append(logs_ref[block, number : number + 1, :])
            number += 1

    def tile(index, carry, masked):
        rows = pl.ds(pl.multiple_of(place_of(index, rank) * TILE, TILE), TILE)
        if masked:
            visible = tile_visible(index * TILE, block * TILE, start)
        out = []
        number = 0
        for first, lanes, heads in chunks:
            keys = qkv_s[1, rows, first : first + lanes]
            values = qkv_s[2, rows, first : first + lanes]
            dk = dv = None
            for h in range(heads):
                scores = matmul(keys, queries[number], 1, 1)
                if masked:
                    scores = jnp.where(visible, scores, negative)
                prob = jnp.exp(scores - logs[number])
                dprob = matmul(values, grads[number], 1, 1)
                dscores = low(prob * (dprob - weighted[number]))
                dv_part = matmul(low(prob), grads[number], 1, 0)
                dk_part = matmul(dscores, queries[number], 1, 0)
                dv = dv_part if dv is None else dv + dv_part
                dk = dk_part if dk is None else dk + dk_part
                out.append(carry[number] + matmul(keys, dscores, 0, 0)[h * HD : (h + 1) * HD])
                number += 1
            dk_s[rows, first : first + lanes] += dk
            dv_s[rows, first : first + lanes] += dv
        return tuple(out)

    carry = tuple(jnp.zeros((HD, TILE), jnp.float32) for _ in range(columns // HD))
    carry = lax.fori_loop(0, block, lambda i, s: tile(i, s, False), carry)
    carry = lax.fori_loop(block, tile_bounds(block, 4, start), lambda i, s: tile(i, s, True), carry)
    number = 0
    for first, lanes, heads in chunks:
        dq = jnp.concatenate(carry[number : number + heads], axis=0) * (1.0 / HD**0.5)
        dq_s[here, first : first + lanes] = low(dq.T)
        number += heads


ANY = pl.BlockSpec(memory_space=pl.ANY)
VMEM = pl.BlockSpec(memory_space=pltpu.VMEM)
LIMIT = 56 << 20


def fetch(parts, into, sem):
    first = 0
    for part in parts:
        rows = part.shape[0]
        pltpu.make_async_copy(part, into.at[pl.ds(first, rows)], sem).start()
        first += rows


def fetched(into, sem):
    pltpu.make_async_copy(into, into, sem).wait()


def send(source, into, sem):
    copy = pltpu.make_async_copy(source, into, sem)
    copy.start()
    return copy


def scratch(*shape):
    return pltpu.VMEM(shape, jnp.bfloat16)


def matmul_call(kernel, name, outs, args, specs, scratches, flops):
    size = sum(a.size * a.dtype.itemsize for a in args)
    return pl.pallas_call(
        kernel,
        in_specs=specs,
        out_specs=[spec for _, _, spec in outs],
        out_shape=[jax.ShapeDtypeStruct(shape, dtype) for shape, dtype, _ in outs],
        scratch_shapes=scratches,
        compiler_params=pltpu.CompilerParams(vmem_limit_bytes=LIMIT),
        cost_estimate=pl.CostEstimate(flops=flops // 16, transcendentals=0, bytes_accessed=size // 8),
        name=name,
    )(*args)


SMEM = pl.BlockSpec(memory_space=pltpu.SMEM)


def front(pieces, weights, places, bias, columns, info, keep):
    count, width = pieces[0].shape
    length = 4 * count
    half = length // 2
    scales = (1.0 / HD**0.5, 1.0, 1.0)

    def kernel(*refs):
        piece_refs, refs = refs[:4], refs[4:]
        weight_refs, refs = refs[: len(weights)], refs[len(weights) :]
        bias_ref, info_ref, keep_ref, refs = refs[0], refs[1], refs[2], refs[3:]
        qkv_ref, all_ref, full_ref, heads_ref, near_ref, far_ref, logs_ref = refs[:7]
        rows_s, full_s, qkv_s, heads_s, sum_s, sems, outs = refs[7:]
        for array, index, row, matrix, column, rows in places:
            source = weight_refs[array]
            source = source if index is None else source.at[index]
            pltpu.make_async_copy(
                source.at[pl.ds(row, rows)], full_s.at[matrix, pl.ds(column, rows)], sems.at[0]
            ).start()
        fetch(piece_refs, rows_s, sems.at[1])
        fetched(full_s, sems.at[0])
        fetched(rows_s, sems.at[1])
        sent = [send(full_s, full_ref, outs.at[0]), send(rows_s, all_ref, outs.at[1])]

        @pl.loop(0, 4)
        def _(block):
            rows = pl.ds(pl.multiple_of(block * count, count), count)
            for t in range(3):
                part = low(matmul(rows_s[rows, :], full_s[t], 1, 1) + bias_ref[t])
                qkv_s[t, rows, :] = low(wide(part) * scales[t])

        sent.append(send(qkv_s, qkv_ref, outs.at[2]))

        @pl.loop(0, 4)
        def _(block):
            attend_block(block, info_ref[0], info_ref[1], keep_ref, qkv_s, heads_s, logs_ref)

        sent.append(send(heads_s, heads_ref, outs.at[3]))

        @pl.loop(0, 4)
        def _(block):
            rows = pl.ds(pl.multiple_of(block * count, count), count)
            sum_s[rows, :] = low(matmul(heads_s[rows, :], full_s[3], 1, 0))

        sent.append(send(sum_s.at[pl.ds(0, half)], near_ref, outs.at[4]))
        sent.append(send(sum_s.at[pl.ds(half, half)], far_ref, outs.at[5]))
        for copy in sent:
            copy.wait()

    def out(*shape):
        return (shape, jnp.bfloat16, ANY)

    return matmul_call(
        kernel,
        "front",
        [
            out(3, length, columns), out(length, width), out(4, columns, width), out(length, columns),
            out(half, width), out(half, width), ((4, columns // HD, TILE), jnp.float32, VMEM),
        ],
        [*pieces, *weights, bias, info, keep],
        [ANY] * (4 + len(weights)) + [VMEM, SMEM, SMEM],
        [
            scratch(length, width), scratch(4, columns, width), scratch(3, length, columns),
            scratch(length, columns), scratch(length, width),
            pltpu.SemaphoreType.DMA((2,)), pltpu.SemaphoreType.DMA((6,)),
        ],
        8 * length * columns * width + 4 * length * length * columns,
    )


def rear(pieces, weights, qkv, heads_low, logs, info, keep):
    count, width = pieces[0].shape
    length = 4 * count
    half = length // 2
    columns = weights.shape[1]

    def kernel(*refs):
        piece_refs, refs = refs[:4], refs[4:]
        weight_ref, qkv_ref, heads_ref, logs_ref, info_ref, keep_ref, refs = *refs[:6], refs[6:]
        dq_ref, dk_ref, dv_ref, all_ref, near_ref, far_ref = refs[:6]
        rows_s, full_s, qkv_s, heads_s, grads_s, dq_s, dk_s, dv_s, low_s, sum_s, sems, outs = refs[6:]
        fetch([weight_ref.at[3]], full_s.at[3], sems.at[0])
        fetch(piece_refs, rows_s, sems.at[1])
        fetch([heads_ref], heads_s, sems.at[2])
        copies = [send(qkv_ref, qkv_s, sems.at[3])]
        copies.append(send(weight_ref.at[pl.ds(0, 3)], full_s.at[pl.ds(0, 3)], sems.at[4]))
        dk_s[...] = jnp.zeros_like(dk_s)
        dv_s[...] = jnp.zeros_like(dv_s)
        fetched(full_s.at[3], sems.at[0])
        fetched(rows_s, sems.at[1])
        sent = [send(rows_s, all_ref, outs.at[0])]

        @pl.loop(0, 4)
        def _(block):
            at = pl.ds(pl.multiple_of(block * count, count), count)
            grads_s[at, :] = low(matmul(rows_s[at, :], full_s[3], 1, 1))

        fetched(heads_s, sems.at[2])
        copies[0].wait()

        @pl.loop(0, 4)
        def _(block):
            attend_back_block(
                block, info_ref[0], info_ref[1], keep_ref, qkv_s, heads_s, grads_s, logs_ref, dq_s, dk_s, dv_s
            )

        copies[1].wait()
        low_s[0] = low(dk_s[...])
        low_s[1] = low(dv_s[...])
        sent.append(send(dq_s, dq_ref, outs.at[1]))
        sent.append(send(low_s.at[0], dk_ref, outs.at[2]))
        sent.append(send(low_s.at[1], dv_ref, outs.at[3]))

        @pl.loop(0, 4)
        def _(block):
            at = pl.ds(pl.multiple_of(block * count, count), count)
            total = matmul(dq_s[at, :], full_s[0], 1, 0)
            total = total + matmul(low_s[0, at, :], full_s[1], 1, 0)
            total = total + matmul(low_s[1, at, :], full_s[2], 1, 0)
            sum_s[at, :] = low(total)

        sent.append(send(sum_s.at[pl.ds(0, half)], near_ref, outs.at[4]))
        sent.append(send(sum_s.at[pl.ds(half, half)], far_ref, outs.at[5]))
        for copy in sent:
            copy.wait()

    def out(*shape):
        return (shape, jnp.bfloat16, ANY)

    return matmul_call(
        kernel,
        "rear",
        [out(length, columns)] * 3 + [out(length, width), out(half, width), out(half, width)],
        [*pieces, weights, qkv, heads_low, logs, info, keep],
        [ANY] * 7 + [VMEM, SMEM, SMEM],
        [
            scratch(length, width), scratch(4, columns, width), scratch(3, length, columns),
            scratch(length, columns), scratch(length, columns), scratch(length, columns),
            pltpu.VMEM((length, columns), jnp.float32), pltpu.VMEM((length, columns), jnp.float32),
            scratch(2, length, columns), scratch(length, width),
            pltpu.SemaphoreType.DMA((5,)), pltpu.SemaphoreType.DMA((6,)),
        ],
        8 * length * columns * width + 10 * length * length * columns,
    )


def gelu_pair(u):
    k = 0.7978845608028654
    t = jnp.tanh(k * (u + 0.044715 * (u * u * u)))
    value = 0.5 * u * (1.0 + t)
    slope = 0.5 * (1.0 + t) + 0.5 * u * (1.0 - t * t) * (k * (1.0 + 3 * 0.044715 * (u * u)))
    return value, slope


def mlp_main(rows, grads, weights, bias):
    count, width = rows[0].shape
    length = 4 * count
    units = weights.shape[0] // 16
    hidden = 8 * units
    half = length // 2

    def kernel(*refs):
        row_refs, grad_refs, weight_ref, refs = refs[:4], refs[4:8], refs[8], refs[9:]
        bias_ref, refs = refs[0], refs[1:]
        rows_ref, grads_ref, hidden_ref, pre_ref, near_ref, far_ref, sum_ref = refs[:7]
        rows_s, grads_s, fc_s, proj_s, hidden_s, slope_s, back_s, sems, outs = refs[7:]
        fetch([weight_ref.at[pl.ds(2 * i * units, units)] for i in range(8)], fc_s, sems.at[0])
        fetch(row_refs, rows_s, sems.at[1])
        fetch([weight_ref.at[pl.ds((2 * i + 1) * units, units)] for i in range(8)], proj_s, sems.at[2])
        fetch(grad_refs, grads_s, sems.at[3])
        fetched(fc_s, sems.at[0])
        fetched(rows_s, sems.at[1])
        sent = [send(rows_s, rows_ref, outs.at[0])]

        @pl.loop(0, 4)
        def _(block):
            at = pl.ds(pl.multiple_of(block * count, count), count)
            value, slope = gelu_pair(matmul(rows_s[at, :], fc_s[...], 1, 1) + bias_ref[...])
            hidden_s[at, :] = low(value)
            slope_s[at, :] = low(slope)

        sent.append(send(hidden_s, hidden_ref, outs.at[1]))
        fetched(proj_s, sems.at[2])
        fetched(grads_s, sems.at[3])
        sent.append(send(grads_s, grads_ref, outs.at[2]))
        sum_ref[...] = jnp.zeros_like(sum_ref)

        @pl.loop(0, 4)
        def _(block):
            at = pl.ds(pl.multiple_of(block * count, count), count)
            pre = low(matmul(grads_s[at, :], proj_s[...], 1, 1) * wide(slope_s[at, :]))
            slope_s[at, :] = pre
            sum_ref[...] += jnp.sum(wide(pre), axis=0, keepdims=True)
            back_s[at, :] = low(matmul(pre, fc_s[...], 1, 0))

        sent.append(send(slope_s, pre_ref, outs.at[3]))
        sent.append(send(back_s.at[pl.ds(0, half)], near_ref, outs.at[4]))
        sent.append(send(back_s.at[pl.ds(half, half)], far_ref, outs.at[5]))
        for copy in sent:
            copy.wait()

    def out(rows, columns):
        return ((rows, columns), jnp.bfloat16, ANY)

    return matmul_call(
        kernel,
        "mlp_main",
        [
            out(length, width), out(length, width), out(length, hidden), out(length, hidden),
            out(half, width), out(half, width), ((1, hidden), jnp.float32, VMEM),
        ],
        [*rows, *grads, weights, bias],
        [ANY] * 9 + [VMEM],
        [
            scratch(length, width), scratch(length, width), scratch(hidden, width), scratch(hidden, width),
            scratch(length, hidden), scratch(length, hidden), scratch(length, width),
            pltpu.SemaphoreType.DMA((4,)), pltpu.SemaphoreType.DMA((6,)),
        ],
        6 * length * hidden * width,
    )


def mlp_rest(rows, grads, hidden, pre, weights):
    length, width = rows.shape
    units = weights.shape[0] // 16
    total = 8 * units
    half = length // 2
    count = length // 4
    tile = 256

    def kernel(*refs):
        rows_ref, grads_ref, hidden_ref, pre_ref = refs[:4]
        weight_ref, near_ref, far_ref, grad_out = refs[4:8]
        rows_s, grads_s, hidden_s, pre_s, proj_s, ahead_s, fc_s, back_s, sems, outs = refs[8:]
        fetch([hidden_ref], hidden_s, sems.at[0])
        fetch([weight_ref.at[pl.ds((2 * i + 1) * units, units)] for i in range(8)], proj_s, sems.at[1])
        fetch([pre_ref], pre_s, sems.at[2])
        fetch([rows_ref], rows_s, sems.at[3])
        fetch([grads_ref], grads_s, sems.at[4])
        fetched(hidden_s, sems.at[0])
        fetched(proj_s, sems.at[1])

        @pl.loop(0, 4)
        def _(block):
            at = pl.ds(pl.multiple_of(block * count, count), count)
            ahead_s[at, :] = low(matmul(hidden_s[at, :], proj_s[...], 1, 0))

        sent = [
            send(ahead_s.at[pl.ds(0, half)], near_ref, outs.at[0]),
            send(ahead_s.at[pl.ds(half, half)], far_ref, outs.at[1]),
        ]
        fetched(pre_s, sems.at[2])
        fetched(rows_s, sems.at[3])

        def pieces(source, kind):
            for k in range(8):
                into = grad_out.at[pl.ds((2 * k + kind) * units, units)]
                sent.append(send(source.at[pl.ds(k * units, units)], into, outs.at[2 + kind * 8 + k]))

        @pl.loop(0, total // tile)
        def _(block):
            at = pl.ds(pl.multiple_of(block * tile, tile), tile)
            fc_s[at, :] = low(matmul(pre_s[:, at], rows_s[...], 0, 0))

        pieces(fc_s, 0)
        fetched(grads_s, sems.at[4])

        @pl.loop(0, total // tile)
        def _(block):
            at = pl.ds(pl.multiple_of(block * tile, tile), tile)
            back_s[at, :] = low(matmul(hidden_s[:, at], grads_s[...], 0, 0))

        pieces(back_s, 1)
        for copy in sent:
            copy.wait()

    def out(*rows):
        return ((*rows, width), jnp.bfloat16, ANY)

    return matmul_call(
        kernel,
        "mlp_rest",
        [out(half), out(half), out(16 * units)],
        [rows, grads, hidden, pre, weights],
        [ANY] * 5,
        [
            scratch(length, width), scratch(length, width), scratch(length, total), scratch(length, total),
            scratch(total, width), scratch(length, width), scratch(total, width), scratch(total, width),
            pltpu.SemaphoreType.DMA((5,)), pltpu.SemaphoreType.DMA((18,)),
        ],
        6 * length * total * width,
    )


def head_weight_grads(lefts, rows, grad_rows, places, outs):
    length, columns = lefts[0].shape
    width = rows.shape[1]

    def kernel(*refs):
        left_refs, (rows_ref, grads_ref), refs = refs[:4], refs[4:6], refs[6:]
        out_refs, (full_s, sem) = refs[: len(outs)], refs[len(outs) :]
        for matrix in range(4):
            right = (rows_ref if matrix < 3 else grads_ref)[...]
            full_s[matrix] = low(matmul(left_refs[matrix][...], right, 0, 0))
        for array, index, row, matrix, column, count in places:
            into = out_refs[array]
            into = into if index is None else into.at[index]
            pltpu.make_async_copy(
                full_s.at[matrix, pl.ds(column, count)], into.at[pl.ds(row, count)], sem.at[0]
            ).start()
        pltpu.make_async_copy(full_s, full_s, sem.at[0]).wait()

    return matmul_call(
        kernel,
        "head_weight_grads",
        [(shape, jnp.bfloat16, ANY) for shape in outs],
        [*lefts, rows, grad_rows],
        [VMEM] * 6,
        [scratch(4, columns, width), pltpu.SemaphoreType.DMA((1,))],
        8 * length * columns * width,
    )


def hidden_blocks(fc, proj):
    shard = proj.shape[1]
    return jnp.concatenate([jnp.transpose(fc).reshape(8, -1, shard), proj.reshape(8, -1, shard)], axis=1)


def hidden_unblock(blocks):
    shard = blocks.shape[-1]
    blocks = blocks.reshape(8, 2, -1, shard)
    return blocks[:, 0].reshape(-1, shard), blocks[:, 1].reshape(-1, shard)


def teacher_blocks(qkv, out):
    columns, shard = out.shape
    stack = jnp.concatenate([jnp.transpose(qkv, (0, 2, 1)), out[None]], axis=0)
    stack = stack.reshape(4, 2, columns // (2 * HD), 2, 2, HD // 4, shard)
    return jnp.transpose(stack, (3, 1, 4, 0, 2, 5, 6)).reshape(8, -1, shard)


def teacher_unblock(heads):
    shard = heads.shape[-1]
    stack = heads.reshape(2, 2, 2, 4, -1, HD // 4, shard)
    return jnp.transpose(stack, (3, 1, 4, 0, 2, 5, 6)).reshape(4, -1, shard)


def student_blocks(qkv, out):
    columns, shard = out.shape
    stack = jnp.concatenate([jnp.transpose(qkv, (0, 2, 1)), out[None]], axis=0)
    stack = stack.reshape(4, columns // HD, 8, HD // 8, shard)
    return jnp.transpose(stack, (2, 0, 1, 3, 4)).reshape(8, -1, shard)


def student_unblock(heads):
    shard = heads.shape[-1]
    return jnp.transpose(heads.reshape(8, 4, -1, HD // 8, shard), (1, 2, 0, 3, 4)).reshape(4, -1, shard)


def teacher_places(columns):
    sub = HD // 4
    heads = columns // (2 * HD)
    places = []
    for matrix in range(4):
        for plane in range(2):
            for head in range(heads):
                for dc in range(2):
                    for dy in range(2):
                        column = (plane * heads + head) * HD + (dc * 2 + dy) * sub
                        places.append((dc * 2 + dy, plane, (matrix * heads + head) * sub, matrix, column, sub))
    return places


def student_places(columns):
    sub = HD // 8
    heads = columns // HD
    places = []
    for matrix in range(4):
        for head in range(heads):
            for part in range(8):
                places.append((part, None, (matrix * heads + head) * sub, matrix, head * HD + part * sub, sub))
    return places


def student_grad_places(columns):
    return [(p // 4, p % 4, row, matrix, column, sub) for p, _, row, matrix, column, sub in student_places(columns)]


def on_pairs(*args):
    teacher_in, student_in = args[0:14], args[14:28]
    span_starts, head_slots = args[28], args[29]
    pos = {name: lax.axis_index(name) for name in EVERY}
    y, x, c, z = pos["y"], pos["x"], pos["c"], pos["z"]
    rank = x * 2 + c
    teacher_columns, student_columns = teacher_in[6].shape[0], student_in[6].shape[0]
    teacher_count, student_count = teacher_columns // 2, student_columns // 2
    shard, student_shard = teacher_in[2].shape[0], student_in[2].shape[0]
    length = 4 * teacher_in[0].shape[1]

    order = (2, 3, 7, 8, 9, 13)
    marks = jnp.stack([span_starts[0] // 32, span_starts[0] % 32, 0, 0]).astype(jnp.bfloat16)
    tall = jnp.concatenate(
        [
            jnp.stack([teacher_in[i] for i in order]),
            jnp.pad(jnp.stack([student_in[i] for i in order]), ((0, 0), (0, shard - student_shard))),
            jnp.broadcast_to(marks[:, None], (4, shard)),
        ],
        axis=0,
    )
    blocks = teacher_blocks(teacher_in[4], teacher_in[6])
    blocks = jnp.concatenate([blocks, jnp.broadcast_to(tall[None], (8,) + tall.shape)], axis=1)
    teacher_got = to_plane(blocks)
    teacher_rows, student_rows = rows_out(teacher_in[0][0]), rows_out(student_in[0][0])

    parts = [
        teacher_in[11], teacher_in[5].reshape(-1), student_in[11], student_in[5].reshape(-1),
        jnp.pad(head_slots.astype(jnp.bfloat16), (0, 128 - head_slots.shape[0])),
    ]
    limits = np.cumsum([0] + [part.shape[0] // 128 for part in parts])
    deep = jnp.concatenate([part.reshape(-1, 128) for part in parts], axis=0)
    deep = [deep] + [plane_swap(deep, step) for step in (1, 2, 3)]

    student_got = to_plane(after(student_blocks(student_in[4], student_in[6]), teacher_got))
    teacher_hidden_got = to_plane(after(hidden_blocks(teacher_in[10], teacher_in[12]), student_got))
    student_hidden_got = to_plane(after(hidden_blocks(student_in[10], student_in[12]), teacher_hidden_got))

    vectors = teacher_got[:, teacher_count:]

    def width_vectors(block):
        block = wide(jnp.transpose(block, (1, 0, 2)).reshape(6, 1, -1))
        return tuple(block[i] for i in range(6))

    teacher_vectors = width_vectors(vectors[:, :6])
    student_vectors = width_vectors(vectors[:, 6:12, :student_shard])
    starts = vectors[:, 12:14, 0].astype(jnp.int32)
    starts = starts[:, 0] * 32 + starts[:, 1]
    info = jnp.stack([pick(starts, y * 4 + z), 2 * c + (x ^ (z & 1))])

    step = Order()
    first = c == 0

    t0 = step(join_shards(teacher_got[:, :teacher_count]))
    t1, t2, t0y = plane_swap(t0, 1), plane_swap(t0, 2), swap(t0, "y")
    full16, student16 = (teacher_rows.shape, jnp.bfloat16), (student_rows.shape, jnp.bfloat16)
    (normed,) = row_call(
        first_norm_kernel, "first_norm", [full16], step(teacher_rows), teacher_vectors[0], teacher_vectors[1]
    )
    teacher_normed = [normed, swap(normed, "x"), swap(normed, "c")]
    step.mark(normed)
    student_cross = cross(step(join_shards(student_got)))
    t2 = step(t2)
    t3, t2y = plane_swap(t2, 1), swap(t2, "y")
    t1 = step(t1)
    t1y = swap(t1, "y")
    tf0 = step(join_shards(teacher_hidden_got))
    teacher_normed[1] = step(teacher_normed[1])
    teacher_normed.append(swap(teacher_normed[1], "c"))
    t3 = step(t3)
    t3y = swap(t3, "y")

    def halves(one, two, three, four):
        front, rear_part = jnp.stack([one, two]), jnp.stack([three, four])
        return jnp.where(first, front, rear_part), swap(jnp.where(first, rear_part, front), "c")

    own, near = halves(t0, t1, t2, t3)
    s0 = step(student_cross)
    s1, s2, s0y = plane_swap(s0, 1), plane_swap(s0, 2), swap(s0, "y")
    (normed,) = row_call(
        first_norm_kernel, "first_norm", [student16], step(student_rows), student_vectors[0], student_vectors[1]
    )
    student_normed = [normed, swap(normed, "x"), swap(normed, "c")]
    step.mark(normed)
    s2 = step(s2)
    s3, s2y = plane_swap(s2, 1), swap(s2, "y")
    s1 = step(s1)
    s1y = swap(s1, "y")
    t0y, t1y, t2y, t3y = step(t0y, t1y, t2y, t3y)
    own_over, near_over = halves(t0y, t1y, t2y, t3y)
    teacher_weights = lax.all_gather(after(tf0, t3y), ("y", "z"), axis=0, tiled=True)
    teacher_up, student_up = rows_out(after(teacher_in[1][0], t3y)), rows_out(after(student_in[1][0], t3y))

    deep = jnp.stack(deep)
    deep = [deep[:, limits[i] : limits[i + 1]].reshape(4, -1) for i in range(5)]
    near_y = jnp.stack([y, 1 - y])
    hidden_spots = (jnp.arange(4)[None] * 8 + jnp.arange(2)[:, None] * 4 + rank).reshape(-1)
    near_c = jnp.stack([c, 1 - c])
    planes = z ^ jnp.arange(4)
    hidden_hot = wide(jnp.arange(4)[:, None] == planes[None]).astype(jnp.bfloat16)

    def hidden_bias(block):
        block = pick(block.reshape(4, 2, 4, -1), rank, 2)
        return jnp.einsum("zk,kyi->yzi", hidden_hot, block, preferred_element_type=jnp.float32).reshape(1, -1)

    teacher_fc_bias, student_fc_bias = hidden_bias(deep[0]), hidden_bias(deep[2])
    two = jnp.where(first, 0, 2)
    block = lax.dynamic_slice_in_dim(deep[1].reshape(4, -1), two, 2, 0)
    block = block.reshape(2, 2, 2, -1, 2, 2, HD // 4)
    block = pick(block, x, 2)
    block = jnp.where(y == 0, block, block[:, :, :, ::-1])
    block = jnp.where(first, block, block[:, :, :, :, ::-1])
    teacher_qv = wide(jnp.transpose(block, (1, 0, 2, 4, 3, 5)).reshape(2, -1))
    slots = lax.dynamic_slice_in_dim(deep[4][:, : head_slots.shape[0]], two, 2, 0)
    keep = wide(pick(slots.reshape(2, 2, -1), x, 1).reshape(-1))
    block = pick(deep[3].reshape(4, 2, -1, 8, HD // 8), z ^ rank)
    eighth = (near_y[:, None] * 4 + planes[None]).reshape(-1)
    order_hot = (jnp.arange(8)[None] == eighth[:, None]).astype(jnp.bfloat16)
    student_qv = jnp.einsum("rp,thpi->thri", order_hot, block, preferred_element_type=jnp.float32).reshape(2, -1)
    ones = jnp.ones((student_qv.shape[1] // HD,), jnp.float32)

    def bias_rows(pair):
        return jnp.stack([pair[0], jnp.zeros_like(pair[0]), pair[1]])[:, None, :]

    teacher_spots, student_spots = teacher_places(teacher_columns), student_places(student_columns)
    head_weights = (own, own_over, near, near_over)
    qkv, normed_all, weights, heads_low, t_near, t_far, logs = front(
        step(*teacher_normed), head_weights, teacher_spots, bias_rows(teacher_qv), teacher_columns, info, keep
    )
    teacher_saved = (qkv, normed_all, weights, heads_low, logs)
    step.mark(t_near)
    t_got = swap(t_far, "c")
    t_over = swap(step(ahead_sum(t_near, t_got)), "x")
    sf0 = step(join_shards(student_hidden_got))
    student_weights = lax.all_gather(sf0, ("y", "z"), axis=0, tiled=True)
    student_normed[1] = step(student_normed[1])
    student_normed.append(swap(student_normed[1], "c"))
    bias_out, gain_two, shift_two = teacher_vectors[2:5]
    full32 = (teacher_rows.shape, jnp.float32)
    t_middle, normed = row_call(
        mid_norm_kernel, "mid_norm", [full32, full16],
        teacher_rows, t_near, t_got, step(t_over), bias_out, gain_two, shift_two,
    )
    step.mark(normed)
    teacher_normed = [normed, swap(normed, "x"), swap(normed, "c")]
    teacher_up = step(teacher_up)
    teacher_ups = [teacher_up, swap(teacher_up, "x"), swap(teacher_up, "c")]
    s3 = step(s3)
    s3y = swap(s3, "y")
    teacher_normed[1] = step(teacher_normed[1])
    teacher_normed.append(swap(teacher_normed[1], "c"))

    head_weights = (s0, s1, s2, s3, s0y, s1y, s2y, s3y)
    qkv, normed_all, weights, heads_low, s_near, s_far, logs = front(
        step(*student_normed), head_weights, student_spots, bias_rows(student_qv), student_columns, info, ones
    )
    student_saved = (qkv, normed_all, weights, heads_low, logs)
    step.mark(s_near)
    s_got = swap(s_far, "c")
    teacher_ups[1] = step(teacher_ups[1])
    teacher_ups.append(swap(teacher_ups[1], "c"))
    s_over = swap(step(ahead_sum(s_near, s_got)), "x")

    *teacher_mlp, t_near, t_far, teacher_fc = mlp_main(
        step(*teacher_normed), teacher_ups, teacher_weights, teacher_fc_bias
    )
    step.mark(t_near)
    t_got = swap(t_far, "c")
    ahead = step(ahead_sum(t_near, t_got))
    t_part, t_over = swap(ahead[:64], "x"), swap(ahead[64:], "x")
    bias_out, gain_two, shift_two = student_vectors[2:5]
    student32 = (student_rows.shape, jnp.float32)
    s_middle, normed = row_call(
        mid_norm_kernel, "mid_norm", [student32, student16],
        student_rows, s_near, s_got, step(s_over), bias_out, gain_two, shift_two,
    )
    step.mark(normed)
    student_normed = [normed, swap(normed, "x"), swap(normed, "c")]
    student_up = step(student_up)
    student_ups = [student_up, swap(student_up, "x"), swap(student_up, "c")]
    teacher_mlp[0] = after(step(teacher_mlp[0]), t_part)
    t_out_near, t_out_far, grads = mlp_rest(*teacher_mlp, teacher_weights)
    step.mark(t_out_near)
    teacher_hidden = lax.psum_scatter(grads, ("y", "z"), scatter_dimension=0, tiled=True)
    width = teacher_rows.shape[1]
    t_dmid, t_ga, teacher_two = row_call(
        mid_back_kernel, "mid_back", [full32, full16, ((4, width), jnp.float32)],
        teacher_up, t_near, t_got, jnp.concatenate([t_part, step(t_over)], axis=0), t_middle, teacher_vectors[3],
    )
    step.mark(t_ga)
    teacher_normed = [t_ga, swap(t_ga, "x"), swap(t_ga, "c")]

    student_normed[1] = step(student_normed[1])
    student_normed.append(swap(student_normed[1], "c"))
    student_ups[1] = step(student_ups[1])
    student_ups.append(swap(student_ups[1], "c"))

    *student_mlp, s_near, s_far, student_fc = mlp_main(
        step(*student_normed), student_ups, student_weights, student_fc_bias
    )
    step.mark(s_near)
    s_got = swap(s_far, "c")
    teacher_normed[1] = step(teacher_normed[1])
    teacher_normed.append(swap(teacher_normed[1], "c"))
    s_over = swap(step(ahead_sum(s_near, s_got)), "x")

    qkv, normed_all, weights, heads_low, logs = teacher_saved
    t_dq, t_dk, t_dv, t_grad_all, t_near, t_far = rear(
        step(*teacher_normed), weights, qkv, heads_low, logs, info, keep
    )
    step.mark(t_near)
    t_got = swap(t_far, "c")
    teacher_saved = ([t_dq, t_dk, t_dv, heads_low], normed_all, t_grad_all)
    width = student_rows.shape[1]
    s_dmid, s_ga, student_two = row_call(
        mid_back_kernel, "mid_back", [student32, student16, ((4, width), jnp.float32)],
        student_up, s_near, s_got, step(s_over), s_middle, student_vectors[3],
    )
    step.mark(s_ga)
    student_normed = [s_ga, swap(s_ga, "x"), swap(s_ga, "c")]
    t_over = swap(step(ahead_sum(t_near, t_got)), "x")
    lefts, right, grad_right = teacher_saved
    lefts[0] = step(lefts[0])
    teacher_width, student_width = teacher_rows.shape[1], student_rows.shape[1]
    th = head_weight_grads(lefts, right, grad_right, teacher_spots, [(2, teacher_count, teacher_width)] * 4)
    teacher_qv_grad = jnp.stack([jnp.sum(wide(t_dq), axis=0), jnp.sum(wide(t_dv), axis=0)])
    step.mark(th[0])
    th_over_got, th_got = swap(th[3], "c"), swap(th[2], "c")

    def planes_of(mine, got):
        odd = jnp.stack([jnp.where(first, mine[1], got[1]), jnp.where(first, got[1], mine[1])])
        even = jnp.stack([jnp.where(first, mine[0], got[0]), jnp.where(first, got[0], mine[0])])
        return odd, even

    odd_over, even_over = planes_of(th[1], step(th_over_got))
    odd_got, even_got = swap(odd_over, "y"), swap(even_over, "y")
    th_odd, th_even = planes_of(th[0], th_got)
    step.mark(odd_over)
    student_mlp[0] = step(student_mlp[0])
    s_out_near, s_out_far, grads = mlp_rest(*student_mlp, student_weights)
    step.mark(s_out_near)
    student_hidden = lax.psum_scatter(grads, ("y", "z"), scatter_dimension=0, tiled=True)
    teacher_dx, teacher_one = row_call(
        first_back_kernel, "first_back", [full16, ((2, teacher_width), jnp.float32)],
        t_near, t_got, step(t_over), teacher_rows, t_dmid, teacher_vectors[0],
    )
    step.mark(teacher_dx)
    t_out_got = swap(after(t_out_far, teacher_dx), "c")
    teacher_dx = rows_home(teacher_dx)
    teacher_hidden = to_plane(split_shards(step(teacher_hidden)))
    student_normed[1] = step(student_normed[1])
    student_normed.append(swap(student_normed[1], "c"))
    qkv, normed_all, weights, heads_low, logs = student_saved
    s_dq, s_dk, s_dv, s_grad_all, s_near, s_far = rear(
        step(*student_normed), weights, qkv, heads_low, logs, info, ones
    )
    step.mark(s_near)
    s_got = swap(s_far, "c")
    odd_got = step(odd_got)
    th_odd_got = plane_swap(step(low(wide(th_odd) + wide(odd_got))), 1)
    s_over = swap(step(ahead_sum(s_near, s_got)), "x")
    teacher_hidden = step(teacher_hidden)
    sh_near, sh_far = head_weight_grads(
        [step(s_dq), s_dk, s_dv, heads_low], normed_all, s_grad_all, student_grad_places(student_columns),
        [(4, student_count, student_width)] * 2,
    )
    student_qv_grad = jnp.stack([jnp.sum(wide(s_dq), axis=0), jnp.sum(wide(s_dv), axis=0)])
    step.mark(sh_near)
    sh_got = swap(sh_far, "y")
    t_out_over = swap(step(ahead_sum(t_out_near, t_out_got)), "x")
    student_dx, student_one = row_call(
        first_back_kernel, "first_back", [student16, ((2, student_width), jnp.float32)],
        s_near, s_got, step(s_over), student_rows, s_dmid, student_vectors[0],
    )
    step.mark(student_dx)
    s_out_got = swap(after(s_out_far, student_dx), "c")
    student_dx = rows_home(student_dx)

    def spread(places, values):
        hot = (jnp.arange(32)[:, None] == places[None]).astype(jnp.float32)
        return jnp.dot(hot, values, precision=lax.Precision.HIGHEST)

    head_planes = planes.reshape(2, 2)
    head_planes = jnp.where(first, head_planes[0], head_planes[1])
    column_spots = (
        head_planes[:, None, None] * 8 + x * 4 + near_y[None, None, :] * 2 + near_c[None, :, None]
    ).reshape(-1)
    eighth_spots = rank * 8 + eighth

    teacher_qv_grad = teacher_qv_grad.reshape(2, 2, -1, 2, 2, HD // 4)
    teacher_qv_grad = jnp.transpose(teacher_qv_grad, (1, 3, 4, 0, 2, 5)).reshape(8, -1)
    student_qv_grad = jnp.transpose(student_qv_grad.reshape(2, -1, 8, HD // 8), (2, 0, 1, 3)).reshape(8, -1)
    hidden_grads = jnp.concatenate([teacher_fc.reshape(8, -1), student_fc.reshape(8, -1)], axis=1)
    hidden_grads = spread(hidden_spots, hidden_grads)
    lanes = hidden_grads.shape[1]
    column_grads = jnp.concatenate(
        [spread(column_spots, teacher_qv_grad), spread(eighth_spots, student_qv_grad)], axis=1
    )
    column_grads = jnp.pad(column_grads, ((0, 0), (0, lanes - column_grads.shape[1])))

    def stacked(one, two):
        tall = jnp.concatenate([one, two, jnp.zeros_like(one)], axis=0)
        return [tall[:, i : i + lanes] for i in range(0, tall.shape[1], lanes)]

    total = jnp.concatenate(
        [hidden_grads, column_grads] + stacked(teacher_one, teacher_two) + stacked(student_one, student_two), axis=0
    )
    total = step(total)
    other = swap(total, "c")
    th_odd_got, even_got = step(th_odd_got, even_got)
    th_even = wide(th_even) + wide(even_got)
    th_even_got = plane_swap(low(th_even[1] + wide(th_odd_got[1])), 2)
    sh_total = step(wide(sh_near) + wide(sh_got))
    sh_odd_got = plane_swap(low(sh_total[1::2]), 1)
    total = total + step(other)
    other = swap(total, "x")
    s_out_over = swap(step(ahead_sum(s_out_near, s_out_got)), "x")
    count = t_middle.shape[0]
    teacher_out = low(
        t_middle + (wide(t_out_near[:count]) + wide(t_out_got[:count]) + wide(step(t_out_over)) + teacher_vectors[5])
    )
    teacher_out = rows_home(teacher_out)
    sh_even = step(sh_total[0::2] + wide(sh_odd_got))
    sh_even_got = plane_swap(low(sh_even[1]), 2)
    teacher_head = low(th_even[0] + wide(th_odd_got[0]) + wide(step(th_even_got)))
    teacher_head = to_plane(split_shards(teacher_head))
    total = total + step(other)
    other = swap(total, "y")
    student_head = cross(low(sh_even[0] + wide(step(sh_even_got))))
    count = s_middle.shape[0]
    student_out = low(
        s_middle + (wide(s_out_near[:count]) + wide(s_out_got[:count]) + wide(step(s_out_over)) + student_vectors[5])
    )
    student_out = rows_home(student_out)
    total = total + step(other)
    other = plane_swap(total, 1)
    student_got = jnp.concatenate([step(student_head), student_hidden], axis=0)
    teacher_grads = (teacher_unblock(step(teacher_head)), *hidden_unblock(teacher_hidden))
    student_got = to_plane(split_shards(student_got))
    total = total + step(other)
    other = plane_swap(total, 2)
    student_got = step(student_got)
    teacher_dx, student_dx, teacher_out, student_out = step(teacher_dx, student_dx, teacher_out, student_out)
    student_grads = (student_unblock(student_got[:, :student_count]), *hidden_unblock(student_got[:, student_count:]))
    total = total + other
    teacher_out, teacher_dx = teacher_out[None], teacher_dx[None]
    student_out, student_dx = student_out[None], student_dx[None]

    def matrices(grads):
        stack, fc_grad, proj_grad = grads
        return (
            wide(jnp.transpose(stack[:3], (0, 2, 1))), wide(stack[3]),
            wide(jnp.transpose(fc_grad)), wide(proj_grad),
        )

    own = y * 4 + rank
    units, student_units = teacher_fc.size // 8, student_fc.size // 8
    columns, student_columns = teacher_columns // 4, student_columns // 4
    hidden_grads = pick(total[:32].reshape(4, 8, lanes), z)
    teacher_fc = hidden_grads[:, :units].reshape(-1)
    student_fc = hidden_grads[:, units : units + student_units].reshape(-1)
    column_grads = pick(total[32:64].reshape(4, 8, lanes), z)
    block = column_grads[:, :columns].reshape(2, 2, 2, 2, -1, HD // 4)
    teacher_qv_grad = jnp.transpose(block, (3, 0, 4, 1, 2, 5)).reshape(2, -1)
    block = column_grads[:, columns : columns + student_columns].reshape(8, 2, -1, HD // 8)
    student_qv_grad = jnp.transpose(block, (1, 2, 0, 3)).reshape(2, -1)
    tall = total[64:].reshape(-1, 8, lanes)
    runs = teacher_width // lanes

    def width_grads(tall, count):
        tall = jnp.concatenate([tall[i] for i in range(count)], axis=1)[:6]
        return tuple(pick(tall.reshape(6, 8, -1), own, 1))

    def arranged(outputs, input_grad, grads, sums, qv_grad, fc_grad):
        return (
            outputs, input_grad, sums[0], sums[1], grads[0], qv_grad, grads[1],
            sums[2], sums[3], sums[4], grads[2], fc_grad, grads[3], sums[5],
        )

    return arranged(
        teacher_out, teacher_dx, matrices(teacher_grads), width_grads(tall[:runs], runs), teacher_qv_grad, teacher_fc
    ) + arranged(
        student_out, student_dx, matrices(student_grads), width_grads(tall[runs:], student_width // lanes), student_qv_grad, student_fc
    )


def on_plane(spec):
    names = {"dp": PLANE, "tensor": "z"}
    return P(*(names.get(entry, None) for entry in spec))


def solution(mesh):
    in_specs = (
        P("dp", "tensor", None),
        P("dp", "tensor", None),
        P("dp"),
        P("dp"),
        P(None, "dp", "tensor"),
        P(None, "tensor"),
        P("tensor", "dp"),
        P("dp"),
        P("dp"),
        P("dp"),
        P("dp", "tensor"),
        P("tensor"),
        P("tensor", "dp"),
        P("dp"),
        P("dp", "tensor", None),
        P("dp", "tensor", None),
        P("dp"),
        P("dp"),
        P(None, "dp", "tensor"),
        P(None, "tensor"),
        P("tensor", "dp"),
        P("dp"),
        P("dp"),
        P("dp"),
        P("dp", "tensor"),
        P("tensor"),
        P("tensor", "dp"),
        P("dp"),
        P("dp"),
        P("tensor"),
    )
    out_specs = (
        P("dp", "tensor", None),
        P("dp", "tensor", None),
        P("dp"),
        P("dp"),
        P(None, "dp", "tensor"),
        P(None, "tensor"),
        P("tensor", "dp"),
        P("dp"),
        P("dp"),
        P("dp"),
        P("dp", "tensor"),
        P("tensor"),
        P("tensor", "dp"),
        P("dp"),
        P("dp", "tensor", None),
        P("dp", "tensor", None),
        P("dp"),
        P("dp"),
        P(None, "dp", "tensor"),
        P(None, "tensor"),
        P("tensor", "dp"),
        P("dp"),
        P("dp"),
        P("dp"),
        P("dp", "tensor"),
        P("tensor"),
        P("tensor", "dp"),
        P("dp"),
    )
    if tuple(mesh.devices.shape) == (8, 4):
        finer = Mesh(mesh.devices.reshape(2, 2, 2, 4), EVERY)
        return jax.shard_map(
            on_pairs,
            mesh=finer,
            in_specs=tuple(on_plane(spec) for spec in in_specs),
            out_specs=tuple(on_plane(spec) for spec in out_specs),
            check_vma=False,
        )
    return jax.shard_map(
        on_device, mesh=mesh, in_specs=in_specs, out_specs=out_specs, check_vma=False
    )
```

```python
import functools

import jax
import jax.numpy as jnp
import numpy as np
from jax import lax
from jax.experimental import pallas as pl
from jax.experimental.pallas import tpu as pltpu
from jax.sharding import Mesh
from jax.sharding import PartitionSpec as P

HD = 64
SPAN = 256


epsilon = 1e-05
negative = -1e30


def layer_norm(values, norm_gain, norm_shift):
    center = values - jnp.mean(values, axis=-1, keepdims=True)
    spread = jnp.mean(center * center, axis=-1, keepdims=True)
    return center * lax.rsqrt(spread + epsilon) * norm_gain + norm_shift


def gelu_tanh(values):
    return jax.nn.gelu(values, approximate=True)


def visibility(first_row, block_rows, length, span_start):
    query_pos = first_row + jnp.arange(block_rows, dtype=jnp.int32)
    key_pos = jnp.arange(length, dtype=jnp.int32)
    query_in = (query_pos >= span_start) & (query_pos < span_start + SPAN)
    key_in = (key_pos >= span_start) & (key_pos < span_start + SPAN)
    return (key_pos[None, :] <= query_pos[:, None]) | query_in[:, None] & key_in[None, :]


def block_scores(query_block, key_rows, visible, score_scale):
    scores = (
        jnp.einsum("qhe,khe->hqk", query_block, key_rows, preferred_element_type=jnp.float32)
        * score_scale
    )
    return jnp.where(visible[None], scores, negative)


def attention_forward(query_rows, key_rows, value_rows, span_start, block_rows, score_scale):
    length = query_rows.shape[0]
    results = []
    log_sums = []
    for block_index in range(length // block_rows):
        first_row = block_index * block_rows
        visible = visibility(first_row, block_rows, length, span_start)
        scores = block_scores(
            query_rows[first_row : first_row + block_rows], key_rows, visible, score_scale
        )
        row_peak = jnp.max(scores, axis=-1, keepdims=True)
        raised = jnp.exp(scores - row_peak)
        row_total = jnp.sum(raised, axis=-1, keepdims=True)
        weights = (raised / row_total).astype(jnp.bfloat16)
        results.append(
            jnp.einsum("hqk,khe->qhe", weights, value_rows, preferred_element_type=jnp.float32)
        )
        log_sums.append(row_peak + jnp.log(row_total))
    return (jnp.concatenate(results, axis=0), log_sums)


def attention_backward(
    query_rows, key_rows, value_rows, log_sums, heads_grad, span_start, block_rows, score_scale
):
    length = query_rows.shape[0]
    query_grads = []
    key_grad = jnp.zeros(key_rows.shape, jnp.float32)
    value_grad = jnp.zeros(value_rows.shape, jnp.float32)
    for block_index in range(length // block_rows):
        first_row = block_index * block_rows
        last_row = first_row + block_rows
        visible = visibility(first_row, block_rows, length, span_start)
        scores = block_scores(query_rows[first_row:last_row], key_rows, visible, score_scale)
        probability = jnp.exp(scores - log_sums[block_index])
        grad_block = heads_grad[first_row:last_row]
        value_grad = value_grad + jnp.einsum(
            "hqk,qhe->khe",
            probability.astype(jnp.bfloat16),
            grad_block,
            preferred_element_type=jnp.float32,
        )
        prob_grad = jnp.einsum(
            "qhe,khe->hqk", grad_block, value_rows, preferred_element_type=jnp.float32
        )
        weighted = jnp.sum(probability * prob_grad, axis=-1, keepdims=True)
        score_grad = (probability * (prob_grad - weighted)).astype(jnp.bfloat16)
        query_grads.append(
            jnp.einsum("hqk,khe->qhe", score_grad, key_rows, preferred_element_type=jnp.float32)
            * score_scale
        )
        key_grad = (
            key_grad
            + jnp.einsum(
                "hqk,qhe->khe",
                score_grad,
                query_rows[first_row:last_row],
                preferred_element_type=jnp.float32,
            )
            * score_scale
        )
    return (jnp.concatenate(query_grads, axis=0), key_grad, value_grad)


def gather_rows(normed):
    return lax.all_gather(normed, "tensor", axis=0, tiled=True)


def gather_grads(branch_grad):
    return lax.all_gather(branch_grad, "tensor", axis=0, tiled=True)


def sum_rows(left_rows, right_weight):
    return lax.psum_scatter(
        jnp.dot(left_rows, right_weight, preferred_element_type=jnp.float32).astype(jnp.bfloat16),
        "tensor",
        scatter_dimension=0,
        tiled=True,
    ).astype(jnp.float32)


def back_rows(grad_stack, weight_stack):
    return lax.psum_scatter(
        jnp.einsum(
            "sle,sde->ld", grad_stack, weight_stack, preferred_element_type=jnp.float32
        ).astype(jnp.bfloat16),
        "tensor",
        scatter_dimension=0,
        tiled=True,
    ).astype(jnp.float32)


def run_block(
    inputs,
    upstream,
    attn_gain,
    attn_shift,
    qkv_weight,
    qv_bias,
    out_weight,
    out_bias,
    mlp_gain,
    mlp_shift,
    fc_weight,
    fc_bias,
    proj_weight,
    proj_bias,
    span_start,
    head_keep,
):
    gathered = (
        lax.all_gather(qkv_weight, "dp", axis=1, tiled=True),
        lax.all_gather(out_weight, "dp", axis=1, tiled=True),
        lax.all_gather(fc_weight, "dp", axis=0, tiled=True),
        lax.all_gather(proj_weight, "dp", axis=1, tiled=True),
        lax.all_gather(attn_gain, "dp", axis=0, tiled=True),
        lax.all_gather(attn_shift, "dp", axis=0, tiled=True),
        lax.all_gather(out_bias, "dp", axis=0, tiled=True),
        lax.all_gather(mlp_gain, "dp", axis=0, tiled=True),
        lax.all_gather(mlp_shift, "dp", axis=0, tiled=True),
        lax.all_gather(proj_bias, "dp", axis=0, tiled=True),
    )
    qkv_full, out_full, fc_full, proj_full = (gathered[0], gathered[1], gathered[2], gathered[3])
    gain_one = gathered[4].astype(jnp.float32)
    shift_one = gathered[5].astype(jnp.float32)
    bias_out = gathered[6].astype(jnp.float32)
    gain_two = gathered[7].astype(jnp.float32)
    shift_two = gathered[8].astype(jnp.float32)
    bias_proj = gathered[9].astype(jnp.float32)
    rows_first = inputs[0].astype(jnp.float32)
    normed, norm_back_one = jax.vjp(layer_norm, rows_first, gain_one, shift_one)
    normed_all = gather_rows(normed.astype(jnp.bfloat16))
    projected = jnp.einsum("ld,tde->tle", normed_all, qkv_full, preferred_element_type=jnp.float32)
    bias_pair = qv_bias.astype(jnp.float32)
    length = normed_all.shape[0]
    head_count = head_keep.shape[0]
    head_split = (length, head_count, HD)
    query_rows = (projected[0] + bias_pair[0]).astype(jnp.bfloat16).reshape(head_split)
    key_rows = projected[1].astype(jnp.bfloat16).reshape(head_split)
    value_rows = (projected[2] + bias_pair[1]).astype(jnp.bfloat16).reshape(head_split)
    block_rows = min(512, length)
    score_scale = 1.0 / HD**0.5
    attended, log_sums = attention_forward(
        query_rows, key_rows, value_rows, span_start, block_rows, score_scale
    )
    keep_float = head_keep.astype(jnp.float32)[None, :, None]
    heads_low = (attended * keep_float).astype(jnp.bfloat16).reshape(length, head_count * HD)
    attn_sum = sum_rows(heads_low, out_full)
    middle = rows_first + (attn_sum + bias_out)
    normed_two, norm_back_two = jax.vjp(layer_norm, middle, gain_two, shift_two)
    normed_two_all = gather_rows(normed_two.astype(jnp.bfloat16))
    hidden_pre = jnp.dot(
        normed_two_all, fc_full, preferred_element_type=jnp.float32
    ) + fc_bias.astype(jnp.float32)
    hidden, gelu_back = jax.vjp(gelu_tanh, hidden_pre)
    hidden_low = hidden.astype(jnp.bfloat16)
    mlp_sum = sum_rows(hidden_low, proj_full)
    result = middle + (mlp_sum + bias_proj)
    outputs = result.astype(jnp.bfloat16)[None]
    grad_result = upstream[0].astype(jnp.float32)
    grad_mlp_all = gather_grads(upstream[0])
    proj_bias_grad = jnp.sum(grad_mlp_all, axis=0, dtype=jnp.float32)
    proj_grad = jnp.einsum(
        "lf,ld->fd", hidden_low, grad_mlp_all, preferred_element_type=jnp.float32
    )
    hidden_grad = jnp.einsum(
        "ld,fd->lf", grad_mlp_all, proj_full, preferred_element_type=jnp.float32
    )
    pre_grad = gelu_back(hidden_grad)[0].astype(jnp.bfloat16)
    fc_bias_grad = jnp.sum(pre_grad, axis=0, dtype=jnp.float32)
    fc_grad = jnp.einsum("ld,lf->df", normed_two_all, pre_grad, preferred_element_type=jnp.float32)
    normed_two_grad = back_rows(pre_grad[None], fc_full[None])
    middle_from_norm, gain_two_grad, shift_two_grad = norm_back_two(normed_two_grad)
    middle_grad = grad_result + middle_from_norm
    grad_attn_all = gather_grads(middle_grad.astype(jnp.bfloat16))
    out_bias_grad = jnp.sum(grad_attn_all, axis=0, dtype=jnp.float32)
    out_grad = jnp.einsum("le,ld->ed", heads_low, grad_attn_all, preferred_element_type=jnp.float32)
    heads_grad = (
        jnp.einsum("ld,ed->le", grad_attn_all, out_full, preferred_element_type=jnp.float32)
        .astype(jnp.bfloat16)
        .reshape(head_split)
    )
    heads_grad = heads_grad * head_keep.astype(jnp.bfloat16)[None, :, None]
    query_grad, key_grad, value_grad = attention_backward(
        query_rows, key_rows, value_rows, log_sums, heads_grad, span_start, block_rows, score_scale
    )
    qkv_low = jnp.stack(
        [
            query_grad.reshape(length, head_count * HD),
            key_grad.reshape(length, head_count * HD),
            value_grad.reshape(length, head_count * HD),
        ]
    ).astype(jnp.bfloat16)
    qv_bias_grad = jnp.stack(
        [
            jnp.sum(qkv_low[0], axis=0, dtype=jnp.float32),
            jnp.sum(qkv_low[2], axis=0, dtype=jnp.float32),
        ]
    )
    qkv_grad = jnp.einsum("ld,tle->tde", normed_all, qkv_low, preferred_element_type=jnp.float32)
    normed_grad = back_rows(qkv_low, qkv_full)
    rows_from_norm, gain_one_grad, shift_one_grad = norm_back_one(normed_grad)
    input_grad = (middle_grad + rows_from_norm).astype(jnp.bfloat16)[None]
    norm_sums = lax.psum((gain_one_grad, shift_one_grad, gain_two_grad, shift_two_grad), "tensor")
    matrices = (
        qkv_grad,
        out_grad,
        fc_grad,
        proj_grad,
        norm_sums[0],
        norm_sums[1],
        out_bias_grad,
        norm_sums[2],
        norm_sums[3],
        proj_bias_grad,
    )
    biases = (qv_bias_grad, fc_bias_grad)
    return (outputs, input_grad, matrices, biases)


def arrange(outputs, input_grad, matrices, biases):
    return (
        outputs,
        input_grad,
        matrices[4],
        matrices[5],
        matrices[0],
        biases[0],
        matrices[1],
        matrices[6],
        matrices[7],
        matrices[8],
        matrices[2],
        biases[1],
        matrices[3],
        matrices[9],
    )


def on_device(
    teacher_input,
    teacher_upstream,
    teacher_attn_gain,
    teacher_attn_shift,
    teacher_qkv_weight,
    teacher_qv_bias,
    teacher_out_weight,
    teacher_out_bias,
    teacher_mlp_gain,
    teacher_mlp_shift,
    teacher_fc_weight,
    teacher_fc_bias,
    teacher_proj_weight,
    teacher_proj_bias,
    student_input,
    student_upstream,
    student_attn_gain,
    student_attn_shift,
    student_qkv_weight,
    student_qv_bias,
    student_out_weight,
    student_out_bias,
    student_mlp_gain,
    student_mlp_shift,
    student_fc_weight,
    student_fc_bias,
    student_proj_weight,
    student_proj_bias,
    span_starts,
    head_slots,
):
    span_start = span_starts[0]
    teacher = run_block(
        teacher_input,
        teacher_upstream,
        teacher_attn_gain,
        teacher_attn_shift,
        teacher_qkv_weight,
        teacher_qv_bias,
        teacher_out_weight,
        teacher_out_bias,
        teacher_mlp_gain,
        teacher_mlp_shift,
        teacher_fc_weight,
        teacher_fc_bias,
        teacher_proj_weight,
        teacher_proj_bias,
        span_start,
        head_slots,
    )
    student_keep = jnp.ones((student_qv_bias.shape[1] // HD,), jnp.int32)
    student = run_block(
        student_input,
        student_upstream,
        student_attn_gain,
        student_attn_shift,
        student_qkv_weight,
        student_qv_bias,
        student_out_weight,
        student_out_bias,
        student_mlp_gain,
        student_mlp_shift,
        student_fc_weight,
        student_fc_bias,
        student_proj_weight,
        student_proj_bias,
        span_start,
        student_keep,
    )
    teach_parts = teacher[2]
    learn_parts = student[2]
    summed = (
        lax.psum_scatter(teach_parts[0], "dp", scatter_dimension=1, tiled=True),
        lax.psum_scatter(teach_parts[1], "dp", scatter_dimension=1, tiled=True),
        lax.psum_scatter(teach_parts[2], "dp", scatter_dimension=0, tiled=True),
        lax.psum_scatter(teach_parts[3], "dp", scatter_dimension=1, tiled=True),
        lax.psum_scatter(teach_parts[4], "dp", scatter_dimension=0, tiled=True),
        lax.psum_scatter(teach_parts[5], "dp", scatter_dimension=0, tiled=True),
        lax.psum_scatter(teach_parts[6], "dp", scatter_dimension=0, tiled=True),
        lax.psum_scatter(teach_parts[7], "dp", scatter_dimension=0, tiled=True),
        lax.psum_scatter(teach_parts[8], "dp", scatter_dimension=0, tiled=True),
        lax.psum_scatter(teach_parts[9], "dp", scatter_dimension=0, tiled=True),
        lax.psum_scatter(learn_parts[0], "dp", scatter_dimension=1, tiled=True),
        lax.psum_scatter(learn_parts[1], "dp", scatter_dimension=1, tiled=True),
        lax.psum_scatter(learn_parts[2], "dp", scatter_dimension=0, tiled=True),
        lax.psum_scatter(learn_parts[3], "dp", scatter_dimension=1, tiled=True),
        lax.psum_scatter(learn_parts[4], "dp", scatter_dimension=0, tiled=True),
        lax.psum_scatter(learn_parts[5], "dp", scatter_dimension=0, tiled=True),
        lax.psum_scatter(learn_parts[6], "dp", scatter_dimension=0, tiled=True),
        lax.psum_scatter(learn_parts[7], "dp", scatter_dimension=0, tiled=True),
        lax.psum_scatter(learn_parts[8], "dp", scatter_dimension=0, tiled=True),
        lax.psum_scatter(learn_parts[9], "dp", scatter_dimension=0, tiled=True),
    )
    totals = lax.psum((teacher[3][0], teacher[3][1], student[3][0], student[3][1]), "dp")
    teacher_matrices = summed[0:10]
    student_matrices = summed[10:20]
    teacher_biases = (totals[0], totals[1])
    student_biases = (totals[2], totals[3])
    return arrange(teacher[0], teacher[1], teacher_matrices, teacher_biases) + arrange(
        student[0], student[1], student_matrices, student_biases
    )


PLANE = ("y", "x", "c")
EVERY = ("y", "x", "c", "z")
TILE = 256


def swap(values, axis):
    return lax.ppermute(values, axis, ((0, 1), (1, 0)))


def index_of(y, x, c, z):
    return ((y * 2 + x) * 2 + c) * 4 + z


def cross(values):
    pairs = tuple(
        ((y * 4 + a) * 4 + z, (y * 4 + z) * 4 + a) for y in range(2) for a in range(4) for z in range(4)
    )
    return lax.ppermute(values, EVERY, pairs)


def row_pairs():
    return tuple(
        (index_of(y, x, c, z), index_of(y, (z ^ c) & 1, z >> 1, 2 * x + c))
        for y in range(2)
        for x in range(2)
        for c in range(2)
        for z in range(4)
    )


def rows_out(values):
    return lax.ppermute(values, EVERY, row_pairs())


def rows_home(values):
    return lax.ppermute(values, EVERY, tuple((b, a) for a, b in row_pairs()))


def pick(values, index, axis=0):
    return lax.dynamic_index_in_dim(values, index, axis, keepdims=False)


def wide(values):
    return values.astype(jnp.float32)


def low(values):
    return values.astype(jnp.bfloat16)


def matmul(left, right, left_dim, right_dim):
    return lax.dot_general(
        left, right, (((left_dim,), (right_dim,)), ((), ())), preferred_element_type=jnp.float32
    )


class Order:
    def __init__(self):
        self.last = None

    def __call__(self, *values):
        if self.last is not None:
            values = lax.optimization_barrier((*values, self.last))[:-1]
        self.last = values[0]
        return values[0] if len(values) == 1 else values

    def mark(self, value):
        self.last = value


def after(values, earlier):
    return lax.optimization_barrier((values, earlier))[0]


def to_plane(blocks):
    return lax.all_to_all(blocks, PLANE, 0, 0)


def join_shards(blocks):
    return jnp.transpose(blocks, (1, 0, 2)).reshape(blocks.shape[1], -1)


def split_shards(rows):
    return jnp.transpose(rows.reshape(rows.shape[0], 8, -1), (1, 0, 2))


def ahead_sum(near, got):
    count = near.shape[0] // 2
    return low(wide(near[count:]) + wide(got[count:]))


def plane_swap(values, bit):
    return lax.ppermute(values, "z", tuple((i, i ^ bit) for i in range(4)))


def row_call(kernel, name, outs, *args):
    rows = outs[0][0][0]
    size = sum(a.size * a.dtype.itemsize for a in args)

    def spec(shape):
        return pl.BlockSpec((min(shape[0], rows), shape[1]), lambda i: (0, 0))

    return pl.pallas_call(
        kernel,
        grid=(1,),
        in_specs=[spec(a.shape) for a in args],
        out_specs=[spec(shape) for shape, _ in outs],
        out_shape=[jax.ShapeDtypeStruct(shape, dtype) for shape, dtype in outs],
        cost_estimate=pl.CostEstimate(flops=args[0].size * 20, transcendentals=0, bytes_accessed=2 * size),
        name=name,
    )(*args)


def centered(rows):
    center = rows - jnp.mean(rows, axis=-1, keepdims=True)
    spread = jnp.mean(center * center, axis=-1, keepdims=True)
    scale = lax.rsqrt(spread + epsilon)
    return center * scale, scale


def first_norm_kernel(x_ref, gain_ref, shift_ref, out_ref):
    unit, _ = centered(wide(x_ref[...]))
    out_ref[...] = low(unit * gain_ref[...] + shift_ref[...])


def mid_norm_kernel(x_ref, a_ref, b_ref, c_ref, bias_ref, gain_ref, shift_ref, mid_ref, out_ref):
    branch = wide(a_ref[...]) + wide(b_ref[...]) + wide(c_ref[...])
    middle = wide(x_ref[...]) + (branch + bias_ref[...])
    mid_ref[...] = middle
    unit, _ = centered(middle)
    out_ref[...] = low(unit * gain_ref[...] + shift_ref[...])


def norm_back(grad, rows, gain):
    unit, scale = centered(rows)
    t = grad * gain
    back = scale * (
        t - jnp.mean(t, axis=-1, keepdims=True) - unit * jnp.mean(t * unit, axis=-1, keepdims=True)
    )
    return back, jnp.sum(grad * unit, axis=0, keepdims=True), jnp.sum(grad, axis=0, keepdims=True)


def mid_back_kernel(g_ref, a_ref, b_ref, c_ref, mid_ref, gain_ref, dmid_ref, ga_ref, sums_ref):
    up = wide(g_ref[...])
    grad = wide(a_ref[...]) + wide(b_ref[...]) + wide(c_ref[...])
    back, gain_sum, shift_sum = norm_back(grad, mid_ref[...], gain_ref[...])
    dmid = up + back
    dmid_ref[...] = dmid
    ga = low(dmid)
    ga_ref[...] = ga
    sums_ref[0:1] = jnp.sum(wide(ga), axis=0, keepdims=True)
    sums_ref[1:2] = gain_sum
    sums_ref[2:3] = shift_sum
    sums_ref[3:4] = jnp.sum(up, axis=0, keepdims=True)


def first_back_kernel(a_ref, b_ref, c_ref, x_ref, dmid_ref, gain_ref, dx_ref, sums_ref):
    grad = wide(a_ref[...]) + wide(b_ref[...]) + wide(c_ref[...])
    back, gain_sum, shift_sum = norm_back(grad, wide(x_ref[...]), gain_ref[...])
    dx_ref[...] = low(dmid_ref[...] + back)
    sums_ref[0:1] = gain_sum
    sums_ref[1:2] = shift_sum


def place_of(block, own):
    return block ^ own


def tile_visible(first_key, first_query, start):
    shape = (TILE, TILE)
    key = first_key + lax.broadcasted_iota(jnp.int32, shape, 0)
    query = first_query + lax.broadcasted_iota(jnp.int32, shape, 1)
    key_in = (key >= start) & (key < start + SPAN)
    query_in = (query >= start) & (query < start + SPAN)
    return (key <= query) | (key_in & query_in)


def tile_bounds(block, blocks, start):
    more = (start // TILE == block) & (start % TILE != 0)
    return jnp.minimum(block + 1 + more.astype(jnp.int32), blocks)


def head_lanes(width, head):
    lane = lax.broadcasted_iota(jnp.int32, (1, width), 1)
    return (lane >= head * HD) & (lane < (head + 1) * HD)


def lane_chunks(columns):
    chunks = []
    for first in range(0, columns, 2 * HD):
        lanes = min(2 * HD, columns - first)
        chunks.append((first, lanes, lanes // HD))
    return chunks


def one_head(values, head, heads):
    if heads == 1:
        return values
    lane = lax.broadcasted_iota(jnp.int32, (1, values.shape[1]), 1)
    return jnp.where((lane >= HD) == (head == 1), values, jnp.zeros_like(values))


def attend_block(block, start, rank, keep_ref, qkv_s, heads_s, logs_ref):
    columns = qkv_s.shape[-1]
    chunks = lane_chunks(columns)
    here = pl.ds(pl.multiple_of(place_of(block, rank) * TILE, TILE), TILE)
    queries = []
    for first, lanes, heads in chunks:
        query = qkv_s[0, here, first : first + lanes]
        queries.append([one_head(query, h, heads) for h in range(heads)])

    def tile(index, carry, masked):
        rows = pl.ds(pl.multiple_of(place_of(index, rank) * TILE, TILE), TILE)
        if masked:
            visible = tile_visible(index * TILE, block * TILE, start)
        scores = []
        for (first, lanes, heads), query in zip(chunks, queries):
            keys = qkv_s[1, rows, first : first + lanes]
            for h in range(heads):
                score = matmul(keys, query[h], 1, 1)
                scores.append(jnp.where(visible, score, negative) if masked else score)
        out = []
        number = 0
        for first, lanes, heads in chunks:
            values = qkv_s[2, rows, first : first + lanes]
            for h in range(heads):
                peak, total, acc = carry[number]
                score = scores[number]
                new_peak = jnp.maximum(peak, jnp.max(score, axis=0, keepdims=True))
                decay = jnp.exp(peak - new_peak)
                raised = jnp.exp(score - new_peak)
                total = total * decay + jnp.sum(raised, axis=0, keepdims=True)
                part = matmul(values, low(raised), 0, 0)
                acc = acc * decay + part[h * HD : (h + 1) * HD]
                out.append((new_peak, total, acc))
                number += 1
        return tuple(out)

    carry = tuple(
        (
            jnp.full((1, TILE), negative, jnp.float32),
            jnp.zeros((1, TILE), jnp.float32),
            jnp.zeros((HD, TILE), jnp.float32),
        )
        for _ in range(columns // HD)
    )
    carry = lax.fori_loop(0, block, lambda i, s: tile(i, s, False), carry)
    carry = lax.fori_loop(block, tile_bounds(block, 4, start), lambda i, s: tile(i, s, True), carry)
    number = 0
    for first, lanes, heads in chunks:
        outs = []
        for _ in range(heads):
            peak, total, acc = carry[number]
            outs.append(acc * (keep_ref[number] / total))
            logs_ref[block, number : number + 1, :] = peak + jnp.log(total)
            number += 1
        heads_s[here, first : first + lanes] = low(jnp.concatenate(outs, axis=0).T)


def attend_back_block(block, start, rank, keep_ref, qkv_s, heads_s, grads_s, logs_ref, dq_s, dk_s, dv_s):
    columns = qkv_s.shape[-1]
    chunks = lane_chunks(columns)
    here = pl.ds(pl.multiple_of(place_of(block, rank) * TILE, TILE), TILE)
    queries, grads, weighted, logs = [], [], [], []
    number = 0
    for first, lanes, heads in chunks:
        query = qkv_s[0, here, first : first + lanes]
        grad = grads_s[here, first : first + lanes]
        turned = (wide(grad) * wide(heads_s[here, first : first + lanes])).T
        for h in range(heads):
            keep = keep_ref[number]
            queries.append(one_head(query, h, heads))
            grads.append(low(wide(one_head(grad, h, heads)) * keep))
            weighted.append(keep * jnp.sum(turned[h * HD : (h + 1) * HD], axis=0, keepdims=True))
            logs.append(logs_ref[block, number : number + 1, :])
            number += 1

    def tile(index, carry, masked):
        rows = pl.ds(pl.multiple_of(place_of(index, rank) * TILE, TILE), TILE)
        if masked:
            visible = tile_visible(index * TILE, block * TILE, start)
        out = []
        number = 0
        for first, lanes, heads in chunks:
            keys = qkv_s[1, rows, first : first + lanes]
            values = qkv_s[2, rows, first : first + lanes]
            dk = dv = None
            for h in range(heads):
                scores = matmul(keys, queries[number], 1, 1)
                if masked:
                    scores = jnp.where(visible, scores, negative)
                prob = jnp.exp(scores - logs[number])
                dprob = matmul(values, grads[number], 1, 1)
                dscores = low(prob * (dprob - weighted[number]))
                dv_part = matmul(low(prob), grads[number], 1, 0)
                dk_part = matmul(dscores, queries[number], 1, 0)
                dv = dv_part if dv is None else dv + dv_part
                dk = dk_part if dk is None else dk + dk_part
                out.append(carry[number] + matmul(keys, dscores, 0, 0)[h * HD : (h + 1) * HD])
                number += 1
            dk_s[rows, first : first + lanes] += dk
            dv_s[rows, first : first + lanes] += dv
        return tuple(out)

    carry = tuple(jnp.zeros((HD, TILE), jnp.float32) for _ in range(columns // HD))
    carry = lax.fori_loop(0, block, lambda i, s: tile(i, s, False), carry)
    carry = lax.fori_loop(block, tile_bounds(block, 4, start), lambda i, s: tile(i, s, True), carry)
    number = 0
    for first, lanes, heads in chunks:
        dq = jnp.concatenate(carry[number : number + heads], axis=0) * (1.0 / HD**0.5)
        dq_s[here, first : first + lanes] = low(dq.T)
        number += heads


ANY = pl.BlockSpec(memory_space=pl.ANY)
VMEM = pl.BlockSpec(memory_space=pltpu.VMEM)
LIMIT = 56 << 20


def fetch(parts, into, sem):
    first = 0
    for part in parts:
        rows = part.shape[0]
        pltpu.make_async_copy(part, into.at[pl.ds(first, rows)], sem).start()
        first += rows


def fetched(into, sem):
    pltpu.make_async_copy(into, into, sem).wait()


def send(source, into, sem):
    copy = pltpu.make_async_copy(source, into, sem)
    copy.start()
    return copy


def scratch(*shape):
    return pltpu.VMEM(shape, jnp.bfloat16)


def matmul_call(kernel, name, outs, args, specs, scratches, flops):
    size = sum(a.size * a.dtype.itemsize for a in args)
    return pl.pallas_call(
        kernel,
        in_specs=specs,
        out_specs=[spec for _, _, spec in outs],
        out_shape=[jax.ShapeDtypeStruct(shape, dtype) for shape, dtype, _ in outs],
        scratch_shapes=scratches,
        compiler_params=pltpu.CompilerParams(vmem_limit_bytes=LIMIT),
        cost_estimate=pl.CostEstimate(flops=flops // 16, transcendentals=0, bytes_accessed=size // 8),
        name=name,
    )(*args)


SMEM = pl.BlockSpec(memory_space=pltpu.SMEM)


def front(pieces, weights, places, bias, columns, info, keep):
    count, width = pieces[0].shape
    length = 4 * count
    half = length // 2
    scales = (1.0 / HD**0.5, 1.0, 1.0)

    def kernel(*refs):
        piece_refs, refs = refs[:4], refs[4:]
        weight_refs, refs = refs[: len(weights)], refs[len(weights) :]
        bias_ref, info_ref, keep_ref, refs = refs[0], refs[1], refs[2], refs[3:]
        qkv_ref, all_ref, full_ref, heads_ref, near_ref, far_ref, logs_ref = refs[:7]
        rows_s, full_s, qkv_s, heads_s, sum_s, sems, outs = refs[7:]
        for array, index, row, matrix, column, rows in places:
            source = weight_refs[array]
            source = source if index is None else source.at[index]
            pltpu.make_async_copy(
                source.at[pl.ds(row, rows)], full_s.at[matrix, pl.ds(column, rows)], sems.at[0]
            ).start()
        fetch(piece_refs, rows_s, sems.at[1])
        fetched(full_s, sems.at[0])
        fetched(rows_s, sems.at[1])
        sent = [send(full_s, full_ref, outs.at[0]), send(rows_s, all_ref, outs.at[1])]

        @pl.loop(0, 4)
        def _(block):
            rows = pl.ds(pl.multiple_of(block * count, count), count)
            for t in range(3):
                part = low(matmul(rows_s[rows, :], full_s[t], 1, 1) + bias_ref[t])
                qkv_s[t, rows, :] = low(wide(part) * scales[t])

        sent.append(send(qkv_s, qkv_ref, outs.at[2]))

        @pl.loop(0, 4)
        def _(block):
            attend_block(block, info_ref[0], info_ref[1], keep_ref, qkv_s, heads_s, logs_ref)

        sent.append(send(heads_s, heads_ref, outs.at[3]))

        @pl.loop(0, 4)
        def _(block):
            rows = pl.ds(pl.multiple_of(block * count, count), count)
            sum_s[rows, :] = low(matmul(heads_s[rows, :], full_s[3], 1, 0))

        sent.append(send(sum_s.at[pl.ds(0, half)], near_ref, outs.at[4]))
        sent.append(send(sum_s.at[pl.ds(half, half)], far_ref, outs.at[5]))
        for copy in sent:
            copy.wait()

    def out(*shape):
        return (shape, jnp.bfloat16, ANY)

    return matmul_call(
        kernel,
        "front",
        [
            out(3, length, columns), out(length, width), out(4, columns, width), out(length, columns),
            out(half, width), out(half, width), ((4, columns // HD, TILE), jnp.float32, VMEM),
        ],
        [*pieces, *weights, bias, info, keep],
        [ANY] * (4 + len(weights)) + [VMEM, SMEM, SMEM],
        [
            scratch(length, width), scratch(4, columns, width), scratch(3, length, columns),
            scratch(length, columns), scratch(length, width),
            pltpu.SemaphoreType.DMA((2,)), pltpu.SemaphoreType.DMA((6,)),
        ],
        8 * length * columns * width + 4 * length * length * columns,
    )


def rear(pieces, weights, qkv, heads_low, logs, info, keep):
    count, width = pieces[0].shape
    length = 4 * count
    half = length // 2
    columns = weights.shape[1]

    def kernel(*refs):
        piece_refs, refs = refs[:4], refs[4:]
        weight_ref, qkv_ref, heads_ref, logs_ref, info_ref, keep_ref, refs = *refs[:6], refs[6:]
        dq_ref, dk_ref, dv_ref, all_ref, near_ref, far_ref = refs[:6]
        rows_s, full_s, qkv_s, heads_s, grads_s, dq_s, dk_s, dv_s, low_s, sum_s, sems, outs = refs[6:]
        fetch([weight_ref.at[3]], full_s.at[3], sems.at[0])
        fetch(piece_refs, rows_s, sems.at[1])
        fetch([heads_ref], heads_s, sems.at[2])
        copies = [send(qkv_ref, qkv_s, sems.at[3])]
        copies.append(send(weight_ref.at[pl.ds(0, 3)], full_s.at[pl.ds(0, 3)], sems.at[4]))
        dk_s[...] = jnp.zeros_like(dk_s)
        dv_s[...] = jnp.zeros_like(dv_s)
        fetched(full_s.at[3], sems.at[0])
        fetched(rows_s, sems.at[1])
        sent = [send(rows_s, all_ref, outs.at[0])]

        @pl.loop(0, 4)
        def _(block):
            at = pl.ds(pl.multiple_of(block * count, count), count)
            grads_s[at, :] = low(matmul(rows_s[at, :], full_s[3], 1, 1))

        fetched(heads_s, sems.at[2])
        copies[0].wait()

        @pl.loop(0, 4)
        def _(block):
            attend_back_block(
                block, info_ref[0], info_ref[1], keep_ref, qkv_s, heads_s, grads_s, logs_ref, dq_s, dk_s, dv_s
            )

        copies[1].wait()
        low_s[0] = low(dk_s[...])
        low_s[1] = low(dv_s[...])
        sent.append(send(dq_s, dq_ref, outs.at[1]))
        sent.append(send(low_s.at[0], dk_ref, outs.at[2]))
        sent.append(send(low_s.at[1], dv_ref, outs.at[3]))

        @pl.loop(0, 4)
        def _(block):
            at = pl.ds(pl.multiple_of(block * count, count), count)
            total = matmul(dq_s[at, :], full_s[0], 1, 0)
            total = total + matmul(low_s[0, at, :], full_s[1], 1, 0)
            total = total + matmul(low_s[1, at, :], full_s[2], 1, 0)
            sum_s[at, :] = low(total)

        sent.append(send(sum_s.at[pl.ds(0, half)], near_ref, outs.at[4]))
        sent.append(send(sum_s.at[pl.ds(half, half)], far_ref, outs.at[5]))
        for copy in sent:
            copy.wait()

    def out(*shape):
        return (shape, jnp.bfloat16, ANY)

    return matmul_call(
        kernel,
        "rear",
        [out(length, columns)] * 3 + [out(length, width), out(half, width), out(half, width)],
        [*pieces, weights, qkv, heads_low, logs, info, keep],
        [ANY] * 7 + [VMEM, SMEM, SMEM],
        [
            scratch(length, width), scratch(4, columns, width), scratch(3, length, columns),
            scratch(length, columns), scratch(length, columns), scratch(length, columns),
            pltpu.VMEM((length, columns), jnp.float32), pltpu.VMEM((length, columns), jnp.float32),
            scratch(2, length, columns), scratch(length, width),
            pltpu.SemaphoreType.DMA((5,)), pltpu.SemaphoreType.DMA((6,)),
        ],
        8 * length * columns * width + 10 * length * length * columns,
    )


def gelu_pair(u):
    k = 0.7978845608028654
    t = jnp.tanh(k * (u + 0.044715 * (u * u * u)))
    value = 0.5 * u * (1.0 + t)
    slope = 0.5 * (1.0 + t) + 0.5 * u * (1.0 - t * t) * (k * (1.0 + 3 * 0.044715 * (u * u)))
    return value, slope


def mlp_main(rows, grads, weights, bias):
    count, width = rows[0].shape
    length = 4 * count
    units = weights.shape[0] // 16
    hidden = 8 * units
    half = length // 2

    def kernel(*refs):
        row_refs, grad_refs, weight_ref, refs = refs[:4], refs[4:8], refs[8], refs[9:]
        bias_ref, refs = refs[0], refs[1:]
        rows_ref, grads_ref, hidden_ref, pre_ref, near_ref, far_ref, sum_ref = refs[:7]
        rows_s, grads_s, fc_s, proj_s, hidden_s, slope_s, back_s, sems, outs = refs[7:]
        fetch([weight_ref.at[pl.ds(2 * i * units, units)] for i in range(8)], fc_s, sems.at[0])
        fetch(row_refs, rows_s, sems.at[1])
        fetch([weight_ref.at[pl.ds((2 * i + 1) * units, units)] for i in range(8)], proj_s, sems.at[2])
        fetch(grad_refs, grads_s, sems.at[3])
        fetched(fc_s, sems.at[0])
        fetched(rows_s, sems.at[1])
        sent = [send(rows_s, rows_ref, outs.at[0])]

        @pl.loop(0, 4)
        def _(block):
            at = pl.ds(pl.multiple_of(block * count, count), count)
            value, slope = gelu_pair(matmul(rows_s[at, :], fc_s[...], 1, 1) + bias_ref[...])
            hidden_s[at, :] = low(value)
            slope_s[at, :] = low(slope)

        sent.append(send(hidden_s, hidden_ref, outs.at[1]))
        fetched(proj_s, sems.at[2])
        fetched(grads_s, sems.at[3])
        sent.append(send(grads_s, grads_ref, outs.at[2]))
        sum_ref[...] = jnp.zeros_like(sum_ref)

        @pl.loop(0, 4)
        def _(block):
            at = pl.ds(pl.multiple_of(block * count, count), count)
            pre = low(matmul(grads_s[at, :], proj_s[...], 1, 1) * wide(slope_s[at, :]))
            slope_s[at, :] = pre
            sum_ref[...] += jnp.sum(wide(pre), axis=0, keepdims=True)
            back_s[at, :] = low(matmul(pre, fc_s[...], 1, 0))

        sent.append(send(slope_s, pre_ref, outs.at[3]))
        sent.append(send(back_s.at[pl.ds(0, half)], near_ref, outs.at[4]))
        sent.append(send(back_s.at[pl.ds(half, half)], far_ref, outs.at[5]))
        for copy in sent:
            copy.wait()

    def out(rows, columns):
        return ((rows, columns), jnp.bfloat16, ANY)

    return matmul_call(
        kernel,
        "mlp_main",
        [
            out(length, width), out(length, width), out(length, hidden), out(length, hidden),
            out(half, width), out(half, width), ((1, hidden), jnp.float32, VMEM),
        ],
        [*rows, *grads, weights, bias],
        [ANY] * 9 + [VMEM],
        [
            scratch(length, width), scratch(length, width), scratch(hidden, width), scratch(hidden, width),
            scratch(length, hidden), scratch(length, hidden), scratch(length, width),
            pltpu.SemaphoreType.DMA((4,)), pltpu.SemaphoreType.DMA((6,)),
        ],
        6 * length * hidden * width,
    )


def mlp_rest(rows, grads, hidden, pre, weights):
    length, width = rows.shape
    units = weights.shape[0] // 16
    total = 8 * units
    half = length // 2
    count = length // 4
    tile = 256

    def kernel(*refs):
        rows_ref, grads_ref, hidden_ref, pre_ref = refs[:4]
        weight_ref, near_ref, far_ref, grad_out = refs[4:8]
        rows_s, grads_s, hidden_s, pre_s, proj_s, ahead_s, fc_s, back_s, sems, outs = refs[8:]
        fetch([hidden_ref], hidden_s, sems.at[0])
        fetch([weight_ref.at[pl.ds((2 * i + 1) * units, units)] for i in range(8)], proj_s, sems.at[1])
        fetch([pre_ref], pre_s, sems.at[2])
        fetch([rows_ref], rows_s, sems.at[3])
        fetch([grads_ref], grads_s, sems.at[4])
        fetched(hidden_s, sems.at[0])
        fetched(proj_s, sems.at[1])

        @pl.loop(0, 4)
        def _(block):
            at = pl.ds(pl.multiple_of(block * count, count), count)
            ahead_s[at, :] = low(matmul(hidden_s[at, :], proj_s[...], 1, 0))

        sent = [
            send(ahead_s.at[pl.ds(0, half)], near_ref, outs.at[0]),
            send(ahead_s.at[pl.ds(half, half)], far_ref, outs.at[1]),
        ]
        fetched(pre_s, sems.at[2])
        fetched(rows_s, sems.at[3])

        def pieces(source, kind):
            for k in range(8):
                into = grad_out.at[pl.ds((2 * k + kind) * units, units)]
                sent.append(send(source.at[pl.ds(k * units, units)], into, outs.at[2 + kind * 8 + k]))

        @pl.loop(0, total // tile)
        def _(block):
            at = pl.ds(pl.multiple_of(block * tile, tile), tile)
            fc_s[at, :] = low(matmul(pre_s[:, at], rows_s[...], 0, 0))

        pieces(fc_s, 0)
        fetched(grads_s, sems.at[4])

        @pl.loop(0, total // tile)
        def _(block):
            at = pl.ds(pl.multiple_of(block * tile, tile), tile)
            back_s[at, :] = low(matmul(hidden_s[:, at], grads_s[...], 0, 0))

        pieces(back_s, 1)
        for copy in sent:
            copy.wait()

    def out(*rows):
        return ((*rows, width), jnp.bfloat16, ANY)

    return matmul_call(
        kernel,
        "mlp_rest",
        [out(half), out(half), out(16 * units)],
        [rows, grads, hidden, pre, weights],
        [ANY] * 5,
        [
            scratch(length, width), scratch(length, width), scratch(length, total), scratch(length, total),
            scratch(total, width), scratch(length, width), scratch(total, width), scratch(total, width),
            pltpu.SemaphoreType.DMA((5,)), pltpu.SemaphoreType.DMA((18,)),
        ],
        6 * length * total * width,
    )


def head_weight_grads(lefts, rows, grad_rows, places, outs):
    length, columns = lefts[0].shape
    width = rows.shape[1]

    def kernel(*refs):
        left_refs, (rows_ref, grads_ref), refs = refs[:4], refs[4:6], refs[6:]
        out_refs, (full_s, sem) = refs[: len(outs)], refs[len(outs) :]
        for matrix in range(4):
            right = (rows_ref if matrix < 3 else grads_ref)[...]
            full_s[matrix] = low(matmul(left_refs[matrix][...], right, 0, 0))
        for array, index, row, matrix, column, count in places:
            into = out_refs[array]
            into = into if index is None else into.at[index]
            pltpu.make_async_copy(
                full_s.at[matrix, pl.ds(column, count)], into.at[pl.ds(row, count)], sem.at[0]
            ).start()
        pltpu.make_async_copy(full_s, full_s, sem.at[0]).wait()

    return matmul_call(
        kernel,
        "head_weight_grads",
        [(shape, jnp.bfloat16, ANY) for shape in outs],
        [*lefts, rows, grad_rows],
        [VMEM] * 6,
        [scratch(4, columns, width), pltpu.SemaphoreType.DMA((1,))],
        8 * length * columns * width,
    )


def hidden_blocks(fc, proj):
    shard = proj.shape[1]
    return jnp.concatenate([jnp.transpose(fc).reshape(8, -1, shard), proj.reshape(8, -1, shard)], axis=1)


def hidden_unblock(blocks):
    shard = blocks.shape[-1]
    blocks = blocks.reshape(8, 2, -1, shard)
    return blocks[:, 0].reshape(-1, shard), blocks[:, 1].reshape(-1, shard)


def teacher_blocks(qkv, out):
    columns, shard = out.shape
    stack = jnp.concatenate([jnp.transpose(qkv, (0, 2, 1)), out[None]], axis=0)
    stack = stack.reshape(4, 2, columns // (2 * HD), 2, 2, HD // 4, shard)
    return jnp.transpose(stack, (3, 1, 4, 0, 2, 5, 6)).reshape(8, -1, shard)


def teacher_unblock(heads):
    shard = heads.shape[-1]
    stack = heads.reshape(2, 2, 2, 4, -1, HD // 4, shard)
    return jnp.transpose(stack, (3, 1, 4, 0, 2, 5, 6)).reshape(4, -1, shard)


def student_blocks(qkv, out):
    columns, shard = out.shape
    stack = jnp.concatenate([jnp.transpose(qkv, (0, 2, 1)), out[None]], axis=0)
    stack = stack.reshape(4, columns // HD, 8, HD // 8, shard)
    return jnp.transpose(stack, (2, 0, 1, 3, 4)).reshape(8, -1, shard)


def student_unblock(heads):
    shard = heads.shape[-1]
    return jnp.transpose(heads.reshape(8, 4, -1, HD // 8, shard), (1, 2, 0, 3, 4)).reshape(4, -1, shard)


def teacher_places(columns):
    sub = HD // 4
    heads = columns // (2 * HD)
    places = []
    for matrix in range(4):
        for plane in range(2):
            for head in range(heads):
                for dc in range(2):
                    for dy in range(2):
                        column = (plane * heads + head) * HD + (dc * 2 + dy) * sub
                        places.append((dc * 2 + dy, plane, (matrix * heads + head) * sub, matrix, column, sub))
    return places


def student_places(columns):
    sub = HD // 8
    heads = columns // HD
    places = []
    for matrix in range(4):
        for head in range(heads):
            for part in range(8):
                places.append((part, None, (matrix * heads + head) * sub, matrix, head * HD + part * sub, sub))
    return places


def student_grad_places(columns):
    return [(p // 4, p % 4, row, matrix, column, sub) for p, _, row, matrix, column, sub in student_places(columns)]


def on_pairs(*args):
    teacher_in, student_in = args[0:14], args[14:28]
    span_starts, head_slots = args[28], args[29]
    pos = {name: lax.axis_index(name) for name in EVERY}
    y, x, c, z = pos["y"], pos["x"], pos["c"], pos["z"]
    rank = x * 2 + c
    teacher_columns, student_columns = teacher_in[6].shape[0], student_in[6].shape[0]
    teacher_count, student_count = teacher_columns // 2, student_columns // 2
    shard, student_shard = teacher_in[2].shape[0], student_in[2].shape[0]
    length = 4 * teacher_in[0].shape[1]

    order = (2, 3, 7, 8, 9, 13)
    marks = jnp.stack([span_starts[0] // 32, span_starts[0] % 32, 0, 0]).astype(jnp.bfloat16)
    tall = jnp.concatenate(
        [
            jnp.stack([teacher_in[i] for i in order]),
            jnp.pad(jnp.stack([student_in[i] for i in order]), ((0, 0), (0, shard - student_shard))),
            jnp.broadcast_to(marks[:, None], (4, shard)),
        ],
        axis=0,
    )
    blocks = teacher_blocks(teacher_in[4], teacher_in[6])
    blocks = jnp.concatenate([blocks, jnp.broadcast_to(tall[None], (8,) + tall.shape)], axis=1)
    teacher_got = to_plane(blocks)
    teacher_rows, student_rows = rows_out(teacher_in[0][0]), rows_out(student_in[0][0])

    parts = [
        teacher_in[11], teacher_in[5].reshape(-1), student_in[11], student_in[5].reshape(-1),
        jnp.pad(head_slots.astype(jnp.bfloat16), (0, 128 - head_slots.shape[0])),
    ]
    limits = np.cumsum([0] + [part.shape[0] // 128 for part in parts])
    deep = jnp.concatenate([part.reshape(-1, 128) for part in parts], axis=0)
    deep = [deep] + [plane_swap(deep, step) for step in (1, 2, 3)]

    blocks = jnp.concatenate(
        [student_blocks(student_in[4], student_in[6]), hidden_blocks(student_in[10], student_in[12])], axis=1
    )
    student_got = to_plane(after(blocks, teacher_got))

    vectors = teacher_got[:, teacher_count:]

    def width_vectors(block):
        block = wide(jnp.transpose(block, (1, 0, 2)).reshape(6, 1, -1))
        return tuple(block[i] for i in range(6))

    teacher_vectors = width_vectors(vectors[:, :6])
    student_vectors = width_vectors(vectors[:, 6:12, :student_shard])
    starts = vectors[:, 12:14, 0].astype(jnp.int32)
    starts = starts[:, 0] * 32 + starts[:, 1]
    info = jnp.stack([pick(starts, y * 4 + z), 2 * c + (x ^ (z & 1))])

    step = Order()
    first = c == 0

    t0 = step(join_shards(teacher_got[:, :teacher_count]))
    t1, t2, t0y = plane_swap(t0, 1), plane_swap(t0, 2), swap(t0, "y")
    full16, student16 = (teacher_rows.shape, jnp.bfloat16), (student_rows.shape, jnp.bfloat16)
    (normed,) = row_call(
        first_norm_kernel, "first_norm", [full16], step(teacher_rows), teacher_vectors[0], teacher_vectors[1]
    )
    teacher_normed = [normed, swap(normed, "x"), swap(normed, "c")]
    step.mark(normed)
    student_cross = cross(step(join_shards(student_got[:, :student_count])))
    t2 = step(t2)
    t3, t2y = plane_swap(t2, 1), swap(t2, "y")
    t1 = step(t1)
    t1y = swap(t1, "y")
    teacher_hidden_got = to_plane(after(hidden_blocks(teacher_in[10], teacher_in[12]), t1))
    teacher_normed[1] = step(teacher_normed[1])
    teacher_normed.append(swap(teacher_normed[1], "c"))
    t3 = step(t3)
    t3y = swap(t3, "y")

    def halves(one, two, three, four):
        front, rear_part = jnp.stack([one, two]), jnp.stack([three, four])
        return jnp.where(first, front, rear_part), swap(jnp.where(first, rear_part, front), "c")

    own, near = halves(t0, t1, t2, t3)
    s0 = step(student_cross)
    s1, s2, s0y = plane_swap(s0, 1), plane_swap(s0, 2), swap(s0, "y")
    (normed,) = row_call(
        first_norm_kernel, "first_norm", [student16], step(student_rows), student_vectors[0], student_vectors[1]
    )
    student_normed = [normed, swap(normed, "x"), swap(normed, "c")]
    step.mark(normed)
    s2 = step(s2)
    s3, s2y = plane_swap(s2, 1), swap(s2, "y")
    s1 = step(s1)
    s1y = swap(s1, "y")
    teacher_up = rows_out(after(teacher_in[1][0], s1))
    tf0 = step(join_shards(teacher_hidden_got))
    t0y, t1y, t2y, t3y = step(t0y, t1y, t2y, t3y)
    own_over, near_over = halves(t0y, t1y, t2y, t3y)
    teacher_weights = lax.all_gather(after(tf0, t3y), ("y", "z"), axis=0, tiled=True)

    deep = jnp.stack(deep)
    deep = [deep[:, limits[i] : limits[i + 1]].reshape(4, -1) for i in range(5)]
    near_y = jnp.stack([y, 1 - y])
    hidden_spots = (jnp.arange(4)[None] * 8 + jnp.arange(2)[:, None] * 4 + rank).reshape(-1)
    near_c = jnp.stack([c, 1 - c])
    planes = z ^ jnp.arange(4)
    hidden_hot = wide(jnp.arange(4)[:, None] == planes[None]).astype(jnp.bfloat16)

    def hidden_bias(block):
        block = pick(block.reshape(4, 2, 4, -1), rank, 2)
        return jnp.einsum("zk,kyi->yzi", hidden_hot, block, preferred_element_type=jnp.float32).reshape(1, -1)

    teacher_fc_bias, student_fc_bias = hidden_bias(deep[0]), hidden_bias(deep[2])
    two = jnp.where(first, 0, 2)
    block = lax.dynamic_slice_in_dim(deep[1].reshape(4, -1), two, 2, 0)
    block = block.reshape(2, 2, 2, -1, 2, 2, HD // 4)
    block = pick(block, x, 2)
    block = jnp.where(y == 0, block, block[:, :, :, ::-1])
    block = jnp.where(first, block, block[:, :, :, :, ::-1])
    teacher_qv = wide(jnp.transpose(block, (1, 0, 2, 4, 3, 5)).reshape(2, -1))
    slots = lax.dynamic_slice_in_dim(deep[4][:, : head_slots.shape[0]], two, 2, 0)
    keep = wide(pick(slots.reshape(2, 2, -1), x, 1).reshape(-1))
    block = pick(deep[3].reshape(4, 2, -1, 8, HD // 8), z ^ rank)
    eighth = (near_y[:, None] * 4 + planes[None]).reshape(-1)
    order_hot = (jnp.arange(8)[None] == eighth[:, None]).astype(jnp.bfloat16)
    student_qv = jnp.einsum("rp,thpi->thri", order_hot, block, preferred_element_type=jnp.float32).reshape(2, -1)
    ones = jnp.ones((student_qv.shape[1] // HD,), jnp.float32)

    def bias_rows(pair):
        return jnp.stack([pair[0], jnp.zeros_like(pair[0]), pair[1]])[:, None, :]

    teacher_spots, student_spots = teacher_places(teacher_columns), student_places(student_columns)
    head_weights = (own, own_over, near, near_over)
    qkv, normed_all, weights, heads_low, t_near, t_far, logs = front(
        step(*teacher_normed), head_weights, teacher_spots, bias_rows(teacher_qv), teacher_columns, info, keep
    )
    teacher_saved = (qkv, normed_all, weights, heads_low, logs)
    step.mark(t_near)
    t_got = swap(t_far, "c")
    t_over = swap(step(ahead_sum(t_near, t_got)), "x")
    sf0 = step(join_shards(student_got[:, student_count:]))
    student_weights = lax.all_gather(sf0, ("y", "z"), axis=0, tiled=True)
    bias_out, gain_two, shift_two = teacher_vectors[2:5]
    full32 = (teacher_rows.shape, jnp.float32)
    t_middle, normed = row_call(
        mid_norm_kernel, "mid_norm", [full32, full16],
        teacher_rows, t_near, t_got, step(t_over), bias_out, gain_two, shift_two,
    )
    step.mark(normed)
    teacher_normed = [normed, swap(normed, "x"), swap(normed, "c")]
    student_normed[1] = step(student_normed[1])
    student_normed.append(swap(student_normed[1], "c"))
    s3 = step(s3)
    s3y = swap(s3, "y")
    teacher_up = step(teacher_up)
    teacher_ups = [teacher_up, swap(teacher_up, "x"), swap(teacher_up, "c")]
    student_up = rows_out(after(student_in[1][0], teacher_up))
    teacher_normed[1] = step(teacher_normed[1])
    teacher_normed.append(swap(teacher_normed[1], "c"))

    head_weights = (s0, s1, s2, s3, s0y, s1y, s2y, s3y)
    qkv, normed_all, weights, heads_low, s_near, s_far, logs = front(
        step(*student_normed), head_weights, student_spots, bias_rows(student_qv), student_columns, info, ones
    )
    student_saved = (qkv, normed_all, weights, heads_low, logs)
    step.mark(s_near)
    s_got = swap(s_far, "c")
    teacher_ups[1] = step(teacher_ups[1])
    teacher_ups.append(swap(teacher_ups[1], "c"))
    ahead = step(ahead_sum(s_near, s_got))
    s_part, s_over = swap(ahead[:64], "x"), swap(ahead[64:], "x")

    *teacher_mlp, t_near, t_far, teacher_fc = mlp_main(
        step(after(teacher_normed[0], s_part), *teacher_normed[1:]), teacher_ups, teacher_weights, teacher_fc_bias
    )
    step.mark(t_near)
    t_got = swap(t_far, "c")
    ahead = step(ahead_sum(t_near, t_got))
    t_part, t_over = swap(ahead[:64], "x"), swap(ahead[64:], "x")
    bias_out, gain_two, shift_two = student_vectors[2:5]
    student32 = (student_rows.shape, jnp.float32)
    s_middle, normed = row_call(
        mid_norm_kernel, "mid_norm", [student32, student16],
        student_rows, s_near, s_got, jnp.concatenate([s_part, step(s_over)], axis=0), bias_out, gain_two, shift_two,
    )
    step.mark(normed)
    student_normed = [normed, swap(normed, "x"), swap(normed, "c")]
    student_up = step(student_up)
    student_ups = [student_up, swap(student_up, "x"), swap(student_up, "c")]
    teacher_mlp[0] = after(step(teacher_mlp[0]), t_part)
    t_out_near, t_out_far, grads = mlp_rest(*teacher_mlp, teacher_weights)
    step.mark(t_out_near)
    teacher_hidden = lax.psum_scatter(grads, ("y", "z"), scatter_dimension=0, tiled=True)
    width = teacher_rows.shape[1]
    t_dmid, t_ga, teacher_two = row_call(
        mid_back_kernel, "mid_back", [full32, full16, ((4, width), jnp.float32)],
        teacher_up, t_near, t_got, jnp.concatenate([t_part, step(t_over)], axis=0), t_middle, teacher_vectors[3],
    )
    step.mark(t_ga)
    teacher_normed = [t_ga, swap(t_ga, "x"), swap(t_ga, "c")]

    student_normed[1] = step(student_normed[1])
    student_normed.append(swap(student_normed[1], "c"))
    student_ups[1] = step(student_ups[1])
    student_ups.append(swap(student_ups[1], "c"))

    *student_mlp, s_near, s_far, student_fc = mlp_main(
        step(*student_normed), student_ups, student_weights, student_fc_bias
    )
    step.mark(s_near)
    s_got = swap(s_far, "c")
    teacher_normed[1] = step(teacher_normed[1])
    teacher_normed.append(swap(teacher_normed[1], "c"))
    s_over = swap(step(ahead_sum(s_near, s_got)), "x")

    qkv, normed_all, weights, heads_low, logs = teacher_saved
    t_dq, t_dk, t_dv, t_grad_all, t_near, t_far = rear(
        step(*teacher_normed), weights, qkv, heads_low, logs, info, keep
    )
    step.mark(t_near)
    t_got = swap(t_far, "c")
    teacher_saved = ([t_dq, t_dk, t_dv, heads_low], normed_all, t_grad_all)
    width = student_rows.shape[1]
    s_dmid, s_ga, student_two = row_call(
        mid_back_kernel, "mid_back", [student32, student16, ((4, width), jnp.float32)],
        student_up, s_near, s_got, step(s_over), s_middle, student_vectors[3],
    )
    step.mark(s_ga)
    student_normed = [s_ga, swap(s_ga, "x"), swap(s_ga, "c")]
    t_over = swap(step(ahead_sum(t_near, t_got)), "x")
    lefts, right, grad_right = teacher_saved
    lefts[0] = step(lefts[0])
    teacher_width, student_width = teacher_rows.shape[1], student_rows.shape[1]
    th = head_weight_grads(lefts, right, grad_right, teacher_spots, [(2, teacher_count, teacher_width)] * 4)
    teacher_qv_grad = jnp.stack([jnp.sum(wide(t_dq), axis=0), jnp.sum(wide(t_dv), axis=0)])
    step.mark(th[0])
    th_over_got, th_got = swap(th[3], "c"), swap(th[2], "c")

    def planes_of(mine, got):
        odd = jnp.stack([jnp.where(first, mine[1], got[1]), jnp.where(first, got[1], mine[1])])
        even = jnp.stack([jnp.where(first, mine[0], got[0]), jnp.where(first, got[0], mine[0])])
        return odd, even

    odd_over, even_over = planes_of(th[1], step(th_over_got))
    odd_got, even_got = swap(odd_over, "y"), swap(even_over, "y")
    th_odd, th_even = planes_of(th[0], th_got)
    step.mark(odd_over)
    student_mlp[0] = step(student_mlp[0])
    s_out_near, s_out_far, grads = mlp_rest(*student_mlp, student_weights)
    step.mark(s_out_near)
    student_hidden = lax.psum_scatter(grads, ("y", "z"), scatter_dimension=0, tiled=True)
    teacher_dx, teacher_one = row_call(
        first_back_kernel, "first_back", [full16, ((2, teacher_width), jnp.float32)],
        t_near, t_got, step(t_over), teacher_rows, t_dmid, teacher_vectors[0],
    )
    step.mark(teacher_dx)
    t_out_got = swap(after(t_out_far, teacher_dx), "c")
    teacher_dx = rows_home(teacher_dx)
    teacher_hidden = to_plane(split_shards(step(teacher_hidden)))
    student_normed[1] = step(student_normed[1])
    student_normed.append(swap(student_normed[1], "c"))
    qkv, normed_all, weights, heads_low, logs = student_saved
    s_dq, s_dk, s_dv, s_grad_all, s_near, s_far = rear(
        step(*student_normed), weights, qkv, heads_low, logs, info, ones
    )
    step.mark(s_near)
    s_got = swap(s_far, "c")
    odd_got = step(odd_got)
    th_odd_got = plane_swap(step(low(wide(th_odd) + wide(odd_got))), 1)
    s_over = swap(step(ahead_sum(s_near, s_got)), "x")
    sh_near, sh_far = head_weight_grads(
        [step(s_dq), s_dk, s_dv, heads_low], normed_all, s_grad_all, student_grad_places(student_columns),
        [(4, student_count, student_width)] * 2,
    )
    student_qv_grad = jnp.stack([jnp.sum(wide(s_dq), axis=0), jnp.sum(wide(s_dv), axis=0)])
    step.mark(sh_near)
    sh_got = swap(sh_far, "y")
    th_odd_got, even_got = step(th_odd_got, even_got)
    th_even = wide(th_even) + wide(even_got)
    th_even_got = plane_swap(low(th_even[1] + wide(th_odd_got[1])), 2)
    t_out_over = swap(step(ahead_sum(t_out_near, t_out_got)), "x")
    student_dx, student_one = row_call(
        first_back_kernel, "first_back", [student16, ((2, student_width), jnp.float32)],
        s_near, s_got, step(s_over), student_rows, s_dmid, student_vectors[0],
    )
    step.mark(student_dx)
    s_out_got = swap(after(s_out_far, student_dx), "c")
    student_dx = rows_home(student_dx)

    def spread(places, values):
        hot = (jnp.arange(32)[:, None] == places[None]).astype(jnp.float32)
        return jnp.dot(hot, values, precision=lax.Precision.HIGHEST)

    head_planes = planes.reshape(2, 2)
    head_planes = jnp.where(first, head_planes[0], head_planes[1])
    column_spots = (
        head_planes[:, None, None] * 8 + x * 4 + near_y[None, None, :] * 2 + near_c[None, :, None]
    ).reshape(-1)
    eighth_spots = rank * 8 + eighth

    teacher_qv_grad = teacher_qv_grad.reshape(2, 2, -1, 2, 2, HD // 4)
    teacher_qv_grad = jnp.transpose(teacher_qv_grad, (1, 3, 4, 0, 2, 5)).reshape(8, -1)
    student_qv_grad = jnp.transpose(student_qv_grad.reshape(2, -1, 8, HD // 8), (2, 0, 1, 3)).reshape(8, -1)
    hidden_grads = jnp.concatenate([teacher_fc.reshape(8, -1), student_fc.reshape(8, -1)], axis=1)
    hidden_grads = spread(hidden_spots, hidden_grads)
    lanes = hidden_grads.shape[1]
    column_grads = jnp.concatenate(
        [spread(column_spots, teacher_qv_grad), spread(eighth_spots, student_qv_grad)], axis=1
    )
    column_grads = jnp.pad(column_grads, ((0, 0), (0, lanes - column_grads.shape[1])))

    def stacked(one, two):
        tall = jnp.concatenate([one, two, jnp.zeros_like(one)], axis=0)
        return [tall[:, i : i + lanes] for i in range(0, tall.shape[1], lanes)]

    total = jnp.concatenate(
        [hidden_grads, column_grads] + stacked(teacher_one, teacher_two) + stacked(student_one, student_two), axis=0
    )
    total = step(total)
    other = swap(total, "c")
    sh_total = step(wide(sh_near) + wide(sh_got))
    sh_odd_got = plane_swap(low(sh_total[1::2]), 1)
    total = total + step(other)
    other = swap(total, "x")
    teacher_hidden = step(teacher_hidden)
    s_out_over = swap(step(ahead_sum(s_out_near, s_out_got)), "x")
    count = t_middle.shape[0]
    teacher_out = low(
        t_middle + (wide(t_out_near[:count]) + wide(t_out_got[:count]) + wide(step(t_out_over)) + teacher_vectors[5])
    )
    teacher_out = rows_home(teacher_out)
    sh_even = step(sh_total[0::2] + wide(sh_odd_got))
    sh_even_got = plane_swap(low(sh_even[1]), 2)
    teacher_head = low(th_even[0] + wide(th_odd_got[0]) + wide(step(th_even_got)))
    teacher_head = to_plane(split_shards(teacher_head))
    total = total + step(other)
    other = swap(total, "y")
    student_head = cross(low(sh_even[0] + wide(step(sh_even_got))))
    count = s_middle.shape[0]
    student_out = low(
        s_middle + (wide(s_out_near[:count]) + wide(s_out_got[:count]) + wide(step(s_out_over)) + student_vectors[5])
    )
    student_out = rows_home(student_out)
    total = total + step(other)
    other = plane_swap(total, 1)
    student_got = jnp.concatenate([step(student_head), student_hidden], axis=0)
    teacher_grads = (teacher_unblock(step(teacher_head)), *hidden_unblock(teacher_hidden))
    student_got = to_plane(split_shards(student_got))
    total = total + step(other)
    other = plane_swap(total, 2)
    teacher_dx, student_dx, teacher_out, student_out = step(teacher_dx, student_dx, teacher_out, student_out)
    student_got = step(student_got)
    student_grads = (student_unblock(student_got[:, :student_count]), *hidden_unblock(student_got[:, student_count:]))
    total = total + other
    teacher_out, teacher_dx = teacher_out[None], teacher_dx[None]
    student_out, student_dx = student_out[None], student_dx[None]

    def matrices(grads):
        stack, fc_grad, proj_grad = grads
        return (
            wide(jnp.transpose(stack[:3], (0, 2, 1))), wide(stack[3]),
            wide(jnp.transpose(fc_grad)), wide(proj_grad),
        )

    own = y * 4 + rank
    units, student_units = teacher_fc.size // 8, student_fc.size // 8
    columns, student_columns = teacher_columns // 4, student_columns // 4
    hidden_grads = pick(total[:32].reshape(4, 8, lanes), z)
    teacher_fc = hidden_grads[:, :units].reshape(-1)
    student_fc = hidden_grads[:, units : units + student_units].reshape(-1)
    column_grads = pick(total[32:64].reshape(4, 8, lanes), z)
    block = column_grads[:, :columns].reshape(2, 2, 2, 2, -1, HD // 4)
    teacher_qv_grad = jnp.transpose(block, (3, 0, 4, 1, 2, 5)).reshape(2, -1)
    block = column_grads[:, columns : columns + student_columns].reshape(8, 2, -1, HD // 8)
    student_qv_grad = jnp.transpose(block, (1, 2, 0, 3)).reshape(2, -1)
    tall = total[64:].reshape(-1, 8, lanes)
    runs = teacher_width // lanes

    def width_grads(tall, count):
        tall = jnp.concatenate([tall[i] for i in range(count)], axis=1)[:6]
        return tuple(pick(tall.reshape(6, 8, -1), own, 1))

    def arranged(outputs, input_grad, grads, sums, qv_grad, fc_grad):
        return (
            outputs, input_grad, sums[0], sums[1], grads[0], qv_grad, grads[1],
            sums[2], sums[3], sums[4], grads[2], fc_grad, grads[3], sums[5],
        )

    return arranged(
        teacher_out, teacher_dx, matrices(teacher_grads), width_grads(tall[:runs], runs), teacher_qv_grad, teacher_fc
    ) + arranged(
        student_out, student_dx, matrices(student_grads), width_grads(tall[runs:], student_width // lanes), student_qv_grad, student_fc
    )


def on_plane(spec):
    names = {"dp": PLANE, "tensor": "z"}
    return P(*(names.get(entry, None) for entry in spec))


def solution(mesh):
    in_specs = (
        P("dp", "tensor", None),
        P("dp", "tensor", None),
        P("dp"),
        P("dp"),
        P(None, "dp", "tensor"),
        P(None, "tensor"),
        P("tensor", "dp"),
        P("dp"),
        P("dp"),
        P("dp"),
        P("dp", "tensor"),
        P("tensor"),
        P("tensor", "dp"),
        P("dp"),
        P("dp", "tensor", None),
        P("dp", "tensor", None),
        P("dp"),
        P("dp"),
        P(None, "dp", "tensor"),
        P(None, "tensor"),
        P("tensor", "dp"),
        P("dp"),
        P("dp"),
        P("dp"),
        P("dp", "tensor"),
        P("tensor"),
        P("tensor", "dp"),
        P("dp"),
        P("dp"),
        P("tensor"),
    )
    out_specs = (
        P("dp", "tensor", None),
        P("dp", "tensor", None),
        P("dp"),
        P("dp"),
        P(None, "dp", "tensor"),
        P(None, "tensor"),
        P("tensor", "dp"),
        P("dp"),
        P("dp"),
        P("dp"),
        P("dp", "tensor"),
        P("tensor"),
        P("tensor", "dp"),
        P("dp"),
        P("dp", "tensor", None),
        P("dp", "tensor", None),
        P("dp"),
        P("dp"),
        P(None, "dp", "tensor"),
        P(None, "tensor"),
        P("tensor", "dp"),
        P("dp"),
        P("dp"),
        P("dp"),
        P("dp", "tensor"),
        P("tensor"),
        P("tensor", "dp"),
        P("dp"),
    )
    if tuple(mesh.devices.shape) == (8, 4):
        finer = Mesh(mesh.devices.reshape(2, 2, 2, 4), EVERY)
        return jax.shard_map(
            on_pairs,
            mesh=finer,
            in_specs=tuple(on_plane(spec) for spec in in_specs),
            out_specs=tuple(on_plane(spec) for spec in out_specs),
            check_vma=False,
        )
    return jax.shard_map(
        on_device, mesh=mesh, in_specs=in_specs, out_specs=out_specs, check_vma=False
    )
```

```python
import functools

import jax
import jax.numpy as jnp
import numpy as np
from jax import lax
from jax.experimental import pallas as pl
from jax.experimental.pallas import tpu as pltpu
from jax.sharding import Mesh
from jax.sharding import PartitionSpec as P

HD = 64
SPAN = 256


epsilon = 1e-05
negative = -1e30


def layer_norm(values, norm_gain, norm_shift):
    center = values - jnp.mean(values, axis=-1, keepdims=True)
    spread = jnp.mean(center * center, axis=-1, keepdims=True)
    return center * lax.rsqrt(spread + epsilon) * norm_gain + norm_shift


def gelu_tanh(values):
    return jax.nn.gelu(values, approximate=True)


def visibility(first_row, block_rows, length, span_start):
    query_pos = first_row + jnp.arange(block_rows, dtype=jnp.int32)
    key_pos = jnp.arange(length, dtype=jnp.int32)
    query_in = (query_pos >= span_start) & (query_pos < span_start + SPAN)
    key_in = (key_pos >= span_start) & (key_pos < span_start + SPAN)
    return (key_pos[None, :] <= query_pos[:, None]) | query_in[:, None] & key_in[None, :]


def block_scores(query_block, key_rows, visible, score_scale):
    scores = (
        jnp.einsum("qhe,khe->hqk", query_block, key_rows, preferred_element_type=jnp.float32)
        * score_scale
    )
    return jnp.where(visible[None], scores, negative)


def attention_forward(query_rows, key_rows, value_rows, span_start, block_rows, score_scale):
    length = query_rows.shape[0]
    results = []
    log_sums = []
    for block_index in range(length // block_rows):
        first_row = block_index * block_rows
        visible = visibility(first_row, block_rows, length, span_start)
        scores = block_scores(
            query_rows[first_row : first_row + block_rows], key_rows, visible, score_scale
        )
        row_peak = jnp.max(scores, axis=-1, keepdims=True)
        raised = jnp.exp(scores - row_peak)
        row_total = jnp.sum(raised, axis=-1, keepdims=True)
        weights = (raised / row_total).astype(jnp.bfloat16)
        results.append(
            jnp.einsum("hqk,khe->qhe", weights, value_rows, preferred_element_type=jnp.float32)
        )
        log_sums.append(row_peak + jnp.log(row_total))
    return (jnp.concatenate(results, axis=0), log_sums)


def attention_backward(
    query_rows, key_rows, value_rows, log_sums, heads_grad, span_start, block_rows, score_scale
):
    length = query_rows.shape[0]
    query_grads = []
    key_grad = jnp.zeros(key_rows.shape, jnp.float32)
    value_grad = jnp.zeros(value_rows.shape, jnp.float32)
    for block_index in range(length // block_rows):
        first_row = block_index * block_rows
        last_row = first_row + block_rows
        visible = visibility(first_row, block_rows, length, span_start)
        scores = block_scores(query_rows[first_row:last_row], key_rows, visible, score_scale)
        probability = jnp.exp(scores - log_sums[block_index])
        grad_block = heads_grad[first_row:last_row]
        value_grad = value_grad + jnp.einsum(
            "hqk,qhe->khe",
            probability.astype(jnp.bfloat16),
            grad_block,
            preferred_element_type=jnp.float32,
        )
        prob_grad = jnp.einsum(
            "qhe,khe->hqk", grad_block, value_rows, preferred_element_type=jnp.float32
        )
        weighted = jnp.sum(probability * prob_grad, axis=-1, keepdims=True)
        score_grad = (probability * (prob_grad - weighted)).astype(jnp.bfloat16)
        query_grads.append(
            jnp.einsum("hqk,khe->qhe", score_grad, key_rows, preferred_element_type=jnp.float32)
            * score_scale
        )
        key_grad = (
            key_grad
            + jnp.einsum(
                "hqk,qhe->khe",
                score_grad,
                query_rows[first_row:last_row],
                preferred_element_type=jnp.float32,
            )
            * score_scale
        )
    return (jnp.concatenate(query_grads, axis=0), key_grad, value_grad)


def gather_rows(normed):
    return lax.all_gather(normed, "tensor", axis=0, tiled=True)


def gather_grads(branch_grad):
    return lax.all_gather(branch_grad, "tensor", axis=0, tiled=True)


def sum_rows(left_rows, right_weight):
    return lax.psum_scatter(
        jnp.dot(left_rows, right_weight, preferred_element_type=jnp.float32).astype(jnp.bfloat16),
        "tensor",
        scatter_dimension=0,
        tiled=True,
    ).astype(jnp.float32)


def back_rows(grad_stack, weight_stack):
    return lax.psum_scatter(
        jnp.einsum(
            "sle,sde->ld", grad_stack, weight_stack, preferred_element_type=jnp.float32
        ).astype(jnp.bfloat16),
        "tensor",
        scatter_dimension=0,
        tiled=True,
    ).astype(jnp.float32)


def run_block(
    inputs,
    upstream,
    attn_gain,
    attn_shift,
    qkv_weight,
    qv_bias,
    out_weight,
    out_bias,
    mlp_gain,
    mlp_shift,
    fc_weight,
    fc_bias,
    proj_weight,
    proj_bias,
    span_start,
    head_keep,
):
    gathered = (
        lax.all_gather(qkv_weight, "dp", axis=1, tiled=True),
        lax.all_gather(out_weight, "dp", axis=1, tiled=True),
        lax.all_gather(fc_weight, "dp", axis=0, tiled=True),
        lax.all_gather(proj_weight, "dp", axis=1, tiled=True),
        lax.all_gather(attn_gain, "dp", axis=0, tiled=True),
        lax.all_gather(attn_shift, "dp", axis=0, tiled=True),
        lax.all_gather(out_bias, "dp", axis=0, tiled=True),
        lax.all_gather(mlp_gain, "dp", axis=0, tiled=True),
        lax.all_gather(mlp_shift, "dp", axis=0, tiled=True),
        lax.all_gather(proj_bias, "dp", axis=0, tiled=True),
    )
    qkv_full, out_full, fc_full, proj_full = (gathered[0], gathered[1], gathered[2], gathered[3])
    gain_one = gathered[4].astype(jnp.float32)
    shift_one = gathered[5].astype(jnp.float32)
    bias_out = gathered[6].astype(jnp.float32)
    gain_two = gathered[7].astype(jnp.float32)
    shift_two = gathered[8].astype(jnp.float32)
    bias_proj = gathered[9].astype(jnp.float32)
    rows_first = inputs[0].astype(jnp.float32)
    normed, norm_back_one = jax.vjp(layer_norm, rows_first, gain_one, shift_one)
    normed_all = gather_rows(normed.astype(jnp.bfloat16))
    projected = jnp.einsum("ld,tde->tle", normed_all, qkv_full, preferred_element_type=jnp.float32)
    bias_pair = qv_bias.astype(jnp.float32)
    length = normed_all.shape[0]
    head_count = head_keep.shape[0]
    head_split = (length, head_count, HD)
    query_rows = (projected[0] + bias_pair[0]).astype(jnp.bfloat16).reshape(head_split)
    key_rows = projected[1].astype(jnp.bfloat16).reshape(head_split)
    value_rows = (projected[2] + bias_pair[1]).astype(jnp.bfloat16).reshape(head_split)
    block_rows = min(512, length)
    score_scale = 1.0 / HD**0.5
    attended, log_sums = attention_forward(
        query_rows, key_rows, value_rows, span_start, block_rows, score_scale
    )
    keep_float = head_keep.astype(jnp.float32)[None, :, None]
    heads_low = (attended * keep_float).astype(jnp.bfloat16).reshape(length, head_count * HD)
    attn_sum = sum_rows(heads_low, out_full)
    middle = rows_first + (attn_sum + bias_out)
    normed_two, norm_back_two = jax.vjp(layer_norm, middle, gain_two, shift_two)
    normed_two_all = gather_rows(normed_two.astype(jnp.bfloat16))
    hidden_pre = jnp.dot(
        normed_two_all, fc_full, preferred_element_type=jnp.float32
    ) + fc_bias.astype(jnp.float32)
    hidden, gelu_back = jax.vjp(gelu_tanh, hidden_pre)
    hidden_low = hidden.astype(jnp.bfloat16)
    mlp_sum = sum_rows(hidden_low, proj_full)
    result = middle + (mlp_sum + bias_proj)
    outputs = result.astype(jnp.bfloat16)[None]
    grad_result = upstream[0].astype(jnp.float32)
    grad_mlp_all = gather_grads(upstream[0])
    proj_bias_grad = jnp.sum(grad_mlp_all, axis=0, dtype=jnp.float32)
    proj_grad = jnp.einsum(
        "lf,ld->fd", hidden_low, grad_mlp_all, preferred_element_type=jnp.float32
    )
    hidden_grad = jnp.einsum(
        "ld,fd->lf", grad_mlp_all, proj_full, preferred_element_type=jnp.float32
    )
    pre_grad = gelu_back(hidden_grad)[0].astype(jnp.bfloat16)
    fc_bias_grad = jnp.sum(pre_grad, axis=0, dtype=jnp.float32)
    fc_grad = jnp.einsum("ld,lf->df", normed_two_all, pre_grad, preferred_element_type=jnp.float32)
    normed_two_grad = back_rows(pre_grad[None], fc_full[None])
    middle_from_norm, gain_two_grad, shift_two_grad = norm_back_two(normed_two_grad)
    middle_grad = grad_result + middle_from_norm
    grad_attn_all = gather_grads(middle_grad.astype(jnp.bfloat16))
    out_bias_grad = jnp.sum(grad_attn_all, axis=0, dtype=jnp.float32)
    out_grad = jnp.einsum("le,ld->ed", heads_low, grad_attn_all, preferred_element_type=jnp.float32)
    heads_grad = (
        jnp.einsum("ld,ed->le", grad_attn_all, out_full, preferred_element_type=jnp.float32)
        .astype(jnp.bfloat16)
        .reshape(head_split)
    )
    heads_grad = heads_grad * head_keep.astype(jnp.bfloat16)[None, :, None]
    query_grad, key_grad, value_grad = attention_backward(
        query_rows, key_rows, value_rows, log_sums, heads_grad, span_start, block_rows, score_scale
    )
    qkv_low = jnp.stack(
        [
            query_grad.reshape(length, head_count * HD),
            key_grad.reshape(length, head_count * HD),
            value_grad.reshape(length, head_count * HD),
        ]
    ).astype(jnp.bfloat16)
    qv_bias_grad = jnp.stack(
        [
            jnp.sum(qkv_low[0], axis=0, dtype=jnp.float32),
            jnp.sum(qkv_low[2], axis=0, dtype=jnp.float32),
        ]
    )
    qkv_grad = jnp.einsum("ld,tle->tde", normed_all, qkv_low, preferred_element_type=jnp.float32)
    normed_grad = back_rows(qkv_low, qkv_full)
    rows_from_norm, gain_one_grad, shift_one_grad = norm_back_one(normed_grad)
    input_grad = (middle_grad + rows_from_norm).astype(jnp.bfloat16)[None]
    norm_sums = lax.psum((gain_one_grad, shift_one_grad, gain_two_grad, shift_two_grad), "tensor")
    matrices = (
        qkv_grad,
        out_grad,
        fc_grad,
        proj_grad,
        norm_sums[0],
        norm_sums[1],
        out_bias_grad,
        norm_sums[2],
        norm_sums[3],
        proj_bias_grad,
    )
    biases = (qv_bias_grad, fc_bias_grad)
    return (outputs, input_grad, matrices, biases)


def arrange(outputs, input_grad, matrices, biases):
    return (
        outputs,
        input_grad,
        matrices[4],
        matrices[5],
        matrices[0],
        biases[0],
        matrices[1],
        matrices[6],
        matrices[7],
        matrices[8],
        matrices[2],
        biases[1],
        matrices[3],
        matrices[9],
    )


def on_device(
    teacher_input,
    teacher_upstream,
    teacher_attn_gain,
    teacher_attn_shift,
    teacher_qkv_weight,
    teacher_qv_bias,
    teacher_out_weight,
    teacher_out_bias,
    teacher_mlp_gain,
    teacher_mlp_shift,
    teacher_fc_weight,
    teacher_fc_bias,
    teacher_proj_weight,
    teacher_proj_bias,
    student_input,
    student_upstream,
    student_attn_gain,
    student_attn_shift,
    student_qkv_weight,
    student_qv_bias,
    student_out_weight,
    student_out_bias,
    student_mlp_gain,
    student_mlp_shift,
    student_fc_weight,
    student_fc_bias,
    student_proj_weight,
    student_proj_bias,
    span_starts,
    head_slots,
):
    span_start = span_starts[0]
    teacher = run_block(
        teacher_input,
        teacher_upstream,
        teacher_attn_gain,
        teacher_attn_shift,
        teacher_qkv_weight,
        teacher_qv_bias,
        teacher_out_weight,
        teacher_out_bias,
        teacher_mlp_gain,
        teacher_mlp_shift,
        teacher_fc_weight,
        teacher_fc_bias,
        teacher_proj_weight,
        teacher_proj_bias,
        span_start,
        head_slots,
    )
    student_keep = jnp.ones((student_qv_bias.shape[1] // HD,), jnp.int32)
    student = run_block(
        student_input,
        student_upstream,
        student_attn_gain,
        student_attn_shift,
        student_qkv_weight,
        student_qv_bias,
        student_out_weight,
        student_out_bias,
        student_mlp_gain,
        student_mlp_shift,
        student_fc_weight,
        student_fc_bias,
        student_proj_weight,
        student_proj_bias,
        span_start,
        student_keep,
    )
    teach_parts = teacher[2]
    learn_parts = student[2]
    summed = (
        lax.psum_scatter(teach_parts[0], "dp", scatter_dimension=1, tiled=True),
        lax.psum_scatter(teach_parts[1], "dp", scatter_dimension=1, tiled=True),
        lax.psum_scatter(teach_parts[2], "dp", scatter_dimension=0, tiled=True),
        lax.psum_scatter(teach_parts[3], "dp", scatter_dimension=1, tiled=True),
        lax.psum_scatter(teach_parts[4], "dp", scatter_dimension=0, tiled=True),
        lax.psum_scatter(teach_parts[5], "dp", scatter_dimension=0, tiled=True),
        lax.psum_scatter(teach_parts[6], "dp", scatter_dimension=0, tiled=True),
        lax.psum_scatter(teach_parts[7], "dp", scatter_dimension=0, tiled=True),
        lax.psum_scatter(teach_parts[8], "dp", scatter_dimension=0, tiled=True),
        lax.psum_scatter(teach_parts[9], "dp", scatter_dimension=0, tiled=True),
        lax.psum_scatter(learn_parts[0], "dp", scatter_dimension=1, tiled=True),
        lax.psum_scatter(learn_parts[1], "dp", scatter_dimension=1, tiled=True),
        lax.psum_scatter(learn_parts[2], "dp", scatter_dimension=0, tiled=True),
        lax.psum_scatter(learn_parts[3], "dp", scatter_dimension=1, tiled=True),
        lax.psum_scatter(learn_parts[4], "dp", scatter_dimension=0, tiled=True),
        lax.psum_scatter(learn_parts[5], "dp", scatter_dimension=0, tiled=True),
        lax.psum_scatter(learn_parts[6], "dp", scatter_dimension=0, tiled=True),
        lax.psum_scatter(learn_parts[7], "dp", scatter_dimension=0, tiled=True),
        lax.psum_scatter(learn_parts[8], "dp", scatter_dimension=0, tiled=True),
        lax.psum_scatter(learn_parts[9], "dp", scatter_dimension=0, tiled=True),
    )
    totals = lax.psum((teacher[3][0], teacher[3][1], student[3][0], student[3][1]), "dp")
    teacher_matrices = summed[0:10]
    student_matrices = summed[10:20]
    teacher_biases = (totals[0], totals[1])
    student_biases = (totals[2], totals[3])
    return arrange(teacher[0], teacher[1], teacher_matrices, teacher_biases) + arrange(
        student[0], student[1], student_matrices, student_biases
    )


PLANE = ("y", "x", "c")
EVERY = ("y", "x", "c", "z")
TILE = 256


def swap(values, axis):
    return lax.ppermute(values, axis, ((0, 1), (1, 0)))


def index_of(y, x, c, z):
    return ((y * 2 + x) * 2 + c) * 4 + z


def cross(values):
    pairs = tuple(
        ((y * 4 + a) * 4 + z, (y * 4 + z) * 4 + a) for y in range(2) for a in range(4) for z in range(4)
    )
    return lax.ppermute(values, EVERY, pairs)


def row_pairs():
    return tuple(
        (index_of(y, x, c, z), index_of(y, (z ^ c) & 1, z >> 1, 2 * x + c))
        for y in range(2)
        for x in range(2)
        for c in range(2)
        for z in range(4)
    )


def rows_out(values):
    return lax.ppermute(values, EVERY, row_pairs())


def rows_home(values):
    return lax.ppermute(values, EVERY, tuple((b, a) for a, b in row_pairs()))


def pick(values, index, axis=0):
    return lax.dynamic_index_in_dim(values, index, axis, keepdims=False)


def wide(values):
    return values.astype(jnp.float32)


def low(values):
    return values.astype(jnp.bfloat16)


def matmul(left, right, left_dim, right_dim):
    return lax.dot_general(
        left, right, (((left_dim,), (right_dim,)), ((), ())), preferred_element_type=jnp.float32
    )


class Order:
    def __init__(self):
        self.last = None

    def __call__(self, *values):
        if self.last is not None:
            values = lax.optimization_barrier((*values, self.last))[:-1]
        self.last = values[0]
        return values[0] if len(values) == 1 else values

    def mark(self, value):
        self.last = value


def after(values, earlier):
    return lax.optimization_barrier((values, earlier))[0]


def to_plane(blocks):
    return lax.all_to_all(blocks, PLANE, 0, 0)


def join_shards(blocks):
    return jnp.transpose(blocks, (1, 0, 2)).reshape(blocks.shape[1], -1)


def split_shards(rows):
    return jnp.transpose(rows.reshape(rows.shape[0], 8, -1), (1, 0, 2))


def ahead_sum(near, got):
    count = near.shape[0] // 2
    return low(wide(near[count:]) + wide(got[count:]))


def plane_swap(values, bit):
    return lax.ppermute(values, "z", tuple((i, i ^ bit) for i in range(4)))


def row_call(kernel, name, outs, *args):
    rows = outs[0][0][0]
    size = sum(a.size * a.dtype.itemsize for a in args)

    def spec(shape):
        return pl.BlockSpec((min(shape[0], rows), shape[1]), lambda i: (0, 0))

    return pl.pallas_call(
        kernel,
        grid=(1,),
        in_specs=[spec(a.shape) for a in args],
        out_specs=[spec(shape) for shape, _ in outs],
        out_shape=[jax.ShapeDtypeStruct(shape, dtype) for shape, dtype in outs],
        cost_estimate=pl.CostEstimate(flops=args[0].size // 16, transcendentals=0, bytes_accessed=size // 128),
        name=name,
    )(*args)


def centered(rows):
    center = rows - jnp.mean(rows, axis=-1, keepdims=True)
    spread = jnp.mean(center * center, axis=-1, keepdims=True)
    scale = lax.rsqrt(spread + epsilon)
    return center * scale, scale


def first_norm_kernel(x_ref, gain_ref, shift_ref, out_ref):
    unit, _ = centered(wide(x_ref[...]))
    out_ref[...] = low(unit * gain_ref[...] + shift_ref[...])


def mid_norm_kernel(x_ref, a_ref, b_ref, c_ref, bias_ref, gain_ref, shift_ref, mid_ref, out_ref):
    branch = wide(a_ref[...]) + wide(b_ref[...]) + wide(c_ref[...])
    middle = wide(x_ref[...]) + (branch + bias_ref[...])
    mid_ref[...] = middle
    unit, _ = centered(middle)
    out_ref[...] = low(unit * gain_ref[...] + shift_ref[...])


def norm_back(grad, rows, gain):
    unit, scale = centered(rows)
    t = grad * gain
    back = scale * (
        t - jnp.mean(t, axis=-1, keepdims=True) - unit * jnp.mean(t * unit, axis=-1, keepdims=True)
    )
    return back, jnp.sum(grad * unit, axis=0, keepdims=True), jnp.sum(grad, axis=0, keepdims=True)


def mid_back_kernel(g_ref, a_ref, b_ref, c_ref, mid_ref, gain_ref, dmid_ref, ga_ref, sums_ref):
    up = wide(g_ref[...])
    grad = wide(a_ref[...]) + wide(b_ref[...]) + wide(c_ref[...])
    back, gain_sum, shift_sum = norm_back(grad, mid_ref[...], gain_ref[...])
    dmid = up + back
    dmid_ref[...] = dmid
    ga = low(dmid)
    ga_ref[...] = ga
    sums_ref[0:1] = jnp.sum(wide(ga), axis=0, keepdims=True)
    sums_ref[1:2] = gain_sum
    sums_ref[2:3] = shift_sum
    sums_ref[3:4] = jnp.sum(up, axis=0, keepdims=True)


def first_back_kernel(a_ref, b_ref, c_ref, x_ref, dmid_ref, gain_ref, dx_ref, sums_ref):
    grad = wide(a_ref[...]) + wide(b_ref[...]) + wide(c_ref[...])
    back, gain_sum, shift_sum = norm_back(grad, wide(x_ref[...]), gain_ref[...])
    dx_ref[...] = low(dmid_ref[...] + back)
    sums_ref[0:1] = gain_sum
    sums_ref[1:2] = shift_sum


def place_of(block, own):
    return block ^ own


def tile_visible(first_key, first_query, start):
    shape = (TILE, TILE)
    key = first_key + lax.broadcasted_iota(jnp.int32, shape, 0)
    query = first_query + lax.broadcasted_iota(jnp.int32, shape, 1)
    key_in = (key >= start) & (key < start + SPAN)
    query_in = (query >= start) & (query < start + SPAN)
    return (key <= query) | (key_in & query_in)


def tile_bounds(block, blocks, start):
    more = (start // TILE == block) & (start % TILE != 0)
    return jnp.minimum(block + 1 + more.astype(jnp.int32), blocks)


def head_lanes(width, head):
    lane = lax.broadcasted_iota(jnp.int32, (1, width), 1)
    return (lane >= head * HD) & (lane < (head + 1) * HD)


def lane_chunks(columns):
    chunks = []
    for first in range(0, columns, 2 * HD):
        lanes = min(2 * HD, columns - first)
        chunks.append((first, lanes, lanes // HD))
    return chunks


def one_head(values, head, heads):
    if heads == 1:
        return values
    lane = lax.broadcasted_iota(jnp.int32, (1, values.shape[1]), 1)
    return jnp.where((lane >= HD) == (head == 1), values, jnp.zeros_like(values))


def attend_block(block, start, rank, keep_ref, qkv_s, heads_s, logs_ref):
    columns = qkv_s.shape[-1]
    chunks = lane_chunks(columns)
    here = pl.ds(pl.multiple_of(place_of(block, rank) * TILE, TILE), TILE)
    queries = []
    for first, lanes, heads in chunks:
        query = qkv_s[0, here, first : first + lanes]
        queries.append([one_head(query, h, heads) for h in range(heads)])

    def tile(index, carry, masked):
        rows = pl.ds(pl.multiple_of(place_of(index, rank) * TILE, TILE), TILE)
        if masked:
            visible = tile_visible(index * TILE, block * TILE, start)
        scores = []
        for (first, lanes, heads), query in zip(chunks, queries):
            keys = qkv_s[1, rows, first : first + lanes]
            for h in range(heads):
                score = matmul(keys, query[h], 1, 1)
                scores.append(jnp.where(visible, score, negative) if masked else score)
        out = []
        number = 0
        for first, lanes, heads in chunks:
            values = qkv_s[2, rows, first : first + lanes]
            for h in range(heads):
                peak, total, acc = carry[number]
                score = scores[number]
                new_peak = jnp.maximum(peak, jnp.max(score, axis=0, keepdims=True))
                decay = jnp.exp(peak - new_peak)
                raised = jnp.exp(score - new_peak)
                total = total * decay + jnp.sum(raised, axis=0, keepdims=True)
                part = matmul(values, low(raised), 0, 0)
                acc = acc * decay + part[h * HD : (h + 1) * HD]
                out.append((new_peak, total, acc))
                number += 1
        return tuple(out)

    carry = tuple(
        (
            jnp.full((1, TILE), negative, jnp.float32),
            jnp.zeros((1, TILE), jnp.float32),
            jnp.zeros((HD, TILE), jnp.float32),
        )
        for _ in range(columns // HD)
    )
    carry = lax.fori_loop(0, block, lambda i, s: tile(i, s, False), carry)
    carry = lax.fori_loop(block, tile_bounds(block, 4, start), lambda i, s: tile(i, s, True), carry)
    number = 0
    for first, lanes, heads in chunks:
        outs = []
        for _ in range(heads):
            peak, total, acc = carry[number]
            outs.append(acc * (keep_ref[number] / total))
            logs_ref[block, number : number + 1, :] = peak + jnp.log(total)
            number += 1
        heads_s[here, first : first + lanes] = low(jnp.concatenate(outs, axis=0).T)


def attend_back_block(block, start, rank, keep_ref, qkv_s, heads_s, grads_s, logs_ref, dq_s, dk_s, dv_s):
    columns = qkv_s.shape[-1]
    chunks = lane_chunks(columns)
    here = pl.ds(pl.multiple_of(place_of(block, rank) * TILE, TILE), TILE)
    queries, grads, weighted, logs = [], [], [], []
    number = 0
    for first, lanes, heads in chunks:
        query = qkv_s[0, here, first : first + lanes]
        grad = grads_s[here, first : first + lanes]
        turned = (wide(grad) * wide(heads_s[here, first : first + lanes])).T
        for h in range(heads):
            keep = keep_ref[number]
            queries.append(one_head(query, h, heads))
            grads.append(low(wide(one_head(grad, h, heads)) * keep))
            weighted.append(keep * jnp.sum(turned[h * HD : (h + 1) * HD], axis=0, keepdims=True))
            logs.append(logs_ref[block, number : number + 1, :])
            number += 1

    def tile(index, carry, masked):
        rows = pl.ds(pl.multiple_of(place_of(index, rank) * TILE, TILE), TILE)
        if masked:
            visible = tile_visible(index * TILE, block * TILE, start)
        out = []
        number = 0
        for first, lanes, heads in chunks:
            keys = qkv_s[1, rows, first : first + lanes]
            values = qkv_s[2, rows, first : first + lanes]
            dk = dv = None
            for h in range(heads):
                scores = matmul(keys, queries[number], 1, 1)
                if masked:
                    scores = jnp.where(visible, scores, negative)
                prob = jnp.exp(scores - logs[number])
                dprob = matmul(values, grads[number], 1, 1)
                dscores = low(prob * (dprob - weighted[number]))
                dv_part = matmul(low(prob), grads[number], 1, 0)
                dk_part = matmul(dscores, queries[number], 1, 0)
                dv = dv_part if dv is None else dv + dv_part
                dk = dk_part if dk is None else dk + dk_part
                out.append(carry[number] + matmul(keys, dscores, 0, 0)[h * HD : (h + 1) * HD])
                number += 1
            dk_s[rows, first : first + lanes] += dk
            dv_s[rows, first : first + lanes] += dv
        return tuple(out)

    carry = tuple(jnp.zeros((HD, TILE), jnp.float32) for _ in range(columns // HD))
    carry = lax.fori_loop(0, block, lambda i, s: tile(i, s, False), carry)
    carry = lax.fori_loop(block, tile_bounds(block, 4, start), lambda i, s: tile(i, s, True), carry)
    number = 0
    for first, lanes, heads in chunks:
        dq = jnp.concatenate(carry[number : number + heads], axis=0) * (1.0 / HD**0.5)
        dq_s[here, first : first + lanes] = low(dq.T)
        number += heads


ANY = pl.BlockSpec(memory_space=pl.ANY)
VMEM = pl.BlockSpec(memory_space=pltpu.VMEM)
LIMIT = 56 << 20


def fetch(parts, into, sem):
    first = 0
    for part in parts:
        rows = part.shape[0]
        pltpu.make_async_copy(part, into.at[pl.ds(first, rows)], sem).start()
        first += rows


def fetched(into, sem):
    pltpu.make_async_copy(into, into, sem).wait()


def send(source, into, sem):
    copy = pltpu.make_async_copy(source, into, sem)
    copy.start()
    return copy


def scratch(*shape):
    return pltpu.VMEM(shape, jnp.bfloat16)


def matmul_call(kernel, name, outs, args, specs, scratches, flops):
    size = sum(a.size * a.dtype.itemsize for a in args)
    return pl.pallas_call(
        kernel,
        in_specs=specs,
        out_specs=[spec for _, _, spec in outs],
        out_shape=[jax.ShapeDtypeStruct(shape, dtype) for shape, dtype, _ in outs],
        scratch_shapes=scratches,
        compiler_params=pltpu.CompilerParams(vmem_limit_bytes=LIMIT),
        cost_estimate=pl.CostEstimate(flops=flops // 256, transcendentals=0, bytes_accessed=size // 128),
        name=name,
    )(*args)


SMEM = pl.BlockSpec(memory_space=pltpu.SMEM)


def front(pieces, weights, places, bias, columns, info, keep):
    count, width = pieces[0].shape
    length = 4 * count
    half = length // 2
    scales = (1.0 / HD**0.5, 1.0, 1.0)

    def kernel(*refs):
        piece_refs, refs = refs[:4], refs[4:]
        weight_refs, refs = refs[: len(weights)], refs[len(weights) :]
        bias_ref, info_ref, keep_ref, refs = refs[0], refs[1], refs[2], refs[3:]
        qkv_ref, all_ref, full_ref, heads_ref, near_ref, far_ref, logs_ref = refs[:7]
        rows_s, full_s, qkv_s, heads_s, sum_s, sems, outs = refs[7:]
        for array, index, row, matrix, column, rows in places:
            source = weight_refs[array]
            source = source if index is None else source.at[index]
            pltpu.make_async_copy(
                source.at[pl.ds(row, rows)], full_s.at[matrix, pl.ds(column, rows)], sems.at[0]
            ).start()
        fetch(piece_refs, rows_s, sems.at[1])
        fetched(full_s, sems.at[0])
        fetched(rows_s, sems.at[1])
        sent = [send(full_s, full_ref, outs.at[0]), send(rows_s, all_ref, outs.at[1])]

        @pl.loop(0, 4)
        def _(block):
            rows = pl.ds(pl.multiple_of(block * count, count), count)
            for t in range(3):
                part = low(matmul(rows_s[rows, :], full_s[t], 1, 1) + bias_ref[t])
                qkv_s[t, rows, :] = low(wide(part) * scales[t])

        sent.append(send(qkv_s, qkv_ref, outs.at[2]))

        @pl.loop(0, 4)
        def _(block):
            attend_block(block, info_ref[0], info_ref[1], keep_ref, qkv_s, heads_s, logs_ref)

        sent.append(send(heads_s, heads_ref, outs.at[3]))

        @pl.loop(0, 4)
        def _(block):
            rows = pl.ds(pl.multiple_of(block * count, count), count)
            sum_s[rows, :] = low(matmul(heads_s[rows, :], full_s[3], 1, 0))

        sent.append(send(sum_s.at[pl.ds(0, half)], near_ref, outs.at[4]))
        sent.append(send(sum_s.at[pl.ds(half, half)], far_ref, outs.at[5]))
        for copy in sent:
            copy.wait()

    def out(*shape):
        return (shape, jnp.bfloat16, ANY)

    return matmul_call(
        kernel,
        "front",
        [
            out(3, length, columns), out(length, width), out(4, columns, width), out(length, columns),
            out(half, width), out(half, width), ((4, columns // HD, TILE), jnp.float32, VMEM),
        ],
        [*pieces, *weights, bias, info, keep],
        [ANY] * (4 + len(weights)) + [VMEM, SMEM, SMEM],
        [
            scratch(length, width), scratch(4, columns, width), scratch(3, length, columns),
            scratch(length, columns), scratch(length, width),
            pltpu.SemaphoreType.DMA((2,)), pltpu.SemaphoreType.DMA((6,)),
        ],
        8 * length * columns * width + 4 * length * length * columns,
    )


def rear(pieces, weights, qkv, heads_low, logs, info, keep):
    count, width = pieces[0].shape
    length = 4 * count
    half = length // 2
    columns = weights.shape[1]

    def kernel(*refs):
        piece_refs, refs = refs[:4], refs[4:]
        weight_ref, qkv_ref, heads_ref, logs_ref, info_ref, keep_ref, refs = *refs[:6], refs[6:]
        dq_ref, dk_ref, dv_ref, all_ref, near_ref, far_ref = refs[:6]
        rows_s, full_s, qkv_s, heads_s, grads_s, dq_s, dk_s, dv_s, low_s, sum_s, sems, outs = refs[6:]
        fetch([weight_ref.at[3]], full_s.at[3], sems.at[0])
        fetch(piece_refs, rows_s, sems.at[1])
        fetch([heads_ref], heads_s, sems.at[2])
        copies = [send(qkv_ref, qkv_s, sems.at[3])]
        copies.append(send(weight_ref.at[pl.ds(0, 3)], full_s.at[pl.ds(0, 3)], sems.at[4]))
        dk_s[...] = jnp.zeros_like(dk_s)
        dv_s[...] = jnp.zeros_like(dv_s)
        fetched(full_s.at[3], sems.at[0])
        fetched(rows_s, sems.at[1])
        sent = [send(rows_s, all_ref, outs.at[0])]

        @pl.loop(0, 4)
        def _(block):
            at = pl.ds(pl.multiple_of(block * count, count), count)
            grads_s[at, :] = low(matmul(rows_s[at, :], full_s[3], 1, 1))

        fetched(heads_s, sems.at[2])
        copies[0].wait()

        @pl.loop(0, 4)
        def _(block):
            attend_back_block(
                block, info_ref[0], info_ref[1], keep_ref, qkv_s, heads_s, grads_s, logs_ref, dq_s, dk_s, dv_s
            )

        copies[1].wait()
        low_s[0] = low(dk_s[...])
        low_s[1] = low(dv_s[...])
        sent.append(send(dq_s, dq_ref, outs.at[1]))
        sent.append(send(low_s.at[0], dk_ref, outs.at[2]))
        sent.append(send(low_s.at[1], dv_ref, outs.at[3]))

        @pl.loop(0, 4)
        def _(block):
            at = pl.ds(pl.multiple_of(block * count, count), count)
            total = matmul(dq_s[at, :], full_s[0], 1, 0)
            total = total + matmul(low_s[0, at, :], full_s[1], 1, 0)
            total = total + matmul(low_s[1, at, :], full_s[2], 1, 0)
            sum_s[at, :] = low(total)

        sent.append(send(sum_s.at[pl.ds(0, half)], near_ref, outs.at[4]))
        sent.append(send(sum_s.at[pl.ds(half, half)], far_ref, outs.at[5]))
        for copy in sent:
            copy.wait()

    def out(*shape):
        return (shape, jnp.bfloat16, ANY)

    return matmul_call(
        kernel,
        "rear",
        [out(length, columns)] * 3 + [out(length, width), out(half, width), out(half, width)],
        [*pieces, weights, qkv, heads_low, logs, info, keep],
        [ANY] * 7 + [VMEM, SMEM, SMEM],
        [
            scratch(length, width), scratch(4, columns, width), scratch(3, length, columns),
            scratch(length, columns), scratch(length, columns), scratch(length, columns),
            pltpu.VMEM((length, columns), jnp.float32), pltpu.VMEM((length, columns), jnp.float32),
            scratch(2, length, columns), scratch(length, width),
            pltpu.SemaphoreType.DMA((5,)), pltpu.SemaphoreType.DMA((6,)),
        ],
        8 * length * columns * width + 10 * length * length * columns,
    )


def gelu_pair(u):
    k = 0.7978845608028654
    t = jnp.tanh(k * (u + 0.044715 * (u * u * u)))
    value = 0.5 * u * (1.0 + t)
    slope = 0.5 * (1.0 + t) + 0.5 * u * (1.0 - t * t) * (k * (1.0 + 3 * 0.044715 * (u * u)))
    return value, slope


def mlp_main(rows, grads, weights, bias):
    count, width = rows[0].shape
    length = 4 * count
    units = weights.shape[0] // 16
    hidden = 8 * units
    half = length // 2

    def kernel(*refs):
        row_refs, grad_refs, weight_ref, refs = refs[:4], refs[4:8], refs[8], refs[9:]
        bias_ref, refs = refs[0], refs[1:]
        rows_ref, grads_ref, hidden_ref, pre_ref, near_ref, far_ref, sum_ref = refs[:7]
        rows_s, grads_s, fc_s, proj_s, hidden_s, slope_s, back_s, sems, outs = refs[7:]
        fetch([weight_ref.at[pl.ds(2 * i * units, units)] for i in range(8)], fc_s, sems.at[0])
        fetch(row_refs, rows_s, sems.at[1])
        fetch([weight_ref.at[pl.ds((2 * i + 1) * units, units)] for i in range(8)], proj_s, sems.at[2])
        fetch(grad_refs, grads_s, sems.at[3])
        fetched(fc_s, sems.at[0])
        fetched(rows_s, sems.at[1])
        sent = [send(rows_s, rows_ref, outs.at[0])]

        @pl.loop(0, 4)
        def _(block):
            at = pl.ds(pl.multiple_of(block * count, count), count)
            value, slope = gelu_pair(matmul(rows_s[at, :], fc_s[...], 1, 1) + bias_ref[...])
            hidden_s[at, :] = low(value)
            slope_s[at, :] = low(slope)

        sent.append(send(hidden_s, hidden_ref, outs.at[1]))
        fetched(proj_s, sems.at[2])
        fetched(grads_s, sems.at[3])
        sent.append(send(grads_s, grads_ref, outs.at[2]))
        sum_ref[...] = jnp.zeros_like(sum_ref)

        @pl.loop(0, 4)
        def _(block):
            at = pl.ds(pl.multiple_of(block * count, count), count)
            pre = low(matmul(grads_s[at, :], proj_s[...], 1, 1) * wide(slope_s[at, :]))
            slope_s[at, :] = pre
            sum_ref[...] += jnp.sum(wide(pre), axis=0, keepdims=True)
            back_s[at, :] = low(matmul(pre, fc_s[...], 1, 0))

        sent.append(send(slope_s, pre_ref, outs.at[3]))
        sent.append(send(back_s.at[pl.ds(0, half)], near_ref, outs.at[4]))
        sent.append(send(back_s.at[pl.ds(half, half)], far_ref, outs.at[5]))
        for copy in sent:
            copy.wait()

    def out(rows, columns):
        return ((rows, columns), jnp.bfloat16, ANY)

    return matmul_call(
        kernel,
        "mlp_main",
        [
            out(length, width), out(length, width), out(length, hidden), out(length, hidden),
            out(half, width), out(half, width), ((1, hidden), jnp.float32, VMEM),
        ],
        [*rows, *grads, weights, bias],
        [ANY] * 9 + [VMEM],
        [
            scratch(length, width), scratch(length, width), scratch(hidden, width), scratch(hidden, width),
            scratch(length, hidden), scratch(length, hidden), scratch(length, width),
            pltpu.SemaphoreType.DMA((4,)), pltpu.SemaphoreType.DMA((6,)),
        ],
        6 * length * hidden * width,
    )


def mlp_rest(rows, grads, hidden, pre, weights):
    length, width = rows.shape
    units = weights.shape[0] // 16
    total = 8 * units
    half = length // 2
    count = length // 4
    tile = 256

    def kernel(*refs):
        rows_ref, grads_ref, hidden_ref, pre_ref = refs[:4]
        weight_ref, near_ref, far_ref, grad_out = refs[4:8]
        rows_s, grads_s, hidden_s, pre_s, proj_s, ahead_s, fc_s, back_s, sems, outs = refs[8:]
        fetch([hidden_ref], hidden_s, sems.at[0])
        fetch([weight_ref.at[pl.ds((2 * i + 1) * units, units)] for i in range(8)], proj_s, sems.at[1])
        fetch([pre_ref], pre_s, sems.at[2])
        fetch([rows_ref], rows_s, sems.at[3])
        fetch([grads_ref], grads_s, sems.at[4])
        fetched(hidden_s, sems.at[0])
        fetched(proj_s, sems.at[1])

        @pl.loop(0, 4)
        def _(block):
            at = pl.ds(pl.multiple_of(block * count, count), count)
            ahead_s[at, :] = low(matmul(hidden_s[at, :], proj_s[...], 1, 0))

        sent = [
            send(ahead_s.at[pl.ds(0, half)], near_ref, outs.at[0]),
            send(ahead_s.at[pl.ds(half, half)], far_ref, outs.at[1]),
        ]
        fetched(pre_s, sems.at[2])
        fetched(rows_s, sems.at[3])

        def pieces(source, kind):
            for k in range(8):
                into = grad_out.at[pl.ds((2 * k + kind) * units, units)]
                sent.append(send(source.at[pl.ds(k * units, units)], into, outs.at[2 + kind * 8 + k]))

        @pl.loop(0, total // tile)
        def _(block):
            at = pl.ds(pl.multiple_of(block * tile, tile), tile)
            fc_s[at, :] = low(matmul(pre_s[:, at], rows_s[...], 0, 0))

        pieces(fc_s, 0)
        fetched(grads_s, sems.at[4])

        @pl.loop(0, total // tile)
        def _(block):
            at = pl.ds(pl.multiple_of(block * tile, tile), tile)
            back_s[at, :] = low(matmul(hidden_s[:, at], grads_s[...], 0, 0))

        pieces(back_s, 1)
        for copy in sent:
            copy.wait()

    def out(*rows):
        return ((*rows, width), jnp.bfloat16, ANY)

    return matmul_call(
        kernel,
        "mlp_rest",
        [out(half), out(half), out(16 * units)],
        [rows, grads, hidden, pre, weights],
        [ANY] * 5,
        [
            scratch(length, width), scratch(length, width), scratch(length, total), scratch(length, total),
            scratch(total, width), scratch(length, width), scratch(total, width), scratch(total, width),
            pltpu.SemaphoreType.DMA((5,)), pltpu.SemaphoreType.DMA((18,)),
        ],
        6 * length * total * width,
    )


def head_weight_grads(lefts, rows, grad_rows, places, outs):
    length, columns = lefts[0].shape
    width = rows.shape[1]

    def kernel(*refs):
        left_refs, (rows_ref, grads_ref), refs = refs[:4], refs[4:6], refs[6:]
        out_refs, (full_s, sem) = refs[: len(outs)], refs[len(outs) :]
        for matrix in range(4):
            right = (rows_ref if matrix < 3 else grads_ref)[...]
            full_s[matrix] = low(matmul(left_refs[matrix][...], right, 0, 0))
        for array, index, row, matrix, column, count in places:
            into = out_refs[array]
            into = into if index is None else into.at[index]
            pltpu.make_async_copy(
                full_s.at[matrix, pl.ds(column, count)], into.at[pl.ds(row, count)], sem.at[0]
            ).start()
        pltpu.make_async_copy(full_s, full_s, sem.at[0]).wait()

    return matmul_call(
        kernel,
        "head_weight_grads",
        [(shape, jnp.bfloat16, ANY) for shape in outs],
        [*lefts, rows, grad_rows],
        [VMEM] * 6,
        [scratch(4, columns, width), pltpu.SemaphoreType.DMA((1,))],
        8 * length * columns * width,
    )


def hidden_blocks(fc, proj):
    shard = proj.shape[1]
    return jnp.concatenate([jnp.transpose(fc).reshape(8, -1, shard), proj.reshape(8, -1, shard)], axis=1)


def hidden_unblock(blocks):
    shard = blocks.shape[-1]
    blocks = blocks.reshape(8, 2, -1, shard)
    return blocks[:, 0].reshape(-1, shard), blocks[:, 1].reshape(-1, shard)


def teacher_blocks(qkv, out):
    columns, shard = out.shape
    stack = jnp.concatenate([jnp.transpose(qkv, (0, 2, 1)), out[None]], axis=0)
    stack = stack.reshape(4, 2, columns // (2 * HD), 2, 2, HD // 4, shard)
    return jnp.transpose(stack, (3, 1, 4, 0, 2, 5, 6)).reshape(8, -1, shard)


def teacher_unblock(heads):
    shard = heads.shape[-1]
    stack = heads.reshape(2, 2, 2, 4, -1, HD // 4, shard)
    return jnp.transpose(stack, (3, 1, 4, 0, 2, 5, 6)).reshape(4, -1, shard)


def student_blocks(qkv, out):
    columns, shard = out.shape
    stack = jnp.concatenate([jnp.transpose(qkv, (0, 2, 1)), out[None]], axis=0)
    stack = stack.reshape(4, columns // HD, 8, HD // 8, shard)
    return jnp.transpose(stack, (2, 0, 1, 3, 4)).reshape(8, -1, shard)


def student_unblock(heads):
    shard = heads.shape[-1]
    return jnp.transpose(heads.reshape(8, 4, -1, HD // 8, shard), (1, 2, 0, 3, 4)).reshape(4, -1, shard)


def teacher_places(columns):
    sub = HD // 4
    heads = columns // (2 * HD)
    places = []
    for matrix in range(4):
        for plane in range(2):
            for head in range(heads):
                for dc in range(2):
                    for dy in range(2):
                        column = (plane * heads + head) * HD + (dc * 2 + dy) * sub
                        places.append((dc * 2 + dy, plane, (matrix * heads + head) * sub, matrix, column, sub))
    return places


def student_places(columns):
    sub = HD // 8
    heads = columns // HD
    places = []
    for matrix in range(4):
        for head in range(heads):
            for part in range(8):
                places.append((part, None, (matrix * heads + head) * sub, matrix, head * HD + part * sub, sub))
    return places


def student_grad_places(columns):
    return [(p // 4, p % 4, row, matrix, column, sub) for p, _, row, matrix, column, sub in student_places(columns)]


def on_pairs(*args):
    teacher_in, student_in = args[0:14], args[14:28]
    span_starts, head_slots = args[28], args[29]
    pos = {name: lax.axis_index(name) for name in EVERY}
    y, x, c, z = pos["y"], pos["x"], pos["c"], pos["z"]
    rank = x * 2 + c
    teacher_columns, student_columns = teacher_in[6].shape[0], student_in[6].shape[0]
    teacher_count, student_count = teacher_columns // 2, student_columns // 2
    shard, student_shard = teacher_in[2].shape[0], student_in[2].shape[0]
    length = 4 * teacher_in[0].shape[1]

    order = (2, 3, 7, 8, 9, 13)
    marks = jnp.stack([span_starts[0] // 32, span_starts[0] % 32, 0, 0]).astype(jnp.bfloat16)
    tall = jnp.concatenate(
        [
            jnp.stack([teacher_in[i] for i in order]),
            jnp.pad(jnp.stack([student_in[i] for i in order]), ((0, 0), (0, shard - student_shard))),
            jnp.broadcast_to(marks[:, None], (4, shard)),
        ],
        axis=0,
    )
    blocks = teacher_blocks(teacher_in[4], teacher_in[6])
    blocks = jnp.concatenate([blocks, jnp.broadcast_to(tall[None], (8,) + tall.shape)], axis=1)
    teacher_got = to_plane(blocks)
    teacher_rows, student_rows = rows_out(teacher_in[0][0]), rows_out(student_in[0][0])

    parts = [
        teacher_in[11], teacher_in[5].reshape(-1), student_in[11], student_in[5].reshape(-1),
        jnp.pad(head_slots.astype(jnp.bfloat16), (0, 128 - head_slots.shape[0])),
    ]
    limits = np.cumsum([0] + [part.shape[0] // 128 for part in parts])
    deep = jnp.concatenate([part.reshape(-1, 128) for part in parts], axis=0)
    deep = [deep] + [plane_swap(deep, step) for step in (1, 2, 3)]

    blocks = jnp.concatenate(
        [student_blocks(student_in[4], student_in[6]), hidden_blocks(student_in[10], student_in[12])], axis=1
    )
    student_got = to_plane(after(blocks, teacher_got))

    vectors = teacher_got[:, teacher_count:]

    def width_vectors(block):
        block = wide(jnp.transpose(block, (1, 0, 2)).reshape(6, 1, -1))
        return tuple(block[i] for i in range(6))

    teacher_vectors = width_vectors(vectors[:, :6])
    student_vectors = width_vectors(vectors[:, 6:12, :student_shard])
    starts = vectors[:, 12:14, 0].astype(jnp.int32)
    starts = starts[:, 0] * 32 + starts[:, 1]
    info = jnp.stack([pick(starts, y * 4 + z), 2 * c + (x ^ (z & 1))])

    step = Order()
    first = c == 0

    t0 = step(join_shards(teacher_got[:, :teacher_count]))
    t1, t2, t0y = plane_swap(t0, 1), plane_swap(t0, 2), swap(t0, "y")
    full16, student16 = (teacher_rows.shape, jnp.bfloat16), (student_rows.shape, jnp.bfloat16)
    (normed,) = row_call(
        first_norm_kernel, "first_norm", [full16], step(teacher_rows), teacher_vectors[0], teacher_vectors[1]
    )
    teacher_normed = [normed, swap(normed, "x"), swap(normed, "c")]
    step.mark(normed)
    student_cross = cross(step(join_shards(student_got[:, :student_count])))
    t2 = step(t2)
    t3, t2y = plane_swap(t2, 1), swap(t2, "y")
    t1 = step(t1)
    t1y = swap(t1, "y")
    teacher_hidden_got = to_plane(after(hidden_blocks(teacher_in[10], teacher_in[12]), t1))
    teacher_normed[1] = step(teacher_normed[1])
    teacher_normed.append(swap(teacher_normed[1], "c"))
    t3 = step(t3)
    t3y = swap(t3, "y")

    def halves(one, two, three, four):
        front, rear_part = jnp.stack([one, two]), jnp.stack([three, four])
        return jnp.where(first, front, rear_part), swap(jnp.where(first, rear_part, front), "c")

    own, near = halves(t0, t1, t2, t3)
    s0 = step(student_cross)
    s1, s2, s0y = plane_swap(s0, 1), plane_swap(s0, 2), swap(s0, "y")
    (normed,) = row_call(
        first_norm_kernel, "first_norm", [student16], step(student_rows), student_vectors[0], student_vectors[1]
    )
    student_normed = [normed, swap(normed, "x"), swap(normed, "c")]
    step.mark(normed)
    s2 = step(s2)
    s3, s2y = plane_swap(s2, 1), swap(s2, "y")
    s1 = step(s1)
    s1y = swap(s1, "y")
    teacher_up = rows_out(after(teacher_in[1][0], s1))
    tf0 = step(join_shards(teacher_hidden_got))
    t0y, t1y, t2y, t3y = step(t0y, t1y, t2y, t3y)
    own_over, near_over = halves(t0y, t1y, t2y, t3y)
    teacher_weights = lax.all_gather(after(tf0, t3y), ("y", "z"), axis=0, tiled=True)

    deep = jnp.stack(deep)
    deep = [deep[:, limits[i] : limits[i + 1]].reshape(4, -1) for i in range(5)]
    near_y = jnp.stack([y, 1 - y])
    hidden_spots = (jnp.arange(4)[None] * 8 + jnp.arange(2)[:, None] * 4 + rank).reshape(-1)
    near_c = jnp.stack([c, 1 - c])
    planes = z ^ jnp.arange(4)
    hidden_hot = wide(jnp.arange(4)[:, None] == planes[None]).astype(jnp.bfloat16)

    def hidden_bias(block):
        block = pick(block.reshape(4, 2, 4, -1), rank, 2)
        return jnp.einsum("zk,kyi->yzi", hidden_hot, block, preferred_element_type=jnp.float32).reshape(1, -1)

    teacher_fc_bias, student_fc_bias = hidden_bias(deep[0]), hidden_bias(deep[2])
    two = jnp.where(first, 0, 2)
    block = lax.dynamic_slice_in_dim(deep[1].reshape(4, -1), two, 2, 0)
    block = block.reshape(2, 2, 2, -1, 2, 2, HD // 4)
    block = pick(block, x, 2)
    block = jnp.where(y == 0, block, block[:, :, :, ::-1])
    block = jnp.where(first, block, block[:, :, :, :, ::-1])
    teacher_qv = wide(jnp.transpose(block, (1, 0, 2, 4, 3, 5)).reshape(2, -1))
    slots = lax.dynamic_slice_in_dim(deep[4][:, : head_slots.shape[0]], two, 2, 0)
    keep = wide(pick(slots.reshape(2, 2, -1), x, 1).reshape(-1))
    block = pick(deep[3].reshape(4, 2, -1, 8, HD // 8), z ^ rank)
    eighth = (near_y[:, None] * 4 + planes[None]).reshape(-1)
    order_hot = (jnp.arange(8)[None] == eighth[:, None]).astype(jnp.bfloat16)
    student_qv = jnp.einsum("rp,thpi->thri", order_hot, block, preferred_element_type=jnp.float32).reshape(2, -1)
    ones = jnp.ones((student_qv.shape[1] // HD,), jnp.float32)

    def bias_rows(pair):
        return jnp.stack([pair[0], jnp.zeros_like(pair[0]), pair[1]])[:, None, :]

    teacher_spots, student_spots = teacher_places(teacher_columns), student_places(student_columns)
    head_weights = (own, own_over, near, near_over)
    qkv, normed_all, weights, heads_low, t_near, t_far, logs = front(
        step(*teacher_normed), head_weights, teacher_spots, bias_rows(teacher_qv), teacher_columns, info, keep
    )
    teacher_saved = (qkv, normed_all, weights, heads_low, logs)
    step.mark(t_near)
    t_got = swap(t_far, "c")
    t_over = swap(step(ahead_sum(t_near, t_got)), "x")
    sf0 = step(join_shards(student_got[:, student_count:]))
    student_weights = lax.all_gather(sf0, ("y", "z"), axis=0, tiled=True)
    bias_out, gain_two, shift_two = teacher_vectors[2:5]
    full32 = (teacher_rows.shape, jnp.float32)
    t_middle, normed = row_call(
        mid_norm_kernel, "mid_norm", [full32, full16],
        teacher_rows, t_near, t_got, step(t_over), bias_out, gain_two, shift_two,
    )
    step.mark(normed)
    teacher_normed = [normed, swap(normed, "x"), swap(normed, "c")]
    student_normed[1] = step(student_normed[1])
    student_normed.append(swap(student_normed[1], "c"))
    s3 = step(s3)
    s3y = swap(s3, "y")
    teacher_up = step(teacher_up)
    teacher_ups = [teacher_up, swap(teacher_up, "x"), swap(teacher_up, "c")]
    student_up = rows_out(after(student_in[1][0], teacher_up))
    teacher_normed[1] = step(teacher_normed[1])
    teacher_normed.append(swap(teacher_normed[1], "c"))

    head_weights = (s0, s1, s2, s3, s0y, s1y, s2y, s3y)
    qkv, normed_all, weights, heads_low, s_near, s_far, logs = front(
        step(*student_normed), head_weights, student_spots, bias_rows(student_qv), student_columns, info, ones
    )
    student_saved = (qkv, normed_all, weights, heads_low, logs)
    step.mark(s_near)
    s_got = swap(s_far, "c")
    teacher_ups[1] = step(teacher_ups[1])
    teacher_ups.append(swap(teacher_ups[1], "c"))
    ahead = step(ahead_sum(s_near, s_got))
    s_part, s_over = swap(ahead[:64], "x"), swap(ahead[64:], "x")

    *teacher_mlp, t_near, t_far, teacher_fc = mlp_main(
        step(after(teacher_normed[0], s_part), *teacher_normed[1:]), teacher_ups, teacher_weights, teacher_fc_bias
    )
    step.mark(t_near)
    t_got = swap(t_far, "c")
    ahead = step(ahead_sum(t_near, t_got))
    t_part, t_over = swap(ahead[:64], "x"), swap(ahead[64:], "x")
    bias_out, gain_two, shift_two = student_vectors[2:5]
    student32 = (student_rows.shape, jnp.float32)
    s_middle, normed = row_call(
        mid_norm_kernel, "mid_norm", [student32, student16],
        student_rows, s_near, s_got, jnp.concatenate([s_part, step(s_over)], axis=0), bias_out, gain_two, shift_two,
    )
    step.mark(normed)
    student_normed = [normed, swap(normed, "x"), swap(normed, "c")]
    student_up = step(student_up)
    student_ups = [student_up, swap(student_up, "x"), swap(student_up, "c")]
    teacher_mlp[0] = after(step(teacher_mlp[0]), t_part)
    t_out_near, t_out_far, grads = mlp_rest(*teacher_mlp, teacher_weights)
    step.mark(t_out_near)
    teacher_hidden = lax.psum_scatter(grads, ("y", "z"), scatter_dimension=0, tiled=True)
    width = teacher_rows.shape[1]
    t_dmid, t_ga, teacher_two = row_call(
        mid_back_kernel, "mid_back", [full32, full16, ((4, width), jnp.float32)],
        teacher_up, t_near, t_got, jnp.concatenate([t_part, step(t_over)], axis=0), t_middle, teacher_vectors[3],
    )
    step.mark(t_ga)
    teacher_normed = [t_ga, swap(t_ga, "x"), swap(t_ga, "c")]

    student_normed[1] = step(student_normed[1])
    student_normed.append(swap(student_normed[1], "c"))
    student_ups[1] = step(student_ups[1])
    student_ups.append(swap(student_ups[1], "c"))

    *student_mlp, s_near, s_far, student_fc = mlp_main(
        step(*student_normed), student_ups, student_weights, student_fc_bias
    )
    step.mark(s_near)
    s_got = swap(s_far, "c")
    teacher_normed[1] = step(teacher_normed[1])
    teacher_normed.append(swap(teacher_normed[1], "c"))
    s_over = swap(step(ahead_sum(s_near, s_got)), "x")

    qkv, normed_all, weights, heads_low, logs = teacher_saved
    t_dq, t_dk, t_dv, t_grad_all, t_near, t_far = rear(
        step(*teacher_normed), weights, qkv, heads_low, logs, info, keep
    )
    step.mark(t_near)
    t_got = swap(t_far, "c")
    teacher_saved = ([t_dq, t_dk, t_dv, heads_low], normed_all, t_grad_all)
    width = student_rows.shape[1]
    s_dmid, s_ga, student_two = row_call(
        mid_back_kernel, "mid_back", [student32, student16, ((4, width), jnp.float32)],
        student_up, s_near, s_got, step(s_over), s_middle, student_vectors[3],
    )
    step.mark(s_ga)
    student_normed = [s_ga, swap(s_ga, "x"), swap(s_ga, "c")]
    t_over = swap(step(ahead_sum(t_near, t_got)), "x")
    lefts, right, grad_right = teacher_saved
    lefts[0] = step(lefts[0])
    teacher_width, student_width = teacher_rows.shape[1], student_rows.shape[1]
    th = head_weight_grads(lefts, right, grad_right, teacher_spots, [(2, teacher_count, teacher_width)] * 4)
    teacher_qv_grad = jnp.stack([jnp.sum(wide(t_dq), axis=0), jnp.sum(wide(t_dv), axis=0)])
    step.mark(th[0])
    th_over_got, th_got = swap(th[3], "c"), swap(th[2], "c")

    def planes_of(mine, got):
        odd = jnp.stack([jnp.where(first, mine[1], got[1]), jnp.where(first, got[1], mine[1])])
        even = jnp.stack([jnp.where(first, mine[0], got[0]), jnp.where(first, got[0], mine[0])])
        return odd, even

    odd_over, even_over = planes_of(th[1], step(th_over_got))
    odd_got, even_got = swap(odd_over, "y"), swap(even_over, "y")
    th_odd, th_even = planes_of(th[0], th_got)
    step.mark(odd_over)
    student_mlp[0] = step(student_mlp[0])
    s_out_near, s_out_far, grads = mlp_rest(*student_mlp, student_weights)
    step.mark(s_out_near)
    student_hidden = lax.psum_scatter(grads, ("y", "z"), scatter_dimension=0, tiled=True)
    teacher_dx, teacher_one = row_call(
        first_back_kernel, "first_back", [full16, ((2, teacher_width), jnp.float32)],
        t_near, t_got, step(t_over), teacher_rows, t_dmid, teacher_vectors[0],
    )
    step.mark(teacher_dx)
    t_out_got = swap(after(t_out_far, teacher_dx), "c")
    teacher_dx = rows_home(teacher_dx)
    teacher_hidden = to_plane(split_shards(step(teacher_hidden)))
    student_normed[1] = step(student_normed[1])
    student_normed.append(swap(student_normed[1], "c"))
    qkv, normed_all, weights, heads_low, logs = student_saved
    s_dq, s_dk, s_dv, s_grad_all, s_near, s_far = rear(
        step(*student_normed), weights, qkv, heads_low, logs, info, ones
    )
    step.mark(s_near)
    s_got = swap(s_far, "c")
    odd_got = step(odd_got)
    th_odd_got = plane_swap(step(low(wide(th_odd) + wide(odd_got))), 1)
    s_over = swap(step(ahead_sum(s_near, s_got)), "x")
    sh_near, sh_far = head_weight_grads(
        [step(s_dq), s_dk, s_dv, heads_low], normed_all, s_grad_all, student_grad_places(student_columns),
        [(4, student_count, student_width)] * 2,
    )
    student_qv_grad = jnp.stack([jnp.sum(wide(s_dq), axis=0), jnp.sum(wide(s_dv), axis=0)])
    step.mark(sh_near)
    sh_got = swap(sh_far, "y")
    th_odd_got, even_got = step(th_odd_got, even_got)
    th_even = wide(th_even) + wide(even_got)
    th_even_got = plane_swap(low(th_even[1] + wide(th_odd_got[1])), 2)
    t_out_over = swap(step(ahead_sum(t_out_near, t_out_got)), "x")
    student_dx, student_one = row_call(
        first_back_kernel, "first_back", [student16, ((2, student_width), jnp.float32)],
        s_near, s_got, step(s_over), student_rows, s_dmid, student_vectors[0],
    )
    step.mark(student_dx)
    s_out_got = swap(after(s_out_far, student_dx), "c")
    student_dx = rows_home(student_dx)

    def spread(places, values):
        hot = (jnp.arange(32)[:, None] == places[None]).astype(jnp.float32)
        return jnp.dot(hot, values, precision=lax.Precision.HIGHEST)

    head_planes = planes.reshape(2, 2)
    head_planes = jnp.where(first, head_planes[0], head_planes[1])
    column_spots = (
        head_planes[:, None, None] * 8 + x * 4 + near_y[None, None, :] * 2 + near_c[None, :, None]
    ).reshape(-1)
    eighth_spots = rank * 8 + eighth

    teacher_qv_grad = teacher_qv_grad.reshape(2, 2, -1, 2, 2, HD // 4)
    teacher_qv_grad = jnp.transpose(teacher_qv_grad, (1, 3, 4, 0, 2, 5)).reshape(8, -1)
    student_qv_grad = jnp.transpose(student_qv_grad.reshape(2, -1, 8, HD // 8), (2, 0, 1, 3)).reshape(8, -1)
    hidden_grads = jnp.concatenate([teacher_fc.reshape(8, -1), student_fc.reshape(8, -1)], axis=1)
    hidden_grads = spread(hidden_spots, hidden_grads)
    lanes = hidden_grads.shape[1]
    column_grads = jnp.concatenate(
        [spread(column_spots, teacher_qv_grad), spread(eighth_spots, student_qv_grad)], axis=1
    )
    column_grads = jnp.pad(column_grads, ((0, 0), (0, lanes - column_grads.shape[1])))

    def stacked(one, two):
        tall = jnp.concatenate([one, two, jnp.zeros_like(one)], axis=0)
        return [tall[:, i : i + lanes] for i in range(0, tall.shape[1], lanes)]

    total = jnp.concatenate(
        [hidden_grads, column_grads] + stacked(teacher_one, teacher_two) + stacked(student_one, student_two), axis=0
    )
    total = step(total)
    other = swap(total, "c")
    sh_total = step(wide(sh_near) + wide(sh_got))
    sh_odd_got = plane_swap(low(sh_total[1::2]), 1)
    total = total + step(other)
    other = swap(total, "x")
    teacher_hidden = step(teacher_hidden)
    s_out_over = swap(step(ahead_sum(s_out_near, s_out_got)), "x")
    count = t_middle.shape[0]
    teacher_out = low(
        t_middle + (wide(t_out_near[:count]) + wide(t_out_got[:count]) + wide(step(t_out_over)) + teacher_vectors[5])
    )
    teacher_out = rows_home(teacher_out)
    sh_even = step(sh_total[0::2] + wide(sh_odd_got))
    sh_even_got = plane_swap(low(sh_even[1]), 2)
    teacher_head = low(th_even[0] + wide(th_odd_got[0]) + wide(step(th_even_got)))
    teacher_head = to_plane(split_shards(teacher_head))
    total = total + step(other)
    other = swap(total, "y")
    student_head = cross(low(sh_even[0] + wide(step(sh_even_got))))
    count = s_middle.shape[0]
    student_out = low(
        s_middle + (wide(s_out_near[:count]) + wide(s_out_got[:count]) + wide(step(s_out_over)) + student_vectors[5])
    )
    student_out = rows_home(student_out)
    total = total + step(other)
    other = plane_swap(total, 1)
    student_got = jnp.concatenate([step(student_head), student_hidden], axis=0)
    teacher_grads = (teacher_unblock(step(teacher_head)), *hidden_unblock(teacher_hidden))
    student_got = to_plane(split_shards(student_got))
    total = total + step(other)
    other = plane_swap(total, 2)
    teacher_dx, student_dx, teacher_out, student_out = step(teacher_dx, student_dx, teacher_out, student_out)
    student_got = step(student_got)
    student_grads = (student_unblock(student_got[:, :student_count]), *hidden_unblock(student_got[:, student_count:]))
    total = total + other
    teacher_out, teacher_dx = teacher_out[None], teacher_dx[None]
    student_out, student_dx = student_out[None], student_dx[None]

    def matrices(grads):
        stack, fc_grad, proj_grad = grads
        return (
            wide(jnp.transpose(stack[:3], (0, 2, 1))), wide(stack[3]),
            wide(jnp.transpose(fc_grad)), wide(proj_grad),
        )

    own = y * 4 + rank
    units, student_units = teacher_fc.size // 8, student_fc.size // 8
    columns, student_columns = teacher_columns // 4, student_columns // 4
    hidden_grads = pick(total[:32].reshape(4, 8, lanes), z)
    teacher_fc = hidden_grads[:, :units].reshape(-1)
    student_fc = hidden_grads[:, units : units + student_units].reshape(-1)
    column_grads = pick(total[32:64].reshape(4, 8, lanes), z)
    block = column_grads[:, :columns].reshape(2, 2, 2, 2, -1, HD // 4)
    teacher_qv_grad = jnp.transpose(block, (3, 0, 4, 1, 2, 5)).reshape(2, -1)
    block = column_grads[:, columns : columns + student_columns].reshape(8, 2, -1, HD // 8)
    student_qv_grad = jnp.transpose(block, (1, 2, 0, 3)).reshape(2, -1)
    tall = total[64:].reshape(-1, 8, lanes)
    runs = teacher_width // lanes

    def width_grads(tall, count):
        tall = jnp.concatenate([tall[i] for i in range(count)], axis=1)[:6]
        return tuple(pick(tall.reshape(6, 8, -1), own, 1))

    def arranged(outputs, input_grad, grads, sums, qv_grad, fc_grad):
        return (
            outputs, input_grad, sums[0], sums[1], grads[0], qv_grad, grads[1],
            sums[2], sums[3], sums[4], grads[2], fc_grad, grads[3], sums[5],
        )

    return arranged(
        teacher_out, teacher_dx, matrices(teacher_grads), width_grads(tall[:runs], runs), teacher_qv_grad, teacher_fc
    ) + arranged(
        student_out, student_dx, matrices(student_grads), width_grads(tall[runs:], student_width // lanes), student_qv_grad, student_fc
    )


def on_plane(spec):
    names = {"dp": PLANE, "tensor": "z"}
    return P(*(names.get(entry, None) for entry in spec))


def solution(mesh):
    in_specs = (
        P("dp", "tensor", None),
        P("dp", "tensor", None),
        P("dp"),
        P("dp"),
        P(None, "dp", "tensor"),
        P(None, "tensor"),
        P("tensor", "dp"),
        P("dp"),
        P("dp"),
        P("dp"),
        P("dp", "tensor"),
        P("tensor"),
        P("tensor", "dp"),
        P("dp"),
        P("dp", "tensor", None),
        P("dp", "tensor", None),
        P("dp"),
        P("dp"),
        P(None, "dp", "tensor"),
        P(None, "tensor"),
        P("tensor", "dp"),
        P("dp"),
        P("dp"),
        P("dp"),
        P("dp", "tensor"),
        P("tensor"),
        P("tensor", "dp"),
        P("dp"),
        P("dp"),
        P("tensor"),
    )
    out_specs = (
        P("dp", "tensor", None),
        P("dp", "tensor", None),
        P("dp"),
        P("dp"),
        P(None, "dp", "tensor"),
        P(None, "tensor"),
        P("tensor", "dp"),
        P("dp"),
        P("dp"),
        P("dp"),
        P("dp", "tensor"),
        P("tensor"),
        P("tensor", "dp"),
        P("dp"),
        P("dp", "tensor", None),
        P("dp", "tensor", None),
        P("dp"),
        P("dp"),
        P(None, "dp", "tensor"),
        P(None, "tensor"),
        P("tensor", "dp"),
        P("dp"),
        P("dp"),
        P("dp"),
        P("dp", "tensor"),
        P("tensor"),
        P("tensor", "dp"),
        P("dp"),
    )
    if tuple(mesh.devices.shape) == (8, 4):
        finer = Mesh(mesh.devices.reshape(2, 2, 2, 4), EVERY)
        return jax.shard_map(
            on_pairs,
            mesh=finer,
            in_specs=tuple(on_plane(spec) for spec in in_specs),
            out_specs=tuple(on_plane(spec) for spec in out_specs),
            check_vma=False,
        )
    return jax.shard_map(
        on_device, mesh=mesh, in_specs=in_specs, out_specs=out_specs, check_vma=False
    )
```
